32 devices in a mesh: ctx: 16 (over z, y, x), wa: 2 (over core).
Axes of the slice: x: 2, y: 2, z: 4, core: 2. Of those that a mesh axis runs over, the one named last changes fastest.
Arguments:
- tokens: bfloat16 [32768, 768], P(('ctx', 'wa')), may hold values from -6 to 6
- seq_ids: int32 [256], replicated, may hold values from 0 to 1, as said below
- w_qkv: bfloat16 [2, 768, 2304], P(None, ('ctx', 'wa')), may hold values from -0.21875 to 0.21875
- w_out: bfloat16 [2, 768, 768], P(None, ('ctx', 'wa')), may hold values from -1.75 to 1.75
- w_up: bfloat16 [2, 768, 3072], P(None, ('ctx', 'wa')), may hold values from -0.21875 to 0.21875
- w_down: bfloat16 [2, 3072, 768], P(None, ('ctx', 'wa')), may hold values from -0.109375 to 0.109375
- biases: bfloat16 [2, 6, 768], P(None, None, ('ctx', 'wa')), may hold values from -1.1953125 to 1.1953125
- up_bias: bfloat16 [2, 3072], P(None, ('ctx', 'wa')), may hold values from -1.1953125 to 1.1953125
- norm_gains: bfloat16 [2, 2, 768], P(None, None, ('ctx', 'wa')), may hold values from 0.5 to 1.5
- pos_table: bfloat16 [128, 768], P(None, ('ctx', 'wa')), may hold values from -3 to 3
- cotangent: bfloat16 [32768, 768], P(('ctx', 'wa')), may hold values from -6 to 6
Outputs:
- layer_out: bfloat16 [32768, 768], P(('ctx', 'wa'))
- grad_tokens: bfloat16 [32768, 768], P(('ctx', 'wa'))
- grad_w_qkv: float32 [2, 768, 2304], P(None, ('ctx', 'wa'))
- grad_w_out: float32 [2, 768, 768], P(None, ('ctx', 'wa'))
- grad_w_up: float32 [2, 768, 3072], P(None, ('ctx', 'wa'))
- grad_w_down: float32 [2, 3072, 768], P(None, ('ctx', 'wa'))
- grad_biases: float32 [2, 6, 768], P(None, None, ('ctx', 'wa'))
- grad_up_bias: float32 [2, 3072], P(None, ('ctx', 'wa'))
- grad_norm_gains: float32 [2, 2, 768], P(None, None, ('ctx', 'wa'))
- grad_pos_table: float32 [128, 768], P(None, ('ctx', 'wa'))
The draws below stay inside these ranges and needn't reach their ends.
Inputs may be any that keep to these rules, and one draw needn't show every extreme that they name: `seq_ids`: every sequence holds exactly 128 segments, spread over the segment slots in any order.
All inputs are finite; a program needn't handle non-finite values.
Results may differ from the reference program's by a relative error of at most 0.023.
Values may be sent and summed in bfloat16 or wider, within the bound.
No kernel may reach another device: no remote copies, remote signals or barrier semaphores. Data moves between devices by JAX's collectives and lax.ppermute only.
A program may use at most 256 MiB of HBM per device.

```python
from functools import partial
import jax
import jax.numpy as jnp
from jax import lax

D = 768
FF = 3072
HDIM = 64
SEG = 128
MAXSEG = 128
HEADS = 12
SEGS = 256
TOKENS = 32768


def draw_seq_ids(key, part):
    shuffled = jax.random.permutation(jax.random.fold_in(key, 17), SEGS)
    labels = (shuffled // MAXSEG).astype(jnp.int32)
    slots = jnp.arange(SEGS, dtype=jnp.int32)
    target = labels[0]
    middle = SEGS // 2
    last_slot = SEGS - 1
    wanted = (labels == target) & (slots != 0)
    found = jnp.argmax(wanted.astype(jnp.int32)).astype(jnp.int32)
    first_val = labels[middle]
    second_val = labels[found]
    labels = labels.at[middle].set(second_val).at[found].set(first_val)
    wanted = (labels == target) & (slots != 0) & (slots != middle)
    found = jnp.argmax(wanted.astype(jnp.int32)).astype(jnp.int32)
    first_val = labels[last_slot]
    second_val = labels[found]
    labels = labels.at[last_slot].set(second_val).at[found].set(first_val)
    return labels


def with_spikes(values, own_key, source, target, parts, factor):
    owner, partner = [(jnp.arange(values.shape[position]) // (values.shape[position] // parts)).reshape([-1 if axis == position else 1 for axis in range(values.ndim)]) for position in (source, target)]
    chosen = jax.random.permutation(own_key, parts)[partner]
    strong = (owner == chosen) | (owner == (partner + parts // 2) % parts)
    return jnp.where(strong, factor * values, values)


def steps_of(stream_key, extent, split, least, largest):
    loudness, own = 1.0, jax.random.fold_in(stream_key, 6)
    for axis_at, shards_of in split:
        steps = jnp.exp(jax.random.uniform(jax.random.fold_in(own, axis_at), (shards_of,), jnp.float32, least / len(split), largest / len(split)))
        loudness = loudness * jnp.repeat(steps, extent[axis_at] // shards_of).reshape([-1 if axis == axis_at else 1 for axis in range(len(extent))])
    return loudness


def noise(rng, shape, width, limit, cuts=(), kind=jnp.bfloat16):
    values = jax.random.normal(rng, shape, jnp.float32) * width
    if len(cuts) > 0:
        values = steps_of(rng, shape, cuts, -0.22, 0.18) * values
    return jnp.clip(values, min=-limit, max=limit).astype(kind)


def gaussian_with(own_key, shape, scale, bound, cuts, heavy, kind=jnp.bfloat16):
    entries = scale * jax.random.normal(own_key, shape, jnp.float32)
    if cuts:
        entries = entries * steps_of(own_key, shape, cuts, -0.22, 0.18)
    return jnp.clip(with_spikes(entries, jax.random.fold_in(own_key, 3), *heavy), -bound, bound).astype(kind)


def setup_inputs(seed: int = 0) -> dict:
    keys = jax.random.split(jax.random.key(seed), 12)
    return {
        "tokens": noise(keys[0], (TOKENS, D), 1.0, 6.0, ((0, 32),)),
        "seq_ids": draw_seq_ids(jax.random.fold_in(keys[11], 71), 0),
        "w_qkv": noise(keys[2], (2, D, 3 * D), D ** -0.5, 0.21875, ((1, 32),)),
        "w_out": noise(keys[3], (2, D, D), (D // 64) ** -0.5, 1.75, ((1, 32),)),
        "w_up": noise(keys[4], (2, D, FF), D ** -0.5, 0.21875, ((1, 32),)),
        "w_down": noise(keys[5], (2, FF, D), FF ** -0.5, 0.109375, ((1, 32),)),
        "biases": noise(keys[6], (2, 6, D), 0.2, 1.1953125, ((2, 32),)),
        "up_bias": noise(keys[7], (2, FF), 0.2, 1.1953125, ((1, 32),)),
        "norm_gains": jnp.clip(1.0 + 0.1 * jax.random.normal(keys[8], (2, 2, D), jnp.float32), 0.5, 1.5).astype(jnp.bfloat16),
        "pos_table": noise(keys[9], (MAXSEG, D), 0.5, 3.0, ((1, 32),)),
        "cotangent": gaussian_with(keys[10], (TOKENS, D), 1.0, 6.0, ((0, 32),), (0, 1, 32, 2.75)),
    }


@jax.custom_vjp
def low(v):
    return lax.optimization_barrier(v.astype(jnp.bfloat16)).astype(jnp.float32)

@jax.custom_vjp
def low_back(v):
    return v

def low_keep(v):
    return (low(v), None)

def low_pass(kept, grad):
    return (grad,)

def back_keep(v):
    return (v, None)

def back_low(kept, grad):
    return (low(grad),)
low.defvjp(low_keep, low_pass)
low_back.defvjp(back_keep, back_low)

def matmul(first, second):
    return jnp.dot(first, second, precision=lax.Precision.HIGHEST, preferred_element_type=jnp.float32)

def layer_norm(values, weight, offset):
    center = values - lax.optimization_barrier(jnp.mean(values, axis=-1, keepdims=True))
    spread = lax.optimization_barrier(jnp.mean(center * center, axis=-1, keepdims=True))
    return center * lax.rsqrt(spread + 1e-05) * weight + offset

def gelu_exact(values):
    return 0.5 * values * (1.0 + lax.erf(values * 0.7071067811865476))

def both_ways(values):
    return low_back(low(values))

def segment_attend(queries, key_rows, value_rows):
    groups = queries.shape[0] // SEG
    blocked = (groups, SEG, HEADS, HDIM)
    scores = jnp.einsum('gqhd,gkhd->ghqk', queries.reshape(blocked), key_rows.reshape(blocked), precision=lax.Precision.HIGHEST) * HDIM ** (-0.5)
    scores = low_back(scores)
    probability = jax.nn.softmax(scores, axis=-1)
    context = jnp.einsum('ghqk,gkhd->gqhd', low(probability), value_rows.reshape(blocked), precision=lax.Precision.HIGHEST)
    return context.reshape(queries.shape)

def cross_attend(queries, key_rows, value_rows, seq_ids):
    rows_all = queries.shape[0]
    block_rows = min(rows_all, 256)
    keys_h = key_rows.reshape(rows_all, HEADS, HDIM)
    values_h = value_rows.reshape(rows_all, HEADS, HDIM)

    def one_block(pieces):
        block_q, block_ids = pieces
        scores = jnp.einsum('qhd,khd->hqk', block_q.reshape(block_rows, HEADS, HDIM), keys_h, precision=lax.Precision.HIGHEST) * HDIM ** (-0.5)
        allowed = (block_ids[:, None] == seq_ids[None, :])[None]
        scores = low_back(jnp.where(allowed, scores, -1e+30))
        probability = jax.nn.softmax(scores, axis=-1)
        context = jnp.einsum('hqk,khd->qhd', low(probability), values_h, precision=lax.Precision.HIGHEST)
        return context.reshape(block_rows, HEADS * HDIM)
    blocks = lax.map(jax.checkpoint(one_block), (queries.reshape(-1, block_rows, HEADS * HDIM), seq_ids.reshape(-1, block_rows)))
    return blocks.reshape(rows_all, HEADS * HDIM)

def encoder_block(hidden, params, attend):
    w_qkv, w_out, w_up, w_down, biases, up_bias, norm_gains = params
    projected = matmul(low(hidden), w_qkv)
    queries = both_ways(projected[:, :D] + biases[0])
    key_rows = both_ways(projected[:, D:2 * D])
    value_rows = both_ways(projected[:, 2 * D:] + biases[1])
    context = both_ways(attend(queries, key_rows, value_rows))
    attn_out = low_back(matmul(context, w_out) + biases[2])
    normed = layer_norm(hidden + attn_out, norm_gains[0], biases[3])
    before = low_back(matmul(low(normed), w_up) + up_bias)
    active = low(gelu_exact(before))
    ffn_out = low_back(matmul(active, w_down) + biases[4])
    return layer_norm(normed + ffn_out, norm_gains[1], biases[5])

def forward(tokens, w_qkv, w_out, w_up, w_down, biases, up_bias, norm_gains, pos_table, seq_ids, onehot):
    first_level = (w_qkv[0], w_out[0], w_up[0], w_down[0], biases[0], up_bias[0], norm_gains[0])
    second_level = (w_qkv[1], w_out[1], w_up[1], w_down[1], biases[1], up_bias[1], norm_gains[1])
    group_rows = min(TOKENS, 4096)

    def one_group(rows_here):
        return encoder_block(rows_here, first_level, segment_attend)
    segment_out = lax.map(jax.checkpoint(one_group), tokens.reshape(-1, group_rows, D)).reshape(SEGS, SEG, D)
    cross_in = segment_out[:, 0, :] + matmul(onehot, pos_table)
    cross_out = encoder_block(cross_in, second_level, partial(cross_attend, seq_ids=seq_ids))
    return segment_out.at[:, 0, :].set(cross_out).reshape(TOKENS, D)

def reference(tokens, seq_ids, w_qkv, w_out, w_up, w_down, biases, up_bias, norm_gains, pos_table, cotangent):
    slots = jnp.arange(SEGS, dtype=jnp.int32)
    earlier = (seq_ids[None, :] == seq_ids[:, None]) & (slots[None, :] < slots[:, None])
    places = lax.optimization_barrier(jnp.sum(earlier.astype(jnp.int32), axis=1))
    onehot = (places[:, None] == jnp.arange(MAXSEG, dtype=jnp.int32)[None, :]).astype(jnp.float32)
    inputs = tuple((operand.astype(jnp.float32) for operand in (tokens, w_qkv, w_out, w_up, w_down, biases, up_bias, norm_gains, pos_table)))
    result, pullback = jax.vjp(lambda *arrays: forward(*arrays, seq_ids, onehot), *inputs)
    gradients = pullback(cotangent.astype(jnp.float32))
    return (result.astype(jnp.bfloat16), gradients[0].astype(jnp.bfloat16), gradients[1], gradients[2], gradients[3], gradients[4], gradients[5], gradients[6], gradients[7], gradients[8])
```

```python
from functools import partial

import jax
import jax.numpy as jnp
from jax import lax
from jax.experimental import pallas as pl
from jax.experimental.pallas import tpu as pltpu
from jax.sharding import PartitionSpec as P

HDIM = 64
SEG = 128
TP = 4
AXES = ("ctx", "wa")
F32 = jnp.float32
BF16 = jnp.bfloat16
SCALE = HDIM ** (-0.5)


def dot(a, b, dims=((1,), (0,))):
    return lax.dot_general(a, b, (dims, ((), ())), preferred_element_type=F32)


def normalize(values):
    center = values - jnp.mean(values, axis=-1, keepdims=True)
    spread = jnp.mean(center * center, axis=-1, keepdims=True)
    inverse = lax.rsqrt(spread + 1e-05)
    return center * inverse, inverse


def normalize_back(grad, normal, inverse):
    return inverse * (
        grad
        - jnp.mean(grad, axis=-1, keepdims=True)
        - normal * jnp.mean(grad * normal, axis=-1, keepdims=True)
    )


def gelu_pair(values):
    phi = 0.5 * (1.0 + lax.erf(values * 0.7071067811865476))
    density = jnp.exp(-0.5 * values * values) * 0.3989422804014327
    return values * phi, phi + values * density


class Net:
    def __init__(self, count):
        self.count = count
        self.bits = count.bit_length() - 1
        self.me = lax.axis_index(AXES)

    def bit(self, b):
        return (self.me >> b) & 1

    def hop(self, value, b):
        return lax.ppermute(value, AXES, [(i, i ^ (1 << b)) for i in range(self.count)])

    def grow(self, value, b, axis):
        other = self.hop(value, b)
        return jnp.where(
            self.bit(b) == 0,
            jnp.concatenate([value, other], axis),
            jnp.concatenate([other, value], axis),
        )

    def pick(self, value, which, axis):
        return lax.dynamic_slice_in_dim(value, which, 1, axis)

    def halve(self, value, b, axis, dtype):
        other = self.hop(self.pick(value, 1 - self.bit(b), axis), b)
        keep = self.pick(value, self.bit(b), axis)
        return (keep.astype(F32) + other.astype(F32)).astype(dtype)

    def trade(self, value, b, axis):
        other = self.hop(self.pick(value, 1 - self.bit(b), axis), b)
        keep = self.pick(value, self.bit(b), axis)
        return jnp.where(
            self.bit(b) == 0,
            jnp.concatenate([keep, other], axis),
            jnp.concatenate([other, keep], axis),
        )

    def total(self, value, bit_list):
        for b in bit_list:
            value = value + self.hop(value, b)
        return value


def place_blocks(net, parts, rows, width):
    arrays = [part[0] for part in parts]

    def body(me_ref, *refs):
        sources, target, sem = refs[: len(parts)], refs[len(parts)], refs[len(parts) + 1]
        me = me_ref[0]
        copies = []
        for source, (array, masks, col) in zip(sources, parts):
            for j, mask in enumerate(masks):
                copies.append(
                    pltpu.make_async_copy(
                        source.at[j],
                        target.at[me ^ mask, :, pl.ds(col, array.shape[2])],
                        sem,
                    )
                )
        for copy in copies:
            copy.start()
        pltpu.make_async_copy(target, target, sem).wait()

    return pl.pallas_call(
        body,
        out_shape=jax.ShapeDtypeStruct((net.count, rows, width), BF16),
        in_specs=[pl.BlockSpec(memory_space=pltpu.SMEM)]
        + [pl.BlockSpec(memory_space=pl.ANY)] * len(parts),
        out_specs=pl.BlockSpec(memory_space=pl.ANY),
        scratch_shapes=[pltpu.SemaphoreType.DMA],
        name="place_blocks",
    )(net.me.reshape(1), *arrays)


def link_orders(net):
    high = [net.bits - 1, net.bits - 2]
    mid = list(range(1, net.bits - 2))
    return high + mid, high + mid[::-1]


def gather_rows(net, shard):
    rows, width = shard.shape
    if rows % 8:
        return lax.all_gather(shard, AXES, axis=0, tiled=True)
    cut = (width // 256) * 128
    parts = []
    for order, col, end in zip(link_orders(net), (0, cut), (cut, width)):
        have, masks = shard[None, :, col:end], [0]
        for b in order[:-1]:
            have = jnp.concatenate([have, net.hop(have, b)], 0)
            masks = masks + [m ^ (1 << b) for m in masks]
        last = order[-1]
        late = net.hop(have, last)
        late_masks = [m ^ (1 << last) for m in masks]
        parts.append((have, masks, col))
        parts.append((net.hop(have, 0), [m ^ 1 for m in masks], col))
        parts.append((late, late_masks, col))
        parts.append((net.hop(late, 0), [m ^ 1 for m in late_masks], col))
    return place_blocks(net, parts, rows, width).reshape(net.count * rows, width)


def scatter_rows(net, grad):
    width = grad.shape[1]
    rows = grad.shape[0] // net.count
    cube = grad.reshape((2,) * net.bits + (rows, width))
    cube = net.halve(cube, 0, net.bits - 1, BF16)
    cut = (width // 256) * 128
    out = []
    for order, col, end in zip(link_orders(net), (0, cut), (cut, width)):
        half = cube[..., col:end]
        for step, b in enumerate(order[::-1]):
            last = step == len(order) - 1
            half = net.halve(half, b, net.bits - 1 - b, F32 if last else BF16)
        out.append(half.reshape(rows, end - col))
    return jnp.concatenate(out, 1)


def head_probability(qkv_ref, head, heads):
    width = heads * HDIM
    queries = qkv_ref[:, head * HDIM : (head + 1) * HDIM]
    keys = qkv_ref[:, width + head * HDIM : width + (head + 1) * HDIM]
    values = qkv_ref[:, 2 * width + head * HDIM : 2 * width + (head + 1) * HDIM]
    scores = dot(queries, keys, ((1,), (1,))) * SCALE
    raised = jnp.exp(scores - jnp.max(scores, axis=-1, keepdims=True))
    chance = raised / jnp.sum(raised, axis=-1, keepdims=True)
    return queries, keys, values, chance


def attend_forward_body(heads, qkv_ref, out_ref):
    for pair in range(heads // 2):
        both = []
        for head in (2 * pair, 2 * pair + 1):
            _, _, values, chance = head_probability(qkv_ref, head, heads)
            both.append(dot(chance.astype(BF16), values))
        out_ref[:, pair * 128 : (pair + 1) * 128] = jnp.concatenate(both, 1).astype(BF16)


def attend_backward_body(heads, qkv_ref, grad_ref, out_ref, sums_ref):
    width = heads * HDIM
    for pair in range(heads // 2):
        got = ([], [], [])
        for head in (2 * pair, 2 * pair + 1):
            queries, keys, values, chance = head_probability(qkv_ref, head, heads)
            grad = grad_ref[:, head * HDIM : (head + 1) * HDIM]
            slope = dot(grad, values, ((1,), (1,)))
            slope = slope - jnp.sum(slope * chance, axis=-1, keepdims=True)
            tilt = (chance * slope).astype(BF16)
            got[0].append(dot(tilt, keys) * SCALE)
            got[1].append(dot(tilt, queries, ((0,), (0,))) * SCALE)
            got[2].append(dot(chance.astype(BF16), grad, ((0,), (0,))))
        for part in range(3):
            low = jnp.concatenate(got[part], 1).astype(BF16)
            at = part * width + pair * 128
            out_ref[:, at : at + 128] = low
            sums_ref[0, :, at : at + 128] = jnp.sum(low.astype(F32), axis=0, keepdims=True)


def segment_attend(qkv):
    rows, width = qkv.shape[0], qkv.shape[1] // 3
    return pl.pallas_call(
        partial(attend_forward_body, width // HDIM),
        out_shape=jax.ShapeDtypeStruct((rows, width), BF16),
        grid=(rows // SEG,),
        in_specs=[pl.BlockSpec((SEG, 3 * width), lambda i: (i, 0))],
        out_specs=pl.BlockSpec((SEG, width), lambda i: (i, 0)),
        name="segment_attend",
    )(qkv)


def segment_attend_back(qkv, grad):
    rows, width = grad.shape
    return pl.pallas_call(
        partial(attend_backward_body, width // HDIM),
        out_shape=(
            jax.ShapeDtypeStruct((rows, 3 * width), BF16),
            jax.ShapeDtypeStruct((rows // SEG, 1, 3 * width), F32),
        ),
        grid=(rows // SEG,),
        in_specs=[
            pl.BlockSpec((SEG, 3 * width), lambda i: (i, 0)),
            pl.BlockSpec((SEG, width), lambda i: (i, 0)),
        ],
        out_specs=(
            pl.BlockSpec((SEG, 3 * width), lambda i: (i, 0)),
            pl.BlockSpec((1, 1, 3 * width), lambda i: (i, 0, 0)),
        ),
        name="segment_attend_back",
    )(qkv, grad)


def tail_forward(hidden, context, w_out, w_up, w_down, biases, up_bias, gains):
    mixed = hidden.astype(F32) + dot(context, w_out) + biases[2]
    normal1, inverse1 = normalize(mixed)
    normed = normal1 * gains[0] + biases[3]
    normed_low = normed.astype(BF16)
    active, slope = gelu_pair(dot(normed_low, w_up) + up_bias)
    active = active.astype(BF16)
    slope = slope.astype(BF16)
    second = normed + dot(active, w_down) + biases[4]
    normal2, inverse2 = normalize(second)
    result = normal2 * gains[1] + biases[5]
    return result, (normal1, inverse1, normed_low, active, slope, normal2, inverse2)


def tail_backward(grad, kept, w_out, w_up, w_down, gains):
    normal1, inverse1, _, _, slope, normal2, inverse2 = kept
    gain2, shift2 = jnp.sum(grad * normal2, axis=0), jnp.sum(grad, axis=0)
    grad_second = normalize_back(grad * gains[1], normal2, inverse2)
    grad_ffn = grad_second.astype(BF16)
    grad_before = (dot(grad_ffn, w_down, ((1,), (1,))) * slope.astype(F32)).astype(BF16)
    grad_normed = grad_second + dot(grad_before, w_up, ((1,), (1,)))
    gain1, shift1 = jnp.sum(grad_normed * normal1, axis=0), jnp.sum(grad_normed, axis=0)
    grad_mixed = normalize_back(grad_normed * gains[0], normal1, inverse1)
    grad_attn = grad_mixed.astype(BF16)
    grad_context = dot(grad_attn, w_out, ((1,), (1,))).astype(BF16)
    sums = (gain1, shift1, gain2, shift2)
    return grad_ffn, grad_before, grad_mixed, grad_attn, grad_context, sums


def column_sums(values):
    return jnp.sum(values.astype(F32), axis=0)


def cross_weights(net, w_qkv, w_out, w_up, w_down):
    rows, width = w_out.shape
    hi, lo = net.bits - 1, net.bits - 2
    plane = net.bits - 2
    part = width // TP
    hidden = w_up.shape[1] // TP
    cols = jnp.concatenate(
        [
            w_qkv.reshape(rows, 3, TP, part).transpose(2, 0, 1, 3).reshape(TP, rows, 3 * part),
            w_up.reshape(rows, TP, hidden).transpose(1, 0, 2),
        ],
        2,
    )
    cols = cols.reshape(2, 2, rows, 3 * part + hidden)
    cols = net.trade(net.trade(cols, hi, 0), lo, 1)
    cols = cols.reshape((TP,) + (1,) * plane + (rows, 3 * part + hidden))
    deep = jnp.concatenate([w_out, w_down], 0)
    deep = deep.reshape((1,) * plane + deep.shape)
    up = list(range(1, plane))
    for b in up + [0]:
        cols = net.grow(cols, b, plane - b)
    for b in up[::-1] + [0]:
        deep = net.grow(deep, b, plane - 1 - b)
    cols = cols.reshape(width, 3 * part + hidden)
    deep = deep.reshape(net.count // TP, -1, width)
    return (
        cols[:, : 3 * part],
        deep[:, :rows].reshape(part, width),
        cols[:, 3 * part :],
        deep[:, rows:].reshape(hidden, width),
    )


def cross_weight_grads(net, grad_qkv, grad_out, grad_up, grad_down):
    hi, lo = net.bits - 1, net.bits - 2
    plane = net.bits - 2
    planes = net.count // TP
    width = grad_qkv.shape[0]
    part = grad_out.shape[0]
    hidden = grad_down.shape[0]
    rows = width // net.count
    cols = jnp.concatenate([grad_qkv, grad_up], 1)
    cols = cols.reshape((TP,) + (2,) * plane + (rows, 3 * part + hidden))
    deep = jnp.concatenate(
        [grad_out.reshape(planes, rows, width), grad_down.reshape(planes, -1, width)], 1
    )
    deep = deep.reshape((2,) * plane + deep.shape[1:])
    up = list(range(1, plane))
    for b in [0] + up[::-1]:
        cols = net.halve(cols, b, plane - b, BF16)
    for step, b in enumerate([0] + up):
        deep = net.halve(deep, b, plane - 1 - b, F32 if step == plane - 1 else BF16)
    cols = cols.reshape(2, 2, rows, 3 * part + hidden)
    cols = net.trade(net.trade(cols, hi, 0), lo, 1).astype(F32)
    cols = cols.reshape(TP, rows, 3 * part + hidden)
    deep = deep.reshape(-1, width)
    return (
        cols[:, :, : 3 * part].reshape(TP, rows, 3, part).transpose(1, 2, 0, 3).reshape(rows, -1),
        deep[:rows],
        cols[:, :, 3 * part :].transpose(1, 0, 2).reshape(rows, -1),
        deep[rows:],
    )


def split_heads(values):
    return values.reshape(values.shape[0], values.shape[1] // HDIM, HDIM)


def cross_encoder(net, cross_in, grad_out, weights, biases, up_bias, gains, seq_ids):
    w_qkv, w_out, w_up, w_down = weights
    own, width = cross_in.shape
    part, hidden = w_out.shape[0], w_down.shape[0]
    planes = net.count // TP
    plane = net.bits - 2
    hi, lo = net.bits - 1, net.bits - 2
    member = net.me >> lo
    here = net.me & (planes - 1)
    up = list(range(1, plane))

    def share(values):
        return net.grow(net.grow(values, lo, 0), hi, 0)

    def mine(values):
        return lax.dynamic_slice_in_dim(values, member * own, own, 0)

    def slab(vector, size):
        return lax.dynamic_slice_in_dim(vector, member * size, size, 0)

    grad_all = share(grad_out).astype(F32)
    hidden_all = share(cross_in)
    hidden_low = hidden_all.astype(BF16)
    projected = dot(hidden_low, w_qkv)
    queries = (projected[:, :part] + slab(biases[0], part)).astype(BF16)
    key_rows = projected[:, part : 2 * part].astype(BF16)
    value_rows = (projected[:, 2 * part :] + slab(biases[1], part)).astype(BF16)
    both = jnp.concatenate([key_rows, value_rows], 1)
    count = both.shape[0]
    both = both.reshape((1,) * plane + both.shape)
    for b in [0] + up:
        both = net.grow(both, b, plane - 1 - b)
    both = both.reshape(planes * count, 2 * part)
    all_keys, all_values = split_heads(both[:, :part]), split_heads(both[:, part:])
    slots = seq_ids.reshape(TP, planes, own)
    key_ids = slots.transpose(1, 0, 2).reshape(-1)
    row_ids = lax.dynamic_slice_in_dim(slots, here, 1, 1).reshape(-1)
    allowed = row_ids[:, None] == key_ids[None, :]
    heads_q = split_heads(queries)
    scores = jnp.einsum("qhd,khd->hqk", heads_q, all_keys, preferred_element_type=F32) * SCALE
    scores = jnp.where(allowed[None], scores, -1e30)
    raised = jnp.exp(scores - jnp.max(scores, axis=-1, keepdims=True))
    chance = raised / jnp.sum(raised, axis=-1, keepdims=True)
    chance_low = chance.astype(BF16)
    context = jnp.einsum("hqk,khd->qhd", chance_low, all_values, preferred_element_type=F32)
    context = context.reshape(count, part).astype(BF16)
    mixed = hidden_all + net.total(dot(context, w_out), (lo, hi)) + biases[2]
    normal1, inverse1 = normalize(mixed)
    normed = normal1 * gains[0] + biases[3]
    normed_low = normed.astype(BF16)
    active, slope = gelu_pair(dot(normed_low, w_up) + slab(up_bias, hidden))
    active = active.astype(BF16)
    second = normed + net.total(dot(active, w_down), (lo, hi)) + biases[4]
    normal2, inverse2 = normalize(second)
    result = mine(normal2 * gains[1] + biases[5])

    grad_second = normalize_back(grad_all * gains[1], normal2, inverse2)
    grad_ffn = grad_second.astype(BF16)
    grad_before = (dot(grad_ffn, w_down, ((1,), (1,))) * slope).astype(BF16)
    grad_down = dot(active, grad_ffn, ((0,), (0,))).astype(BF16)
    grad_up = dot(normed_low, grad_before, ((0,), (0,))).astype(BF16)
    grad_normed = grad_second + net.total(dot(grad_before, w_up, ((1,), (1,))), (lo, hi))
    grad_mixed = normalize_back(grad_normed * gains[0], normal1, inverse1)
    grad_attn = grad_mixed.astype(BF16)
    grad_wout = dot(context, grad_attn, ((0,), (0,))).astype(BF16)
    grad_context = split_heads(dot(grad_attn, w_out, ((1,), (1,))).astype(BF16))
    slopes = jnp.einsum("qhd,khd->hqk", grad_context, all_values, preferred_element_type=F32)
    slopes = slopes - jnp.sum(slopes * chance, axis=-1, keepdims=True)
    tilt = (chance * slopes).astype(BF16)
    grad_q = jnp.einsum("hqk,khd->qhd", tilt, all_keys, preferred_element_type=F32) * SCALE
    part_k = jnp.einsum("hqk,qhd->khd", tilt, heads_q, preferred_element_type=F32) * SCALE
    part_v = jnp.einsum("hqk,qhd->khd", chance_low, grad_context, preferred_element_type=F32)
    both = jnp.concatenate([part_k.reshape(-1, part), part_v.reshape(-1, part)], 1)
    both = both.reshape((2,) * plane + (count, 2 * part))
    for b in [0] + up[::-1]:
        both = net.halve(both, b, plane - 1 - b, F32)
    both = both.reshape(count, 2 * part)
    grad_qkv = jnp.concatenate([grad_q.reshape(count, part), both], 1).astype(BF16)
    grad_wqkv = dot(hidden_low, grad_qkv, ((0,), (0,))).astype(BF16)
    back = dot(grad_qkv, w_qkv, ((1,), (1,))).reshape(2, 2, own, width)
    back = net.halve(net.halve(back, hi, 0, F32), lo, 1, F32).reshape(own, width)
    grad_in = mine(grad_mixed) + back

    def spread(vector, size):
        return lax.dynamic_update_slice_in_dim(jnp.zeros((size * TP,), F32), vector, member * size, 0)

    grad_own = mine(grad_all)
    normed_own = mine(grad_normed)
    bias_rows = jnp.stack(
        [
            spread(column_sums(grad_qkv[:, :part]), part),
            spread(column_sums(grad_qkv[:, 2 * part :]), part),
            column_sums(mine(grad_attn)),
            column_sums(normed_own),
            column_sums(mine(grad_ffn)),
            column_sums(grad_own),
        ]
    )
    gain_rows = jnp.stack(
        [column_sums(normed_own * mine(normal1)), column_sums(grad_own * mine(normal2))]
    )
    up_row = spread(column_sums(grad_before), hidden)
    return (
        result,
        grad_in,
        (grad_wqkv, grad_wout, grad_up, grad_down),
        (bias_rows, up_row, gain_rows),
    )


def pack_small(count, bias_rows, up_row, gain_rows):
    flat = jnp.concatenate(
        [
            bias_rows.reshape(6, count, -1).transpose(1, 0, 2).reshape(count, -1),
            up_row.reshape(count, -1),
            gain_rows.reshape(2, count, -1).transpose(1, 0, 2).reshape(count, -1),
        ],
        1,
    )
    return flat


def unpack_small(flat, share, hidden):
    lead = flat.shape[:-1]
    return (
        flat[..., : 6 * share].reshape(lead + (6, share)),
        flat[..., 6 * share : 6 * share + hidden],
        flat[..., 6 * share + hidden :].reshape(lead + (2, share)),
    )


def scatter_small(net, flat):
    cube = flat.reshape((2,) * net.bits + flat.shape[1:])
    for b in range(net.bits):
        cube = net.halve(cube, b, net.bits - 1 - b, F32)
    return cube.reshape(flat.shape[1:])


def gather_small(net, flat):
    cube = flat.reshape((1,) * net.bits + flat.shape)
    for b in list(range(1, net.bits)) + [0]:
        cube = net.grow(cube, b, net.bits - 1 - b)
    return cube.reshape((net.count,) + flat.shape)


def places_of(local_ids, local_slots, seq_ids, table_rows):
    all_slots = jnp.arange(seq_ids.shape[0], dtype=jnp.int32)
    earlier = (seq_ids[None, :] == local_ids[:, None]) & (all_slots[None, :] < local_slots[:, None])
    places = jnp.sum(earlier.astype(jnp.int32), axis=1)
    return places[:, None] == table_rows[None, :]


def shards(
    count, tokens, seq_ids, w_qkv, w_out, w_up, w_down, biases, up_bias, norm_gains, pos_table, cotangent
):
    net = Net(count)
    rows_here, width = tokens.shape
    segs_here = rows_here // SEG
    share, hidden = biases.shape[2], up_bias.shape[1]
    first_seg = net.me * segs_here
    local_ids = lax.dynamic_slice_in_dim(seq_ids, first_seg, segs_here)
    table_rows = jnp.arange(pos_table.shape[0], dtype=jnp.int32)
    local_slots = first_seg + jnp.arange(segs_here, dtype=jnp.int32)
    onehot = places_of(local_ids, local_slots, seq_ids, table_rows)

    small = jnp.concatenate(
        [
            pos_table.T.reshape(-1),
            *[
                jnp.concatenate([biases[e].reshape(-1), up_bias[e], norm_gains[e].reshape(-1)])
                for e in (0, 1)
            ],
        ]
    )
    table_size = pos_table.size
    small = jnp.pad(small, (0, -small.size % 128)).reshape(-1, 128)
    small = gather_small(net, small).reshape(count, -1)
    table = small[:, :table_size].reshape(width, pos_table.shape[0])
    each = 8 * share + hidden
    params = []
    for e in (0, 1):
        piece = small[:, table_size + e * each : table_size + (e + 1) * each].astype(F32)
        b, u, g = unpack_small(piece, share, hidden)
        params.append(
            (
                b.transpose(1, 0, 2).reshape(6, width),
                u.reshape(-1),
                g.transpose(1, 0, 2).reshape(2, width),
            )
        )
    biases0, up_bias0, gains0 = params[0]

    w_qkv0 = gather_rows(net, w_qkv[0])
    w_out0 = gather_rows(net, w_out[0])
    w_up0 = gather_rows(net, w_up[0])
    w_down0 = gather_rows(net, w_down[0])
    weights1 = cross_weights(net, w_qkv[1], w_out[1], w_up[1], w_down[1])

    projected = dot(tokens, w_qkv0)
    shift = jnp.concatenate([biases0[0], jnp.zeros((width,), F32), biases0[1]])
    qkv = (projected + shift).astype(BF16)
    context = segment_attend(qkv)
    result0, kept = tail_forward(tokens, context, w_out0, w_up0, w_down0, biases0, up_bias0, gains0)
    blocked = result0.reshape(segs_here, SEG, width)
    cross_in = blocked[:, 0, :] + dot(onehot.astype(BF16), table, ((1,), (1,)))
    grad_rows = cotangent.reshape(segs_here, SEG, width)
    result1, grad_cross, grads1, small1 = cross_encoder(
        net, cross_in, grad_rows[:, 0, :], weights1, *params[1], seq_ids
    )
    layer_out = blocked.at[:, 0, :].set(result1).reshape(rows_here, width).astype(BF16)

    shares1 = cross_weight_grads(net, *grads1)
    grad_places = lax.dot_general(
        grad_cross,
        onehot.astype(F32),
        (((0,), (0,)), ((), ())),
        precision=lax.Precision.HIGHEST,
        preferred_element_type=F32,
    ).reshape(count, -1)
    packed1 = scatter_small(net, jnp.concatenate([grad_places, pack_small(count, *small1)], 1))

    grad_segment = grad_rows.astype(F32).at[:, 0, :].set(grad_cross).reshape(rows_here, width)
    grad_ffn, grad_before, grad_mixed, grad_attn, grad_context, sums = tail_backward(
        grad_segment, kept, w_out0, w_up0, w_down0, gains0
    )
    _, _, normed_low, active, _, _, _ = kept
    grad_down0 = scatter_rows(net, dot(active, grad_ffn, ((0,), (0,))).astype(BF16))
    grad_up0 = scatter_rows(net, dot(normed_low, grad_before, ((0,), (0,))).astype(BF16))
    grad_out0 = scatter_rows(net, dot(context, grad_attn, ((0,), (0,))).astype(BF16))
    grad_qkv, qkv_sums = segment_attend_back(qkv, grad_context)
    qkv_sums = jnp.sum(qkv_sums, axis=(0, 1))
    grad_qkv0 = scatter_rows(net, dot(tokens, grad_qkv, ((0,), (0,))).astype(BF16))
    grad_tokens = (grad_mixed + dot(grad_qkv, w_qkv0, ((1,), (1,)))).astype(BF16)
    gain1, shift1, gain2, shift2 = sums
    packed0 = scatter_small(
        net,
        pack_small(
            count,
            jnp.stack(
                [
                    qkv_sums[:width],
                    qkv_sums[2 * width :],
                    column_sums(grad_attn),
                    shift1,
                    column_sums(grad_ffn),
                    shift2,
                ]
            ),
            column_sums(grad_before),
            jnp.stack([gain1, gain2]),
        ),
    )
    small0 = unpack_small(packed0, share, hidden)
    small1 = unpack_small(packed1[table_size:], share, hidden)
    return (
        layer_out,
        grad_tokens,
        jnp.stack([grad_qkv0, shares1[0]]),
        jnp.stack([grad_out0, shares1[1]]),
        jnp.stack([grad_up0, shares1[2]]),
        jnp.stack([grad_down0, shares1[3]]),
        jnp.stack([small0[0], small1[0]]),
        jnp.stack([small0[1], small1[1]]),
        jnp.stack([small0[2], small1[2]]),
        packed1[:table_size].reshape(share, -1).T,
    )


def solution(mesh):
    count = mesh.shape["ctx"] * mesh.shape["wa"]
    in_specs = (
        P(AXES, None),
        P(),
        P(None, AXES, None),
        P(None, AXES, None),
        P(None, AXES, None),
        P(None, AXES, None),
        P(None, None, AXES),
        P(None, AXES),
        P(None, None, AXES),
        P(None, AXES),
        P(AXES, None),
    )
    out_specs = (
        P(AXES, None),
        P(AXES, None),
        P(None, AXES, None),
        P(None, AXES, None),
        P(None, AXES, None),
        P(None, AXES, None),
        P(None, None, AXES),
        P(None, AXES),
        P(None, None, AXES),
        P(None, AXES),
    )
    return jax.shard_map(
        partial(shards, count), mesh=mesh, in_specs=in_specs, out_specs=out_specs, check_vma=False
    )
```

```python
from functools import partial

import jax
import jax.numpy as jnp
from jax import lax
from jax.experimental import pallas as pl
from jax.experimental.pallas import tpu as pltpu
from jax.sharding import PartitionSpec as P

HDIM = 64
SEG = 128
TP = 4
AXES = ("ctx", "wa")
F32 = jnp.float32
BF16 = jnp.bfloat16
SCALE = HDIM ** (-0.5)


def dot(a, b, dims=((1,), (0,))):
    return lax.dot_general(a, b, (dims, ((), ())), preferred_element_type=F32)


def normalize(values):
    center = values - jnp.mean(values, axis=-1, keepdims=True)
    spread = jnp.mean(center * center, axis=-1, keepdims=True)
    inverse = lax.rsqrt(spread + 1e-05)
    return center * inverse, inverse


def normalize_back(grad, normal, inverse):
    return inverse * (
        grad
        - jnp.mean(grad, axis=-1, keepdims=True)
        - normal * jnp.mean(grad * normal, axis=-1, keepdims=True)
    )


def gelu_pair(values):
    phi = 0.5 * (1.0 + lax.erf(values * 0.7071067811865476))
    density = jnp.exp(-0.5 * values * values) * 0.3989422804014327
    return values * phi, phi + values * density


class Net:
    def __init__(self, count):
        self.count = count
        self.bits = count.bit_length() - 1
        self.me = lax.axis_index(AXES)

    def bit(self, b):
        return (self.me >> b) & 1

    def hop(self, value, b):
        return lax.ppermute(value, AXES, [(i, i ^ (1 << b)) for i in range(self.count)])

    def grow(self, value, b, axis):
        other = self.hop(value, b)
        return jnp.where(
            self.bit(b) == 0,
            jnp.concatenate([value, other], axis),
            jnp.concatenate([other, value], axis),
        )

    def pick(self, value, which, axis):
        return lax.dynamic_slice_in_dim(value, which, 1, axis)


def tie(*values):
    return lax.optimization_barrier(values)


def place_blocks(net, parts, blocks, shapes):
    arrays = [part[0] for part in parts]

    def body(me_ref, *refs):
        sources = refs[: len(parts)]
        targets = refs[len(parts) : len(parts) + len(shapes)]
        sem = refs[-1]
        me = me_ref[0]
        for source, (array, masks, half) in zip(sources, parts):
            for j, mask in enumerate(masks):
                for row, rows, lane, lanes, which, to_row, to_lane in blocks(half):
                    pltpu.make_async_copy(
                        source.at[j, pl.ds(row, rows), pl.ds(lane, lanes)],
                        targets[which].at[me ^ mask, pl.ds(to_row, rows), pl.ds(to_lane, lanes)],
                        sem,
                    ).start()
        for target in targets:
            pltpu.make_async_copy(target, target, sem).wait()

    return pl.pallas_call(
        body,
        out_shape=[jax.ShapeDtypeStruct(shape, BF16) for shape in shapes],
        in_specs=[pl.BlockSpec(memory_space=pltpu.SMEM)]
        + [pl.BlockSpec(memory_space=pl.ANY)] * len(parts),
        out_specs=[pl.BlockSpec(memory_space=pltpu.VMEM)] * len(shapes),
        scratch_shapes=[pltpu.SemaphoreType.DMA],
        name="place_blocks",
    )(net.me.reshape(1), *arrays)


def link_orders(net):
    mid = list(range(1, net.bits - 2))
    return mid, mid[::-1]


class Task:
    def __init__(self, steps):
        self.steps, self.flight, self.result = steps, None, None
        self.advance(None)

    def advance(self, arrived):
        try:
            self.flight = list(self.steps.send(arrived))
        except StopIteration as stop:
            self.flight, self.result = [], stop.value

    def get(self):
        while self.flight:
            self.advance(self.flight)
        return self.result


def window(values, tasks):
    done = tie(*values, *[f for task in tasks for f in task.flight])
    at = len(values)
    for task in tasks:
        size = len(task.flight)
        if size:
            task.advance(list(done[at : at + size]))
        at += size
    return done[: len(values)]


def gather_steps(net, have, high):
    have, masks = have[None], [0]
    for b in high:
        (other,) = yield [net.hop(have, b)]
        have = jnp.concatenate([have, other], 0)
        masks = masks + [m ^ (1 << b) for m in masks]
    cut = have.shape[2] // 2
    halves = [have[:, :, :cut], have[:, :, cut:]]
    orders = link_orders(net)
    lists = [masks, masks]
    for step in range(len(orders[0]) - 1):
        others = yield [net.hop(h, o[step]) for h, o in zip(halves, orders)]
        halves = [jnp.concatenate([h, o], 0) for h, o in zip(halves, others)]
        lists = [l + [m ^ (1 << o[step]) for m in l] for l, o in zip(lists, orders)]
    last = [o[-1] for o in orders]
    late = yield [net.hop(h, b) for h, b in zip(halves, last)]
    core = yield [net.hop(h, 0) for pair in zip(halves, late) for h in pair]
    parts = []
    for n in (0, 1):
        late_list = [m ^ (1 << last[n]) for m in lists[n]]
        parts.append((halves[n], lists[n], n))
        parts.append((core[2 * n], [m ^ 1 for m in lists[n]], n))
        parts.append((late[n], late_list, n))
        parts.append((core[2 * n + 1], [m ^ 1 for m in late_list], n))
    return parts


def stack_columns(width, *shares):
    pieces = []
    for share in shares:
        for at in range(0, share.shape[1], width):
            pieces.append(share[:, at : at + width])
    return jnp.concatenate(pieces, 0)


def flat_rows(out):
    return out.reshape(-1, out.shape[2])


def pack_small(table, small):
    small = jnp.pad(small, ((0, 0), (0, 128 - small.shape[1])))
    return jnp.concatenate([v[i : i + 8] for v in (table, small) for i in (0, 8, 16)], 1)


def gather_first(net, w_qkv, table, small, packed):
    rows, width = w_qkv.shape[0], w_qkv.shape[1] // 3
    half = width // 2
    if packed is None:
        cube = lax.all_gather(w_qkv, AXES, axis=0, tiled=True).reshape(width, 3, 2, half)
        return (
            cube[:, :, 0].reshape(width, -1),
            cube[:, :, 1].reshape(width, -1),
            lax.all_gather(table, AXES, axis=0, tiled=True),
            lax.all_gather(small, AXES, axis=0),
        )
    parts = yield from gather_steps(net, packed, (net.bits - 1, net.bits - 2))
    left, right, table, small = place_blocks(
        net,
        parts,
        lambda h: [(i * rows, rows, 0, half, h, 0, i * half) for i in range(3)]
        + [(3 * rows, 8, i * 128, 128, 2 + h, i * 8, 0) for i in range(3)],
        [(net.count, rows, 3 * half)] * 2 + [(net.count, 24, 128)] * 2,
    )
    return flat_rows(left), flat_rows(right), flat_rows(table), small[:, :, :rows]


def gather_rest(net, w_out, w_up, w_down, packed):
    rows, width = w_out.shape
    if packed is None:
        return [lax.all_gather(w, AXES, axis=0, tiled=True) for w in (w_out, w_up, w_down)]
    parts = yield from gather_steps(net, packed, (net.bits - 1, net.bits - 2))
    columns = w_up.shape[1] // width
    half = width // 2
    out, up, down = place_blocks(
        net,
        parts,
        lambda h: [(0, rows, 0, half, 0, 0, h * half)]
        + [((i + 1) * rows, rows, 0, half, 1, 0, i * width + h * half) for i in range(columns)]
        + [((columns + 1) * rows, w_down.shape[0], 0, half, 2, 0, h * half)],
        [(net.count,) + w.shape for w in (w_out, w_up, w_down)],
    )
    return flat_rows(out), flat_rows(up), flat_rows(down)


def settle(keep, other, dtype=BF16):
    return (keep.astype(F32) + other.astype(F32)).astype(dtype)


def reduce_steps(net, grads, order):
    axis = lambda b: net.bits - 1 - b
    cubes = [g.reshape((2,) * net.bits + (g.shape[0] // net.count, g.shape[1])) for g in grads]
    widths = [g.shape[1] for g in grads]
    join = lambda values: jnp.concatenate(values, -1) if len(values) > 1 else values[0]
    arrived = yield [net.hop(net.pick(c, 1 - net.bit(0), axis(0)), 0) for c in cubes]
    pairs = [(net.pick(c, net.bit(0), axis(0)), f) for c, f in zip(cubes, arrived)]
    for n, b in enumerate(order):
        side = lambda which: join(
            [settle(net.pick(k, which, axis(b)), net.pick(f, which, axis(b))) for k, f in pairs]
        )
        sent, kept = side(1 - net.bit(b)), side(net.bit(b))
        (other,) = yield [net.hop(sent, b)]
        pairs = [(kept, other)]
    whole = settle(*pairs[0], F32)
    whole = whole.reshape(whole.shape[-2:])
    out, at = [], 0
    for w in widths:
        out.append(whole[:, at : at + w])
        at += w
    return out


def total_steps(net, value):
    for b in [0] + list(range(1, net.bits)):
        (other,) = yield [net.hop(value, b)]
        value = value + other
    return value


def ordered(net, value, other, b, axis):
    return jnp.where(
        net.bit(b) == 0,
        jnp.concatenate([value, other], axis),
        jnp.concatenate([other, value], axis),
    )


def trade_pair(net, value, b, axis):
    return net.hop(net.pick(value, 1 - net.bit(b), axis), b), net.pick(value, net.bit(b), axis)


def dot_nt(a, b):
    return dot(a, b, ((1,), (1,)))


def dot_tn(a, b):
    return dot(a, b, ((0,), (0,)))


def pick_lanes(mask, values):
    return jnp.where(mask, values, jnp.zeros_like(values))


def head_masks(rows):
    lane = lax.broadcasted_iota(jnp.int32, (rows, 2 * HDIM), 1)
    return lane < HDIM, lane >= HDIM


def chance_of(keys, queries):
    scores = dot_nt(keys, queries) * SCALE
    raised = jnp.exp(scores - jnp.max(scores, axis=0, keepdims=True))
    return raised * (1.0 / jnp.sum(raised, axis=0, keepdims=True))


def attend_forward_body(heads, qkv_ref, out_ref):
    width = heads * HDIM
    for at in range(0, width, 2 * HDIM):
        queries, keys, values = [qkv_ref[:, n * width + at : n * width + at + 128] for n in range(3)]
        total = 0.0
        for mask in head_masks(SEG):
            chance = chance_of(pick_lanes(mask, keys), queries).astype(BF16)
            total = total + dot_tn(pick_lanes(mask, values), chance)
        out_ref[:, at : at + 128] = total.T.astype(BF16)


def attend_backward_body(heads, qkv_ref, grad_ref, out_ref, sums_ref):
    width = heads * HDIM
    for at in range(0, width, 2 * HDIM):
        queries, keys, values = [qkv_ref[:, n * width + at : n * width + at + 128] for n in range(3)]
        grad = grad_ref[:, at : at + 128]
        totals = [0.0, 0.0, 0.0]
        for mask in head_masks(SEG):
            own_keys = pick_lanes(mask, keys)
            chance = chance_of(own_keys, queries)
            slope = dot_nt(pick_lanes(mask, values), grad)
            slope = slope - jnp.sum(slope * chance, axis=0, keepdims=True)
            tilt = (chance * slope).astype(BF16)
            totals[0] = totals[0] + dot_tn(tilt, own_keys)
            totals[1] = totals[1] + dot(tilt, pick_lanes(mask, queries))
            totals[2] = totals[2] + dot(chance.astype(BF16), pick_lanes(mask, grad))
        for n, (total, scale) in enumerate(zip(totals, (SCALE, SCALE, 1.0))):
            low = (total * scale).astype(BF16)
            out_ref[:, n * width + at : n * width + at + 128] = low
            sums_ref[0, :, n * width + at : n * width + at + 128] = jnp.sum(
                low.astype(F32), axis=0, keepdims=True
            )


def segment_attend(qkv, half, context=None):
    rows, width = qkv.shape[0], qkv.shape[1] // 3

    def body(*refs):
        attend_forward_body(width // HDIM, refs[0], refs[-1])

    return pl.pallas_call(
        body,
        out_shape=jax.ShapeDtypeStruct((rows, 2 * width), BF16),
        grid=(rows // SEG,),
        in_specs=[pl.BlockSpec((SEG, 3 * width), lambda i: (i, 0))]
        + [pl.BlockSpec(memory_space=pl.ANY)] * half,
        out_specs=pl.BlockSpec((SEG, width), lambda i: (i, half)),
        input_output_aliases={1: 0} if half else {},
        name="segment_attend",
    )(*([qkv, context] if half else [qkv]))


def segment_attend_back(qkv, grad, half):
    rows, width = qkv.shape[0], qkv.shape[1] // 3
    return pl.pallas_call(
        partial(attend_backward_body, width // HDIM),
        out_shape=(
            jax.ShapeDtypeStruct((rows, 3 * width), BF16),
            jax.ShapeDtypeStruct((rows // SEG, 1, 3 * width), F32),
        ),
        grid=(rows // SEG,),
        in_specs=[
            pl.BlockSpec((SEG, 3 * width), lambda i: (i, 0)),
            pl.BlockSpec((SEG, width), lambda i: (i, half)),
        ],
        out_specs=(
            pl.BlockSpec((SEG, 3 * width), lambda i: (i, 0)),
            pl.BlockSpec((1, 1, 3 * width), lambda i: (i, 0, 0)),
        ),
        name="segment_attend_back",
    )(qkv, grad)


def column_sums(values):
    return jnp.sum(values.astype(F32), axis=0)


def cross_weight_steps(net, w_qkv, w_out, w_up, w_down):
    rows, width = w_out.shape
    hi, lo = net.bits - 1, net.bits - 2
    part = width // TP
    planes = net.count // TP
    cube = w_qkv.reshape(rows, 3, TP, part)
    ups = w_up.reshape(rows, TP, -1)
    hidden = ups.shape[2]
    assert hidden == width
    kvq = jnp.concatenate([cube[:, 1], cube[:, 2], cube[:, 0], jnp.zeros_like(cube[:, 0])], 2)
    cols = jnp.stack([ups, kvq]).transpose(2, 0, 1, 3).reshape(2, 2, 2 * rows, width)
    for b, axis in ((hi, 0), (lo, 1)):
        flight, keep = trade_pair(net, cols, b, axis)
        (other,) = yield [flight]
        cols = ordered(net, keep, other, b, axis)
    have = jnp.concatenate([cols.reshape(-1, width), w_out, w_down], 0)
    if rows % 8:
        value = have[None]
        for b in range(net.bits - 2):
            (other,) = yield [net.hop(value, b)]
            value = ordered(net, value, other, b, 0)
        cols = value[:, : 8 * rows].reshape(planes, TP, 2, rows, width).transpose(1, 0, 3, 2, 4)
        return (
            cols.reshape(width, 2 * width),
            value[:, 8 * rows : 9 * rows].reshape(part, width),
            value[:, 9 * rows :].reshape(hidden, width),
        )
    parts = yield from gather_steps(net, have, ())
    parts = [(array, [m & (planes - 1) for m in masks], h) for array, masks, h in parts]
    half = width // 2
    plane = Net.__new__(Net)
    plane.me = net.me & (planes - 1)
    outs = place_blocks(
        plane,
        parts,
        lambda h: [
            ((2 * t + k) * rows, rows, 0, half, t, 0, k * width + h * half)
            for t in range(TP)
            for k in (0, 1)
        ]
        + [
            (8 * rows, rows, 0, half, TP, 0, h * half),
            (9 * rows, 4 * rows, 0, half, TP + 1, 0, h * half),
        ],
        [(planes, rows, 2 * width)] * TP + [(planes, rows, width), (planes, 4 * rows, width)],
    )
    return (
        jnp.concatenate([flat_rows(o) for o in outs[:TP]], 0),
        flat_rows(outs[TP]),
        flat_rows(outs[TP + 1]),
    )


def cross_grad_steps(net, ups, rest, grad_out, grad_down, order):
    hi, lo = net.bits - 1, net.bits - 2
    plane = net.bits - 2
    planes = net.count // TP
    width = ups.shape[0]
    rows = width // net.count
    part = width // TP
    pair = jnp.stack([ups.reshape(TP, planes, rows, width), rest.reshape(TP, planes, rows, width)])
    whole = jnp.concatenate(
        [
            pair.transpose(2, 1, 0, 3, 4).reshape(planes, 8 * rows, width),
            grad_out.reshape(planes, rows, width),
            grad_down.reshape(planes, 4 * rows, width),
        ],
        1,
    ).reshape((2,) * plane + (13 * rows, width))
    axis = lambda b: plane - 1 - b
    (other,) = yield [net.hop(net.pick(whole, 1 - net.bit(0), axis(0)), 0)]
    kept = net.pick(whole, net.bit(0), axis(0))
    for b in order:
        side = lambda which: settle(net.pick(kept, which, axis(b)), net.pick(other, which, axis(b)))
        sent, kept = side(1 - net.bit(b)), side(net.bit(b))
        (other,) = yield [net.hop(sent, b)]
    whole = settle(kept, other).reshape(13 * rows, width)
    cols = whole[: 8 * rows].reshape(2, 2, 2 * rows, width)
    for b, at in ((hi, 0), (lo, 1)):
        flight, keep = trade_pair(net, cols, b, at)
        (back,) = yield [flight]
        cols = ordered(net, keep, back, b, at)
    whole, cols = yield [whole, cols]
    cols = cols.reshape(TP, 2, rows, width).transpose(1, 2, 0, 3).astype(F32)
    deep = whole[8 * rows :].astype(F32)
    pieces = [cols[1, :, :, n * part : (n + 1) * part].reshape(rows, width) for n in (2, 0, 1)]
    return (
        jnp.concatenate(pieces, 1),
        deep[:rows],
        cols[0].reshape(rows, -1),
        deep[rows:],
        cols[1, :, 0, 3 * part :],
    )


def lanes_between(values, first, last):
    lane = lax.broadcasted_iota(jnp.int32, values.shape, values.ndim - 1)
    return jnp.where((lane >= first) & (lane < last), values, jnp.zeros_like(values))


def stack_heads(values, heads, first):
    return jnp.concatenate(
        [lanes_between(values, first + h * HDIM, first + (h + 1) * HDIM) for h in range(heads)], 0
    )


def merge_heads(values, heads, first):
    rows = values.shape[0] // heads
    return sum(
        lanes_between(values[h * rows : (h + 1) * rows], first + h * HDIM, first + (h + 1) * HDIM)
        for h in range(heads)
    )


def fused(body, outs, *args, name):
    return pl.pallas_call(
        body, out_shape=[jax.ShapeDtypeStruct(shape, dtype) for shape, dtype in outs], name=name
    )(*args)


def cross_encoder(net, cross_in, grad_own, weights, params, allowed, onehot):
    cols, w_out, w_down = weights
    own, width = cross_in.shape
    part, hidden = w_out.shape[0], w_down.shape[0]
    plane = net.bits - 2
    hi, lo = net.bits - 1, net.bits - 2
    member = net.me >> lo
    up = list(range(1, plane))
    heads = part // HDIM
    biases, gains, up_bias = params
    row = lambda n: biases[n : n + 1]
    slab = lambda vector, size: lax.dynamic_slice_in_dim(vector, member * size, size, 1)
    bias_kv = jnp.concatenate([jnp.zeros((1, part), F32), slab(row(1), part)], 1)
    bias_q = slab(row(0), part)
    bias_up = slab(up_bias.reshape(1, -1), hidden)
    both = jnp.concatenate([cross_in, grad_own], 0)[None]
    both = net.grow(net.grow(both, lo, 0), hi, 0)
    count = TP * own
    full, wide, flat = (count, width), (count, 2 * part), (count, part)

    def project(x_ref, cols_ref, bias_kv_ref, bias_q_ref, hidden_ref, grad_ref, low_ref, kv_ref, q_ref):
        values = jnp.concatenate([x_ref[t, :own, :] for t in range(TP)], 0)
        hidden_ref[...] = values
        grad_ref[...] = jnp.concatenate([x_ref[t, own:, :] for t in range(TP)], 0)
        low = values.astype(BF16)
        low_ref[...] = low
        kv = dot(low, cols_ref[:, hidden : hidden + 2 * part]) + bias_kv_ref[...]
        kv_ref[...] = kv.astype(BF16)
        q_ref[...] = (dot(low, cols_ref[:, hidden + 2 * part : hidden + 3 * part]) + bias_q_ref[...]).astype(BF16)

    hidden_all, grad_all, hidden_low, kv, queries = fused(
        project,
        [(full, F32), (full, F32), (full, BF16), (wide, BF16), (flat, BF16)],
        both, cols, bias_kv, bias_q,
        name="cross_project",
    )
    have = kv
    for b in up:
        have = jnp.concatenate([have, net.hop(have, b)], 0)
    late = net.hop(have, 0)
    seen = 2 * have.shape[0]

    def attend(q_ref, have_ref, late_ref, allowed_ref, out_w_ref, chance_ref, context_ref, part_ref):
        kv = jnp.concatenate([have_ref[...], late_ref[...]], 0)
        q = q_ref[...]
        spread = stack_heads(jnp.concatenate([q, jnp.zeros_like(q)], 1), heads, 0)
        scores = dot_nt(spread, kv) * SCALE
        scores = jnp.where(jnp.concatenate([allowed_ref[...]] * heads, 0) > 0.5, scores, -1e30)
        raised = jnp.exp(scores - jnp.max(scores, axis=1, keepdims=True))
        chance = raised * (1.0 / jnp.sum(raised, axis=1, keepdims=True))
        chance_ref[...] = chance
        context = merge_heads(dot(chance.astype(BF16), kv), heads, part)[:, part:].astype(BF16)
        context_ref[...] = context
        part_ref[...] = dot(context, out_w_ref[...]).astype(BF16)

    chance, context, partial_sum = fused(
        attend,
        [((heads * count, seen), F32), (flat, BF16), (full, BF16)],
        queries, have, late, allowed, w_out,
        name="cross_attend",
    )
    half_sum = settle(partial_sum, net.hop(partial_sum, lo))
    other_sum = net.hop(half_sum, hi)

    def feed(
        x_ref, a_ref, b_ref, bias_ref, gain_ref, cols_ref, bias_up_ref, down_ref,
        normed_ref, normal_ref, inverse_ref, low_ref, active_ref, slope_ref, part_ref,
    ):
        mixed = x_ref[...] + (a_ref[...].astype(F32) + b_ref[...].astype(F32)) + bias_ref[2:3, :]
        normal, inverse = normalize(mixed)
        normed = normal * gain_ref[0:1, :] + bias_ref[3:4, :]
        low = normed.astype(BF16)
        active, slope = gelu_pair(dot(low, cols_ref[:, :hidden]) + bias_up_ref[...])
        active = active.astype(BF16)
        normed_ref[...] = normed
        normal_ref[...] = normal
        inverse_ref[...] = inverse
        low_ref[...] = low
        active_ref[...] = active
        slope_ref[...] = slope
        part_ref[...] = dot(active, down_ref[...]).astype(BF16)

    normed, normal1, inverse1, normed_low, active, slope, partial_sum = fused(
        feed,
        [
            (full, F32), (full, F32), ((count, 1), F32), (full, BF16),
            ((count, hidden), BF16), ((count, hidden), F32), (full, BF16),
        ],
        hidden_all, half_sum, other_sum, biases, gains, cols, bias_up, w_down,
        name="cross_feed",
    )
    half_sum = settle(partial_sum, net.hop(partial_sum, lo))
    other_sum = net.hop(half_sum, hi)

    def turn(
        normed_ref, a_ref, b_ref, bias_ref, gain_ref, grad_ref, down_ref, slope_ref, cols_ref,
        result_ref, normal_ref, second_ref, ffn_ref, before_ref, part_ref,
    ):
        second = normed_ref[...] + (a_ref[...].astype(F32) + b_ref[...].astype(F32)) + bias_ref[4:5, :]
        normal, inverse = normalize(second)
        gain = gain_ref[1:2, :]
        result_ref[...] = normal * gain + bias_ref[5:6, :]
        normal_ref[...] = normal
        grad_second = normalize_back(grad_ref[...] * gain, normal, inverse)
        second_ref[...] = grad_second
        ffn = grad_second.astype(BF16)
        ffn_ref[...] = ffn
        before = (dot_nt(ffn, down_ref[...]) * slope_ref[...]).astype(BF16)
        before_ref[...] = before
        part_ref[...] = dot_nt(before, cols_ref[:, :hidden]).astype(BF16)

    result, normal2, grad_second, grad_ffn, grad_before, partial_sum = fused(
        turn,
        [
            (full, F32), (full, F32), (full, F32), (full, BF16),
            ((count, hidden), BF16), (full, BF16),
        ],
        normed, half_sum, other_sum, biases, gains, grad_all, w_down, slope, cols,
        name="cross_turn",
    )
    half_sum = settle(partial_sum, net.hop(partial_sum, lo))
    other_sum = net.hop(half_sum, hi)

    def attend_back(
        second_ref, a_ref, b_ref, normal_ref, inverse_ref, gain_ref, out_w_ref, chance_ref,
        q_ref, have_ref, late_ref,
        normed_ref, mixed_ref, attn_ref, grad_q_ref, keep_ref, send_ref,
    ):
        grad_normed = second_ref[...] + (a_ref[...].astype(F32) + b_ref[...].astype(F32))
        normed_ref[...] = grad_normed
        grad_mixed = normalize_back(
            grad_normed * gain_ref[0:1, :], normal_ref[...], inverse_ref[...]
        )
        mixed_ref[...] = grad_mixed
        attn = grad_mixed.astype(BF16)
        attn_ref[...] = attn
        grad = dot_nt(attn, out_w_ref[...]).astype(BF16)
        grads = stack_heads(jnp.concatenate([jnp.zeros_like(grad), grad], 1), heads, part)
        q = q_ref[...]
        spread = stack_heads(jnp.concatenate([q, jnp.zeros_like(q)], 1), heads, 0)
        kv = jnp.concatenate([have_ref[...], late_ref[...]], 0)
        chance = chance_ref[...]
        slopes = dot_nt(grads, kv)
        slopes = slopes - jnp.sum(slopes * chance, axis=1, keepdims=True)
        tilt = (chance * slopes).astype(BF16)
        grad_q = merge_heads(dot(tilt, kv), heads, 0)[:, :part] * SCALE
        grad_q_ref[...] = grad_q.astype(BF16)
        grad_kv = dot_tn(tilt, spread) * SCALE + dot_tn(chance.astype(BF16), grads)
        keep_ref[...] = grad_kv[: seen // 2]
        send_ref[...] = grad_kv[seen // 2 :]

    grad_normed, grad_mixed, grad_attn, grad_q, keep, send = fused(
        attend_back,
        [
            (full, F32), (full, F32), (full, BF16), (flat, BF16),
            ((seen // 2, 2 * part), F32), ((seen // 2, 2 * part), F32),
        ],
        grad_second, half_sum, other_sum, normal1, inverse1, gains, w_out, chance,
        queries, have, late,
        name="cross_attend_back",
    )
    other = net.hop(send, 0)
    for b in up[::-1]:
        size = keep.shape[0] // 2
        total = keep + other
        keep, other = total[:size], net.hop(total[size:], b)

    def project_back(grad_q_ref, keep_ref, other_ref, cols_ref, grad_ref, back_ref):
        grad_kv = (keep_ref[...] + other_ref[...]).astype(BF16)
        grad_q = grad_q_ref[...]
        grad_ref[...] = jnp.concatenate([grad_kv, grad_q], 1)
        back = dot_nt(grad_kv, cols_ref[:, hidden : hidden + 2 * part]) + dot_nt(
            grad_q, cols_ref[:, hidden + 2 * part : hidden + 3 * part]
        )
        back_ref[...] = back.astype(BF16)

    grad_kvq, back = fused(
        project_back,
        [((count, 3 * part), BF16), (full, BF16)],
        grad_q, keep, other, cols,
        name="cross_project_back",
    )
    half_sum = settle(back, net.hop(back, lo))
    grad_in = grad_mixed + settle(half_sum, net.hop(half_sum, hi), F32)
    mine = lambda values: lax.dynamic_slice_in_dim(values, member * own, own, 0)

    def weight_grads(
        low_ref, grad_ref, normed_ref, before_ref, context_ref, attn_ref, active_ref, ffn_ref,
        in_ref, onehot_ref, up_ref, rest_ref, out_ref, down_ref,
    ):
        up_ref[...] = dot_tn(normed_ref[...], before_ref[...]).astype(BF16)
        table = dot_tn(in_ref[...].astype(BF16), onehot_ref[...])
        rest_ref[...] = jnp.concatenate(
            [
                dot_tn(low_ref[...], grad_ref[...]),
                table,
                jnp.zeros((width, part - table.shape[1]), F32),
            ],
            1,
        ).astype(BF16)
        out_ref[...] = dot_tn(context_ref[...], attn_ref[...]).astype(BF16)
        down_ref[...] = dot_tn(active_ref[...], ffn_ref[...]).astype(BF16)

    grads = fused(
        weight_grads,
        [
            ((width, hidden), BF16),
            ((width, width), BF16),
            (w_out.shape, BF16),
            (w_down.shape, BF16),
        ],
        hidden_low, grad_kvq, normed_low, grad_before, context, grad_attn, active, grad_ffn,
        grad_in, onehot,
        name="cross_weight_grads",
    )

    def small_sums(
        member_ref, grad_ref, attn_ref, normed_ref, ffn_ref, result_grad_ref, normal1_ref,
        normal2_ref, before_ref, out_ref,
    ):
        member = member_ref[0]
        rows = lax.broadcasted_iota(jnp.int32, full, 0) // own == member
        ours = lambda values: jnp.sum(jnp.where(rows, values, 0.0), axis=0, keepdims=True)
        every = lambda values: jnp.sum(values.astype(F32), axis=0, keepdims=True)

        def spread(values):
            return jnp.concatenate([jnp.where(member == j, values, 0.0) for j in range(TP)], 1)

        sums = every(grad_ref[...])
        grad_normed, grad_result = normed_ref[...], result_grad_ref[...]
        out_ref[...] = jnp.zeros_like(out_ref)
        out_ref[0:1, :] = spread(sums[:, 2 * part :])
        out_ref[1:2, :] = spread(sums[:, part : 2 * part])
        out_ref[2:3, :] = ours(attn_ref[...].astype(F32))
        out_ref[3:4, :] = ours(grad_normed)
        out_ref[4:5, :] = ours(ffn_ref[...].astype(F32))
        out_ref[5:6, :] = ours(grad_result)
        out_ref[6:7, :] = ours(grad_normed * normal1_ref[...])
        out_ref[7:8, :] = ours(grad_result * normal2_ref[...])
        up_sums = every(before_ref[...])
        per = hidden // width
        for j in range(TP):
            for k in range(per):
                at = 8 + j * per + k
                out_ref[at : at + 1, :] = jnp.where(
                    member == j, up_sums[:, k * width : (k + 1) * width], 0.0
                )

    lines = 8 + hidden * TP // width
    small = pl.pallas_call(
        small_sums,
        out_shape=jax.ShapeDtypeStruct((lines, width), F32),
        in_specs=[pl.BlockSpec(memory_space=pltpu.SMEM)]
        + [pl.BlockSpec(memory_space=pltpu.VMEM)] * 8,
        name="cross_small_sums",
    )(member.reshape(1), grad_kvq, grad_attn, grad_normed, grad_ffn, grad_all, normal1, normal2,
      grad_before)
    return mine(result), mine(grad_in), grads, small


def places_of(ids, slots, seq_ids, table_rows):
    all_slots = jnp.arange(seq_ids.shape[0], dtype=jnp.int32)
    earlier = (seq_ids[None, :] == ids[:, None]) & (all_slots[None, :] < slots[:, None])
    places = jnp.sum(earlier.astype(jnp.int32), axis=1)
    rows = jnp.arange(table_rows, dtype=jnp.int32)
    return (places[:, None] == rows[None, :]).astype(BF16)


def shards(
    count, tokens, seq_ids, w_qkv, w_out, w_up, w_down, biases, up_bias, norm_gains, pos_table, cotangent
):
    net = Net(count)
    rows_here, width = tokens.shape
    segs_here = rows_here // SEG
    share, hidden = biases.shape[2], up_bias.shape[1]
    half = width // 2
    lo, hi = net.bits - 2, net.bits - 1
    planes = count // TP

    order = list(range(1, net.bits - 2)) + [0]
    masks = [0]
    for b in order:
        masks = masks + [m | 1 << b for m in masks]
    slots = jnp.arange(seq_ids.shape[0], dtype=jnp.int32).reshape(TP, planes, segs_here)
    key_slots = jnp.take(slots, (net.me & (planes - 1)) ^ jnp.array(masks, jnp.int32), axis=1)
    row_slots = key_slots[:, 0].reshape(-1)
    key_ids = seq_ids[key_slots.transpose(1, 0, 2).reshape(-1)]
    row_ids = seq_ids[row_slots]
    allowed = (row_ids[:, None] == key_ids[None, :]).astype(F32)
    onehot = places_of(row_ids, row_slots, seq_ids, pos_table.shape[0])

    grad_rows = cotangent.reshape(segs_here, SEG, width)
    table = pos_table.T
    small = jnp.concatenate(
        [v.reshape(-1, share) for v in (biases, norm_gains, up_bias)], 0
    )
    if share % 8:
        first_packed = packed = None
    else:
        first_packed = jnp.concatenate(
            [stack_columns(width, w_qkv[0]), pack_small(table, small)], 0
        )
        packed = jnp.concatenate([stack_columns(width, w_out[0], w_up[0]), w_down[0]], 0)
    cross_shares = (w_qkv[1], w_out[1], w_up[1], w_down[1])

    get_qkv = Task(gather_first(net, w_qkv[0], table, small, first_packed))
    packed, *cross_shares = window([packed, *cross_shares], [get_qkv]) if packed is not None else (
        packed, *cross_shares
    )
    get_rest = Task(gather_rest(net, w_out[0], w_up[0], w_down[0], packed))
    cross_shares = window([*cross_shares], [get_qkv])
    window([], [get_rest])
    cross_shares = window([*cross_shares], [get_qkv])
    get_cross = Task(cross_weight_steps(net, *cross_shares))
    (tokens,) = window([tokens], [get_qkv])
    *weights_qkv, table, small = get_qkv.get()
    small = small.astype(F32)
    narrow = small[:, :16].transpose(1, 0, 2).reshape(16, width)
    long = small[:, 16:].reshape(count, 2, -1).transpose(1, 0, 2).reshape(2, 1, -1)
    biases0, gains0, up_bias0 = narrow[:6], narrow[12:14], long[0, 0]
    params1 = narrow[6:12], narrow[14:], long[1]

    qkv, context = [], None
    for n, weight in enumerate(weights_qkv):
        shift = jnp.concatenate(
            [
                biases0[0, n * half : (n + 1) * half],
                jnp.zeros((half,), F32),
                biases0[1, n * half : (n + 1) * half],
            ]
        )
        qkv.append((dot(tokens, weight) + shift).astype(BF16))
        context = segment_attend(qkv[n], n, context)
        context, tokens = window([context, tokens], [get_rest, get_cross])
    (context,) = window([context], [get_rest, get_cross])
    w_out0, w_up0, w_down0 = get_rest.get()

    mixed = tokens.astype(F32) + dot(context, w_out0) + biases0[2]
    normal1, inverse1 = normalize(mixed)
    normed = normal1 * gains0[0] + biases0[3]
    normed_low = normed.astype(BF16)
    active, slope = gelu_pair(dot(normed_low, w_up0) + up_bias0)
    active, slope = active.astype(BF16), slope.astype(BF16)
    active, slope = window([active, slope], [get_cross])
    second = normed + dot(active, w_down0) + biases0[4]
    normal2, inverse2 = normalize(second)
    blocked = (normal2 * gains0[1] + biases0[5]).reshape(segs_here, SEG, width)

    firsts = blocked[:, 0, :]
    own_onehot = lax.dynamic_slice_in_dim(onehot, (net.me >> lo) * segs_here, segs_here, 0)
    cross_in = firsts + dot_nt(own_onehot, table)
    result1, grad_cross, grads1, small1 = cross_encoder(
        net,
        cross_in,
        grad_rows[:, 0, :].astype(F32),
        get_cross.get(),
        params1,
        allowed,
        onehot,
    )
    is_first = lax.broadcasted_iota(jnp.int32, (1, SEG, 1), 1) == 0
    layer_out = jnp.where(is_first, result1[:, None, :], blocked)
    layer_out = layer_out.reshape(rows_here, width).astype(BF16)

    ways, back_ways = link_orders(net)
    grad = jnp.where(is_first, grad_cross[:, None, :], grad_rows.astype(F32))
    grad = grad.reshape(rows_here, width)
    red_cross = Task(cross_grad_steps(net, *grads1, ways))
    grad_second = normalize_back(grad * gains0[1], normal2, inverse2)
    grad_ffn = grad_second.astype(BF16)
    grad_down = dot_tn(active, grad_ffn).astype(BF16)
    grad_down, grad_ffn = window([grad_down, grad_ffn], [red_cross])
    red_down = Task(reduce_steps(net, [grad_down], back_ways + [lo, hi]))
    grad_before = (dot_nt(grad_ffn, w_down0) * slope.astype(F32)).astype(BF16)
    (grad_before,) = window([grad_before], [red_down])
    grad_up = dot_tn(normed_low, grad_before).astype(BF16)
    grad_up, grad_before = window([grad_up, grad_before], [])
    red_up = Task(reduce_steps(net, [grad_up], ways + [lo, hi]))
    grad_normed = grad_second + dot_nt(grad_before, w_up0)
    (grad_normed,) = window([grad_normed], [red_cross, red_up])
    grad_mixed = normalize_back(grad_normed * gains0[0], normal1, inverse1)
    grad_attn = grad_mixed.astype(BF16)
    grad_context = dot_nt(grad_attn, w_out0).astype(BF16)
    grad_out = dot_tn(context, grad_attn).astype(BF16)
    grad_context, grad_out = window([grad_context, grad_out], [])
    back_left, sums_left = segment_attend_back(qkv[0], grad_context, 0)
    back_left, grad_context = window([back_left, grad_context], [red_down, red_cross])
    grad_left = dot_tn(tokens, back_left).astype(BF16)
    grad_left, grad_context, grad_out = window([grad_left, grad_context, grad_out], [])
    red_left = Task(reduce_steps(net, [grad_left, grad_out], ways + [lo, hi]))
    back_right, sums_right = segment_attend_back(qkv[1], grad_context, 1)
    (back_right,) = window([back_right], [red_up, red_left, red_cross])
    grad_right = dot_tn(tokens, back_right).astype(BF16)
    grad_right, back_right = window([grad_right, back_right], [])
    red_right = Task(reduce_steps(net, [grad_right], back_ways + [lo, hi]))
    grad_tokens = grad_mixed + dot_nt(back_left, weights_qkv[0]) + dot_nt(back_right, weights_qkv[1])
    (grad_tokens, sums_left, sums_right) = window(
        [grad_tokens.astype(BF16), sums_left, sums_right], [red_down, red_right, red_cross]
    )

    sums = [jnp.sum(v, axis=(0, 1)).reshape(3, half) for v in (sums_left, sums_right)]
    small0 = jnp.concatenate(
        [
            jnp.stack(
                [
                    jnp.concatenate([v[0] for v in sums]),
                    jnp.concatenate([v[2] for v in sums]),
                    column_sums(grad_attn),
                    column_sums(grad_normed),
                    column_sums(grad_ffn),
                    column_sums(grad),
                    column_sums(grad_normed * normal1),
                    column_sums(grad * normal2),
                ]
            ),
            column_sums(grad_before).reshape(-1, width),
        ]
    )
    red_small = Task(total_steps(net, jnp.stack([small0, small1])))
    window([], [red_up, red_left, red_small])
    window([], [red_down, red_right, red_small])
    window([], [red_up, red_left, red_small])
    window([], [red_down, red_right, red_small])
    window([], [red_up, red_left, red_small])
    window([], [red_right])
    for _ in range(net.bits):
        window([], [red_down, red_up, red_left, red_right, red_small])

    small = red_small.get()
    narrow = lax.dynamic_slice_in_dim(small[:, :8], net.me * share, share, 2)
    long = lax.dynamic_slice_in_dim(small[:, 8:].reshape(2, -1), net.me * hidden, hidden, 1)
    (grad_down0,) = red_down.get()
    (grad_up0,) = red_up.get()
    grad_left0, grad_out0 = red_left.get()
    halves = [r.reshape(-1, 3, half) for r in (grad_left0, red_right.get()[0])]
    grad_qkv0 = jnp.stack(halves, 2).reshape(share, -1)
    shares1 = red_cross.get()
    return (
        layer_out,
        grad_tokens,
        jnp.stack([grad_qkv0, shares1[0]]),
        jnp.stack([grad_out0, shares1[1]]),
        jnp.stack([grad_up0, shares1[2]]),
        jnp.stack([grad_down0, shares1[3]]),
        narrow[:, :6],
        long,
        narrow[:, 6:],
        shares1[4][:, : pos_table.shape[0]].T,
    )


def solution(mesh):
    count = mesh.shape["ctx"] * mesh.shape["wa"]
    in_specs = (
        P(AXES, None),
        P(),
        P(None, AXES, None),
        P(None, AXES, None),
        P(None, AXES, None),
        P(None, AXES, None),
        P(None, None, AXES),
        P(None, AXES),
        P(None, None, AXES),
        P(None, AXES),
        P(AXES, None),
    )
    out_specs = (
        P(AXES, None),
        P(AXES, None),
        P(None, AXES, None),
        P(None, AXES, None),
        P(None, AXES, None),
        P(None, AXES, None),
        P(None, None, AXES),
        P(None, AXES),
        P(None, None, AXES),
        P(None, AXES),
    )
    return jax.shard_map(
        partial(shards, count), mesh=mesh, in_specs=in_specs, out_specs=out_specs, check_vma=False
    )
```

```python
from functools import partial

import jax
import jax.numpy as jnp
from jax import lax
from jax.experimental import pallas as pl
from jax.experimental.pallas import tpu as pltpu
from jax.sharding import PartitionSpec as P

HDIM = 64
SEG = 128
TP = 4
AXES = ("ctx", "wa")
F32 = jnp.float32
BF16 = jnp.bfloat16
SCALE = HDIM ** (-0.5)


def work(microseconds):
    return pl.CostEstimate(flops=microseconds * 10**9, transcendentals=0, bytes_accessed=0)


def dot(a, b, dims=((1,), (0,))):
    return lax.dot_general(a, b, (dims, ((), ())), preferred_element_type=F32)


def normalize(values):
    center = values - jnp.mean(values, axis=-1, keepdims=True)
    spread = jnp.mean(center * center, axis=-1, keepdims=True)
    inverse = lax.rsqrt(spread + 1e-05)
    return center * inverse, inverse


def normalize_back(grad, normal, inverse):
    return inverse * (
        grad
        - jnp.mean(grad, axis=-1, keepdims=True)
        - normal * jnp.mean(grad * normal, axis=-1, keepdims=True)
    )


def gelu_pair(values):
    phi = 0.5 * (1.0 + lax.erf(values * 0.7071067811865476))
    density = jnp.exp(-0.5 * values * values) * 0.3989422804014327
    return values * phi, phi + values * density


class Net:
    def __init__(self, count):
        self.count = count
        self.bits = count.bit_length() - 1
        self.me = lax.axis_index(AXES)

    def bit(self, b):
        return (self.me >> b) & 1

    def hop(self, value, b):
        return lax.ppermute(value, AXES, [(i, i ^ (1 << b)) for i in range(self.count)])

    def grow(self, value, b, axis):
        other = self.hop(value, b)
        return jnp.where(
            self.bit(b) == 0,
            jnp.concatenate([value, other], axis),
            jnp.concatenate([other, value], axis),
        )

    def pick(self, value, which, axis):
        return lax.dynamic_slice_in_dim(value, which, 1, axis)


def tie(*values):
    return lax.optimization_barrier(values)


def place_blocks(net, parts, blocks, shapes):
    arrays = [part[0] for part in parts]

    def body(me_ref, *refs):
        sources = refs[: len(parts)]
        targets = refs[len(parts) : len(parts) + len(shapes)]
        sem = refs[-1]
        me = me_ref[0]
        for source, (array, masks, half) in zip(sources, parts):
            for j, mask in enumerate(masks):
                for row, rows, lane, lanes, which, to_row, to_lane in blocks(half):
                    which, lead = which if isinstance(which, tuple) else (which, ())
                    to = lead + (me ^ mask, pl.ds(to_row, rows), pl.ds(to_lane, lanes))
                    pltpu.make_async_copy(
                        source.at[j, pl.ds(row, rows), pl.ds(lane, lanes)], targets[which].at[to], sem
                    ).start()
        for target in targets:
            pltpu.make_async_copy(target, target, sem).wait()

    return pl.pallas_call(
        body,
        out_shape=[jax.ShapeDtypeStruct(shape, BF16) for shape in shapes],
        in_specs=[pl.BlockSpec(memory_space=pltpu.SMEM)]
        + [pl.BlockSpec(memory_space=pl.ANY)] * len(parts),
        out_specs=[pl.BlockSpec(memory_space=pltpu.VMEM)] * len(shapes),
        scratch_shapes=[pltpu.SemaphoreType.DMA],
        name="place_blocks",
        compiler_params=pltpu.CompilerParams(vmem_limit_bytes=16 << 20),
        cost_estimate=work(5),
    )(net.me.reshape(1), *arrays)


def link_orders(net):
    mid = list(range(1, net.bits - 2))
    return mid, mid[::-1]


class Task:
    def __init__(self, steps):
        self.steps, self.flight, self.result = steps, None, None
        self.advance(None)

    def advance(self, arrived):
        try:
            self.flight = list(self.steps.send(arrived))
        except StopIteration as stop:
            self.flight, self.result = [], stop.value

    def get(self):
        while self.flight:
            self.advance(self.flight)
        return self.result


def window(values, tasks):
    done = tie(*values, *[f for task in tasks for f in task.flight])
    at = len(values)
    for task in tasks:
        size = len(task.flight)
        if size:
            task.advance(list(done[at : at + size]))
        at += size
    return done[: len(values)]


def gather_steps(net, have, high, early=False):
    have, masks = have[None], [0]
    for b in high:
        (other,) = yield [net.hop(have, b)]
        have = jnp.concatenate([have, other], 0)
        masks = masks + [m ^ (1 << b) for m in masks]
    cut = have.shape[2] // 2
    halves = [have[:, :, :cut], have[:, :, cut:]]
    orders = link_orders(net)
    lists = [masks, masks]
    for step in range(len(orders[0]) - 1):
        others = yield [net.hop(h, o[step]) for h, o in zip(halves, orders)]
        halves = [jnp.concatenate([h, o], 0) for h, o in zip(halves, others)]
        lists = [l + [m ^ (1 << o[step]) for m in l] for l, o in zip(lists, orders)]
    last = [o[-1] for o in orders]
    if early:
        arrived = yield [net.hop(h, b) for h, b in zip(halves, last)] + [
            net.hop(h, 0) for h in halves
        ]
        late, early_core = arrived[:2], arrived[2:]
        late_core = yield [net.hop(h, 0) for h in late]
    else:
        late = yield [net.hop(h, b) for h, b in zip(halves, last)]
        arrived = yield [net.hop(h, 0) for h in halves + late]
        early_core, late_core = arrived[:2], arrived[2:]
    core = [c for pair in zip(early_core, late_core) for c in pair]
    parts = []
    for n in (0, 1):
        late_list = [m ^ (1 << last[n]) for m in lists[n]]
        parts.append((halves[n], lists[n], n))
        parts.append((core[2 * n], [m ^ 1 for m in lists[n]], n))
        parts.append((late[n], late_list, n))
        parts.append((core[2 * n + 1], [m ^ 1 for m in late_list], n))
    return parts


def stack_columns(width, *shares):
    pieces = []
    for share in shares:
        for at in range(0, share.shape[1], width):
            pieces.append(share[:, at : at + width])
    return jnp.concatenate(pieces, 0)


def flat_rows(out):
    return out.reshape(-1, out.shape[2])


def pack_first(w_qkv, table, biases, gains, up_bias):
    rows, width = w_qkv.shape[1], w_qkv.shape[2] // 3
    share = biases.shape[2]
    groups = up_bias.shape[1] // share

    def body(qkv_ref, table_ref, bias_ref, gain_ref, up_ref, out_ref):
        for i in range(3):
            out_ref[i * rows : (i + 1) * rows, :] = qkv_ref[0, :, i * width : (i + 1) * width]
        up = up_ref[...].astype(F32)
        small = jnp.concatenate(
            [bias_ref[e].astype(F32) for e in (0, 1)]
            + [gain_ref[e].astype(F32) for e in (0, 1)]
            + [up[e : e + 1, k * share : (k + 1) * share] for e in (0, 1) for k in range(groups)],
            0,
        )
        small = jnp.concatenate([small, jnp.zeros((24, 128 - share), F32)], 1)
        table = table_ref[...].astype(F32)
        out_ref[3 * rows :, :] = jnp.concatenate(
            [v[i : i + 8] for v in (table, small) for i in (0, 8, 16)], 1
        ).astype(BF16)

    return pl.pallas_call(
        body, out_shape=jax.ShapeDtypeStruct((3 * rows + 8, width), BF16), name="pack_first",
        cost_estimate=work(2),
    )(w_qkv, table, biases, gains, up_bias)


def gather_first(net, w_qkv, table, small, packed):
    rows, width = w_qkv.shape[0], w_qkv.shape[1] // 3
    half = width // 2
    if packed is None:
        cube = lax.all_gather(w_qkv, AXES, axis=0, tiled=True).reshape(width, 3, 2, half)
        return (
            cube[:, :, 0].reshape(width, -1),
            cube[:, :, 1].reshape(width, -1),
            lax.all_gather(table, AXES, axis=0, tiled=True),
            lax.all_gather(small, AXES, axis=0),
        )
    parts = yield from gather_steps(net, packed, (net.bits - 1, net.bits - 2), True)
    left, right, table, small = place_blocks(
        net,
        parts,
        lambda h: [(i * rows, rows, 0, half, h, 0, i * half) for i in range(3)]
        + [(3 * rows, 8, i * 128, 128, 2 + h, i * 8, 0) for i in range(3)],
        [(net.count, rows, 3 * half)] * 2 + [(net.count, 24, 128)] * 2,
    )
    return flat_rows(left), flat_rows(right), flat_rows(table), small[:, :, :rows]


def gather_middle(net, w_out, w_up, packed):
    rows, width = w_out.shape
    if packed is None:
        return [lax.all_gather(w, AXES, axis=0, tiled=True) for w in (w_out, w_up)]
    parts = yield from gather_steps(net, packed, (net.bits - 1, net.bits - 2))
    columns = w_up.shape[1] // width
    half = width // 2
    out, up = place_blocks(
        net,
        parts,
        lambda h: [(0, rows, 0, half, 0, 0, h * half)]
        + [((i + 1) * rows, rows, 0, half, 1, 0, i * width + h * half) for i in range(columns)],
        [(net.count,) + w.shape for w in (w_out, w_up)],
    )
    return flat_rows(out), flat_rows(up)


def gather_down(net, w_down):
    rows, width = w_down.shape
    if rows % 32:
        return lax.all_gather(w_down, AXES, axis=0, tiled=True)
    parts = yield from gather_steps(net, w_down, (net.bits - 1, net.bits - 2))
    half = width // 2
    (down,) = place_blocks(
        net, parts, lambda h: [(0, rows, 0, half, 0, 0, h * half)], [(net.count, rows, width)]
    )
    return flat_rows(down)


def settle(keep, other, dtype=BF16):
    return (keep.astype(F32) + other.astype(F32)).astype(dtype)


def reduce_steps(net, grads, order):
    axis = lambda b: net.bits - 1 - b
    cubes = [g.reshape((2,) * net.bits + (g.shape[0] // net.count, g.shape[1])) for g in grads]
    widths = [g.shape[1] for g in grads]
    join = lambda values: jnp.concatenate(values, -1) if len(values) > 1 else values[0]
    arrived = yield [net.hop(net.pick(c, 1 - net.bit(0), axis(0)), 0) for c in cubes]
    pairs = [(net.pick(c, net.bit(0), axis(0)), f) for c, f in zip(cubes, arrived)]
    for b in order:
        if isinstance(b, tuple):
            if len(pairs) != 2:
                keep, other = join([k for k, _ in pairs]), join([f for _, f in pairs])
                cut = keep.shape[-1] // 256 * 128
                pairs = [(keep[..., :cut], other[..., :cut]), (keep[..., cut:], other[..., cut:])]
            sides = lambda turn: [
                settle(net.pick(k, t, axis(x)), net.pick(f, t, axis(x)))
                for (k, f), x in zip(pairs, b)
                for t in [net.bit(x) ^ turn]
            ]
            sent, kept = sides(1), sides(0)
            arrived = yield [net.hop(v, x) for v, x in zip(sent, b)]
            pairs = list(zip(kept, arrived))
            continue
        side = lambda which: join(
            [settle(net.pick(k, which, axis(b)), net.pick(f, which, axis(b))) for k, f in pairs]
        )
        sent, kept = side(1 - net.bit(b)), side(net.bit(b))
        (other,) = yield [net.hop(sent, b)]
        pairs = [(kept, other)]
    whole = settle(*pairs[0], F32)
    whole = whole.reshape(whole.shape[-2:])
    out, at = [], 0
    for w in widths:
        out.append(whole[:, at : at + w])
        at += w
    return out


def total_steps(net, value):
    for b in [0] + list(range(1, net.bits)):
        (other,) = yield [net.hop(value, b)]
        value = value + other
    return value


def ordered(net, value, other, b, axis):
    return jnp.where(
        net.bit(b) == 0,
        jnp.concatenate([value, other], axis),
        jnp.concatenate([other, value], axis),
    )


def trade_pair(net, value, b, axis):
    return net.hop(net.pick(value, 1 - net.bit(b), axis), b), net.pick(value, net.bit(b), axis)


def dot_nt(a, b):
    return dot(a, b, ((1,), (1,)))


def dot_tn(a, b):
    return dot(a, b, ((0,), (0,)))


def pick_lanes(mask, values):
    return jnp.where(mask, values, jnp.zeros_like(values))


def head_masks(rows):
    lane = lax.broadcasted_iota(jnp.int32, (rows, 2 * HDIM), 1)
    return lane < HDIM, lane >= HDIM


def chance_of(keys, queries):
    scores = dot_nt(keys, queries) * SCALE
    raised = jnp.exp(scores - jnp.max(scores, axis=0, keepdims=True))
    return raised * (1.0 / jnp.sum(raised, axis=0, keepdims=True))


def attend_forward_body(heads, qkv_ref, out_ref):
    width = heads * HDIM
    for at in range(0, width, 2 * HDIM):
        queries, keys, values = [qkv_ref[:, n * width + at : n * width + at + 128] for n in range(3)]
        total = 0.0
        for mask in head_masks(SEG):
            chance = chance_of(pick_lanes(mask, keys), queries).astype(BF16)
            total = total + dot_tn(pick_lanes(mask, values), chance)
        out_ref[:, at : at + 128] = total.T.astype(BF16)


def attend_backward_body(heads, qkv_ref, grad_ref, out_ref, sums_ref):
    width = heads * HDIM
    for at in range(0, width, 2 * HDIM):
        queries, keys, values = [qkv_ref[:, n * width + at : n * width + at + 128] for n in range(3)]
        grad = grad_ref[:, at : at + 128]
        totals = [0.0, 0.0, 0.0]
        for mask in head_masks(SEG):
            own_keys = pick_lanes(mask, keys)
            chance = chance_of(own_keys, queries)
            slope = dot_nt(pick_lanes(mask, values), grad)
            slope = slope - jnp.sum(slope * chance, axis=0, keepdims=True)
            tilt = (chance * slope).astype(BF16)
            totals[0] = totals[0] + dot_tn(tilt, own_keys)
            totals[1] = totals[1] + dot(tilt, pick_lanes(mask, queries))
            totals[2] = totals[2] + dot(chance.astype(BF16), pick_lanes(mask, grad))
        for n, (total, scale) in enumerate(zip(totals, (SCALE, SCALE, 1.0))):
            low = (total * scale).astype(BF16)
            out_ref[:, n * width + at : n * width + at + 128] = low
            sums_ref[0, :, n * width + at : n * width + at + 128] = jnp.sum(
                low.astype(F32), axis=0, keepdims=True
            )


def segment_attend(qkv, half, context=None):
    rows, width = qkv.shape[0], qkv.shape[1] // 3

    def body(*refs):
        attend_forward_body(width // HDIM, refs[0], refs[-1])

    return pl.pallas_call(
        body,
        out_shape=jax.ShapeDtypeStruct((rows, 2 * width), BF16),
        grid=(rows // SEG,),
        in_specs=[pl.BlockSpec((SEG, 3 * width), lambda i: (i, 0))]
        + [pl.BlockSpec(memory_space=pl.ANY)] * half,
        out_specs=pl.BlockSpec((SEG, width), lambda i: (i, half)),
        input_output_aliases={1: 0} if half else {},
        name="segment_attend",
        compiler_params=pltpu.CompilerParams(vmem_limit_bytes=12 << 20),
        cost_estimate=work(10),
    )(*([qkv, context] if half else [qkv]))


def segment_attend_back(qkv, grad, half):
    rows, width = qkv.shape[0], qkv.shape[1] // 3
    return pl.pallas_call(
        partial(attend_backward_body, width // HDIM),
        out_shape=(
            jax.ShapeDtypeStruct((rows, 3 * width), BF16),
            jax.ShapeDtypeStruct((rows // SEG, 1, 3 * width), F32),
        ),
        grid=(rows // SEG,),
        in_specs=[
            pl.BlockSpec((SEG, 3 * width), lambda i: (i, 0)),
            pl.BlockSpec((SEG, width), lambda i: (i, half)),
        ],
        out_specs=(
            pl.BlockSpec((SEG, 3 * width), lambda i: (i, 0)),
            pl.BlockSpec((1, 1, 3 * width), lambda i: (i, 0, 0)),
        ),
        name="segment_attend_back",
        compiler_params=pltpu.CompilerParams(vmem_limit_bytes=16 << 20),
        cost_estimate=work(12),
    )(qkv, grad)


BLOCK = 256


def row_block(width):
    return pl.BlockSpec((BLOCK, width), lambda i: (i, 0))


def whole(shape):
    return pl.BlockSpec(
        shape, lambda i: (0,) * len(shape), pipeline_mode=pl.Buffered(1)
    )


def feed_up(tokens, context, w_out, w_up, biases, gains, up_bias):
    rows, width = tokens.shape
    hidden = w_up.shape[1]

    def body(
        tokens_ref, context_ref, out_ref, up_ref, bias_ref, gain_ref, up_bias_ref,
        normed_ref, normal_ref, inverse_ref, low_ref, active_ref, slope_ref,
    ):
        mixed = tokens_ref[...].astype(F32) + dot(context_ref[...], out_ref[...]) + bias_ref[2:3, :]
        normal, inverse = normalize(mixed)
        normal_ref[...] = normal.astype(BF16)
        inverse_ref[...] = inverse
        normed = normal * gain_ref[0:1, :] + bias_ref[3:4, :]
        normed_ref[...] = normed
        low = normed.astype(BF16)
        low_ref[...] = low
        for at in range(0, hidden, width):
            part = slice(at, at + width)
            active, slope = gelu_pair(dot(low, up_ref[:, part]) + up_bias_ref[:, part])
            active_ref[:, part] = active.astype(BF16)
            slope_ref[:, part] = slope.astype(BF16)

    outs = [(width, F32), (width, BF16), (1, F32), (width, BF16), (hidden, BF16), (hidden, BF16)]
    return pl.pallas_call(
        body,
        grid=(rows // BLOCK,),
        out_shape=[jax.ShapeDtypeStruct((rows, w), t) for w, t in outs],
        in_specs=[row_block(width)] * 2
        + [whole(v.shape) for v in (w_out, w_up, biases, gains, up_bias)],
        out_specs=[row_block(w) for w, _ in outs],
        name="feed_up",
        compiler_params=pltpu.CompilerParams(vmem_limit_bytes=36 << 20),
        cost_estimate=work(18),
    )(tokens, context, w_out, w_up, biases, gains, up_bias)


def feed_down(normed, active, w_down, biases, gains):
    rows, width = normed.shape
    per = BLOCK // SEG

    def body(
        normed_ref, active_ref, down_ref, bias_ref, gain_ref,
        result_ref, first_ref, normal_ref, inverse_ref,
    ):
        second = normed_ref[...] + dot(active_ref[...], down_ref[...]) + bias_ref[4:5, :]
        normal, inverse = normalize(second)
        normal_ref[...] = normal.astype(BF16)
        inverse_ref[...] = inverse
        result = normal * gain_ref[1:2, :] + bias_ref[5:6, :]
        result_ref[...] = result.astype(BF16)
        for k in range(per):
            first_ref[0, k : k + 1, :] = result[k * SEG : k * SEG + 1]

    return pl.pallas_call(
        body,
        grid=(rows // BLOCK,),
        out_shape=[
            jax.ShapeDtypeStruct((rows, width), BF16),
            jax.ShapeDtypeStruct((rows // BLOCK, per, width), F32),
            jax.ShapeDtypeStruct((rows, width), BF16),
            jax.ShapeDtypeStruct((rows, 1), F32),
        ],
        in_specs=[row_block(width), row_block(active.shape[1])]
        + [whole(v.shape) for v in (w_down, biases, gains)],
        out_specs=[
            row_block(width), pl.BlockSpec((1, per, width), lambda i: (i, 0, 0)), row_block(width),
            row_block(1),
        ],
        name="feed_down",
        compiler_params=pltpu.CompilerParams(vmem_limit_bytes=28 << 20),
        cost_estimate=work(11),
    )(normed, active, w_down, biases, gains)


def tail_backward(cotangent, firsts, kept, w_out, w_up, w_down, gains):
    normal1, inverse1, slope, normal2, inverse2 = kept
    rows, width = cotangent.shape
    hidden = w_up.shape[1]
    per = BLOCK // SEG
    lines = 8 + hidden // width

    def body(
        cotangent_ref, first_ref, normal1_ref, inverse1_ref, slope_ref, normal2_ref, inverse2_ref,
        out_ref, up_ref, down_ref, gain_ref,
        ffn_ref, before_ref, mixed_ref, attn_ref, context_ref, sums_ref,
    ):
        grad = cotangent_ref[...].astype(F32)
        row = lax.broadcasted_iota(jnp.int32, (BLOCK, 1), 0)
        for k in range(per):
            grad = jnp.where(row == k * SEG, first_ref[0, k : k + 1, :], grad)
        normal2 = normal2_ref[...].astype(F32)
        grad_second = normalize_back(grad * gain_ref[1:2, :], normal2, inverse2_ref[...])
        ffn = grad_second.astype(BF16)
        ffn_ref[...] = ffn
        grad_normed = grad_second
        up_sums = []
        for at in range(0, hidden, width):
            part = slice(at, at + width)
            before = dot_nt(ffn, down_ref[part, :]) * slope_ref[:, part].astype(F32)
            before = before.astype(BF16)
            before_ref[:, part] = before
            up_sums.append(before)
            grad_normed = grad_normed + dot_nt(before, up_ref[:, part])
        normal1 = normal1_ref[...].astype(F32)
        grad_mixed = normalize_back(grad_normed * gain_ref[0:1, :], normal1, inverse1_ref[...])
        mixed_ref[...] = grad_mixed
        attn = grad_mixed.astype(BF16)
        attn_ref[...] = attn
        context_ref[...] = dot_nt(attn, out_ref[...]).astype(BF16)

        @pl.when(pl.program_id(0) == 0)
        def _():
            sums_ref[...] = jnp.zeros_like(sums_ref)

        values = [attn, grad_normed, ffn, grad, grad_normed * normal1, grad * normal2] + up_sums
        for n, value in enumerate(values):
            sums_ref[n + 2 : n + 3, :] += jnp.sum(value.astype(F32), axis=0, keepdims=True)

    return pl.pallas_call(
        body,
        grid=(rows // BLOCK,),
        out_shape=[
            jax.ShapeDtypeStruct((rows, width), BF16),
            jax.ShapeDtypeStruct((rows, hidden), BF16),
            jax.ShapeDtypeStruct((rows, width), F32),
            jax.ShapeDtypeStruct((rows, width), BF16),
            jax.ShapeDtypeStruct((rows, width), BF16),
            jax.ShapeDtypeStruct((lines, width), F32),
        ],
        in_specs=[
            row_block(width),
            pl.BlockSpec((1, per, width), lambda i: (i, 0, 0)),
            row_block(width), row_block(1), row_block(hidden), row_block(width), row_block(1),
        ]
        + [whole(v.shape) for v in (w_out, w_up, w_down, gains)],
        out_specs=[
            row_block(width), row_block(hidden), row_block(width), row_block(width),
            row_block(width), pl.BlockSpec((lines, width), lambda i: (0, 0)),
        ],
        name="tail_backward",
        compiler_params=pltpu.CompilerParams(vmem_limit_bytes=36 << 20),
        cost_estimate=work(24),
    )(
        cotangent, firsts.reshape(-1, per, width), normal1, inverse1, slope, normal2, inverse2,
        w_out, w_up, w_down, gains,
    )


def put_firsts(values, firsts):
    rows, width = values.shape

    def body(old_ref, first_ref, out_ref):
        row = lax.broadcasted_iota(jnp.int32, (16, 1), 0)
        old = old_ref[...].astype(F32)
        out_ref[...] = jnp.where(row == 0, first_ref[0], old).astype(BF16)

    block = pl.BlockSpec((16, width), lambda i: (i * (SEG // 16), 0))
    return pl.pallas_call(
        body,
        grid=(rows // SEG,),
        out_shape=jax.ShapeDtypeStruct(values.shape, BF16),
        in_specs=[block, pl.BlockSpec((1, 1, width), lambda i: (i, 0, 0))],
        out_specs=block,
        input_output_aliases={0: 0},
        name="put_firsts",
        compiler_params=pltpu.CompilerParams(vmem_limit_bytes=4 << 20),
        cost_estimate=work(4),
    )(values, firsts[:, None, :])


def cross_weight_steps(net, w_qkv, w_out, w_up, w_down):
    rows, width = w_out.shape
    hi, lo = net.bits - 1, net.bits - 2
    part = width // TP
    planes = net.count // TP
    cube = w_qkv.reshape(rows, 3, TP, part)
    ups = w_up.reshape(rows, TP, -1)
    hidden = ups.shape[2]
    assert hidden == width
    kvq = jnp.concatenate([cube[:, 1], cube[:, 2], cube[:, 0], jnp.zeros_like(cube[:, 0])], 2)
    cols = jnp.stack([ups, kvq]).transpose(2, 0, 1, 3).reshape(2, 2, 2 * rows, width)
    for b, axis in ((hi, 0), (lo, 1)):
        flight, keep = trade_pair(net, cols, b, axis)
        (other,) = yield [flight]
        cols = ordered(net, keep, other, b, axis)
    have = jnp.concatenate([cols.reshape(-1, width), w_out, w_down], 0)
    if rows % 8:
        value = have[None]
        for b in range(net.bits - 2):
            (other,) = yield [net.hop(value, b)]
            value = ordered(net, value, other, b, 0)
        cols = value[:, : 8 * rows].reshape(planes, TP, 2, rows, width).transpose(1, 0, 3, 2, 4)
        return (
            cols.reshape(width, 2 * width),
            value[:, 8 * rows : 9 * rows].reshape(part, width),
            value[:, 9 * rows :].reshape(hidden, width),
        )
    parts = yield from gather_steps(net, have, ())
    parts = [(array, [m & (planes - 1) for m in masks], h) for array, masks, h in parts]
    half = width // 2
    plane = Net.__new__(Net)
    plane.me = net.me & (planes - 1)
    outs = place_blocks(
        plane,
        parts,
        lambda h: [
            ((2 * t + k) * rows, rows, 0, half, (0, (t,)), 0, k * width + h * half)
            for t in range(TP)
            for k in (0, 1)
        ]
        + [
            (8 * rows, rows, 0, half, 1, 0, h * half),
            (9 * rows, 4 * rows, 0, half, 2, 0, h * half),
        ],
        [(TP, planes, rows, 2 * width), (planes, rows, width), (planes, 4 * rows, width)],
    )
    return outs[0].reshape(width, 2 * width), flat_rows(outs[1]), flat_rows(outs[2])


def cross_grad_steps(net, ups, rest, grad_out, grad_down, order):
    hi, lo = net.bits - 1, net.bits - 2
    plane = net.bits - 2
    planes = net.count // TP
    width = ups.shape[0]
    rows = width // net.count
    part = width // TP
    pair = jnp.stack([ups.reshape(TP, planes, rows, width), rest.reshape(TP, planes, rows, width)])
    whole = jnp.concatenate(
        [
            pair.transpose(2, 1, 0, 3, 4).reshape(planes, 8 * rows, width),
            grad_out.reshape(planes, rows, width),
            grad_down.reshape(planes, 4 * rows, width),
        ],
        1,
    ).reshape((2,) * plane + (13 * rows, width))
    axis = lambda b: plane - 1 - b
    (other,) = yield [net.hop(net.pick(whole, 1 - net.bit(0), axis(0)), 0)]
    kept = net.pick(whole, net.bit(0), axis(0))
    for b in order:
        side = lambda which: settle(net.pick(kept, which, axis(b)), net.pick(other, which, axis(b)))
        sent, kept = side(1 - net.bit(b)), side(net.bit(b))
        (other,) = yield [net.hop(sent, b)]
    whole = settle(kept, other).reshape(13 * rows, width)
    cols = whole[: 8 * rows].reshape(2, 2, 2 * rows, width)
    for b, at in ((hi, 0), (lo, 1)):
        flight, keep = trade_pair(net, cols, b, at)
        (back,) = yield [flight]
        cols = ordered(net, keep, back, b, at)
    whole, cols = yield [whole, cols]
    cols = cols.reshape(TP, 2, rows, width).transpose(1, 2, 0, 3).astype(F32)
    deep = whole[8 * rows :].astype(F32)
    pieces = [cols[1, :, :, n * part : (n + 1) * part].reshape(rows, width) for n in (2, 0, 1)]
    return (
        jnp.concatenate(pieces, 1),
        deep[:rows],
        cols[0].reshape(rows, -1),
        deep[rows:],
        cols[1, :, 0, 3 * part :],
    )


def lanes_between(values, first, last):
    lane = lax.broadcasted_iota(jnp.int32, values.shape, values.ndim - 1)
    return jnp.where((lane >= first) & (lane < last), values, jnp.zeros_like(values))


def stack_heads(values, heads, first):
    return jnp.concatenate(
        [lanes_between(values, first + h * HDIM, first + (h + 1) * HDIM) for h in range(heads)], 0
    )


def merge_heads(values, heads, first):
    rows = values.shape[0] // heads
    return sum(
        lanes_between(values[h * rows : (h + 1) * rows], first + h * HDIM, first + (h + 1) * HDIM)
        for h in range(heads)
    )


def fused(body, outs, *args, name):
    return pl.pallas_call(
        body, out_shape=[jax.ShapeDtypeStruct(shape, dtype) for shape, dtype in outs], name=name,
        compiler_params=pltpu.CompilerParams(vmem_limit_bytes=32 << 20),
        cost_estimate=work(3),
    )(*args)


def cross_encoder(net, cross_in, grad_own, weights, params, allowed, onehot):
    cols, w_out, w_down = weights
    own, width = cross_in.shape
    part, hidden = w_out.shape[0], w_down.shape[0]
    plane = net.bits - 2
    hi, lo = net.bits - 1, net.bits - 2
    member = net.me >> lo
    up = list(range(1, plane))
    heads = part // HDIM
    biases, gains, up_bias = params
    row = lambda n: biases[n : n + 1]
    slab = lambda vector, size: lax.dynamic_slice_in_dim(vector, member * size, size, 1)
    bias_kv = jnp.concatenate([jnp.zeros((1, part), F32), slab(row(1), part)], 1)
    bias_q = slab(row(0), part)
    bias_up = slab(up_bias.reshape(1, -1), hidden)
    both = jnp.concatenate([cross_in, grad_own], 0)[None]
    both = net.grow(net.grow(both, lo, 0), hi, 0)
    count = TP * own
    full, wide, flat = (count, width), (count, 2 * part), (count, part)

    def project(x_ref, cols_ref, bias_kv_ref, bias_q_ref, hidden_ref, grad_ref, low_ref, kv_ref, q_ref):
        values = jnp.concatenate([x_ref[t, :own, :] for t in range(TP)], 0)
        hidden_ref[...] = values
        grad_ref[...] = jnp.concatenate([x_ref[t, own:, :] for t in range(TP)], 0)
        low = values.astype(BF16)
        low_ref[...] = low
        kv = dot(low, cols_ref[:, hidden : hidden + 2 * part]) + bias_kv_ref[...]
        kv_ref[...] = kv.astype(BF16)
        q_ref[...] = (dot(low, cols_ref[:, hidden + 2 * part : hidden + 3 * part]) + bias_q_ref[...]).astype(BF16)

    hidden_all, grad_all, hidden_low, kv, queries = fused(
        project,
        [(full, F32), (full, F32), (full, BF16), (wide, BF16), (flat, BF16)],
        both, cols, bias_kv, bias_q,
        name="cross_project",
    )
    have = kv
    for b in up:
        have = jnp.concatenate([have, net.hop(have, b)], 0)
    late = net.hop(have, 0)
    seen = 2 * have.shape[0]

    def attend(q_ref, have_ref, late_ref, allowed_ref, out_w_ref, chance_ref, context_ref, part_ref):
        kv = jnp.concatenate([have_ref[...], late_ref[...]], 0)
        q = q_ref[...]
        spread = stack_heads(jnp.concatenate([q, jnp.zeros_like(q)], 1), heads, 0)
        scores = dot_nt(spread, kv) * SCALE
        scores = jnp.where(jnp.concatenate([allowed_ref[...]] * heads, 0) > 0.5, scores, -1e30)
        raised = jnp.exp(scores - jnp.max(scores, axis=1, keepdims=True))
        chance = raised * (1.0 / jnp.sum(raised, axis=1, keepdims=True))
        chance_ref[...] = chance
        context = merge_heads(dot(chance.astype(BF16), kv), heads, part)[:, part:].astype(BF16)
        context_ref[...] = context
        part_ref[...] = dot(context, out_w_ref[...]).astype(BF16)

    chance, context, partial_sum = fused(
        attend,
        [((heads * count, seen), F32), (flat, BF16), (full, BF16)],
        queries, have, late, allowed, w_out,
        name="cross_attend",
    )
    half_sum = settle(partial_sum, net.hop(partial_sum, lo))
    other_sum = net.hop(half_sum, hi)

    def feed(
        x_ref, a_ref, b_ref, bias_ref, gain_ref, cols_ref, bias_up_ref, down_ref,
        normed_ref, normal_ref, inverse_ref, low_ref, active_ref, slope_ref, part_ref,
    ):
        mixed = x_ref[...] + (a_ref[...].astype(F32) + b_ref[...].astype(F32)) + bias_ref[2:3, :]
        normal, inverse = normalize(mixed)
        normed = normal * gain_ref[0:1, :] + bias_ref[3:4, :]
        low = normed.astype(BF16)
        active, slope = gelu_pair(dot(low, cols_ref[:, :hidden]) + bias_up_ref[...])
        active = active.astype(BF16)
        normed_ref[...] = normed
        normal_ref[...] = normal
        inverse_ref[...] = inverse
        low_ref[...] = low
        active_ref[...] = active
        slope_ref[...] = slope
        part_ref[...] = dot(active, down_ref[...]).astype(BF16)

    normed, normal1, inverse1, normed_low, active, slope, partial_sum = fused(
        feed,
        [
            (full, F32), (full, F32), ((count, 1), F32), (full, BF16),
            ((count, hidden), BF16), ((count, hidden), F32), (full, BF16),
        ],
        hidden_all, half_sum, other_sum, biases, gains, cols, bias_up, w_down,
        name="cross_feed",
    )
    half_sum = settle(partial_sum, net.hop(partial_sum, lo))
    other_sum = net.hop(half_sum, hi)

    def turn(
        normed_ref, a_ref, b_ref, bias_ref, gain_ref, grad_ref, down_ref, slope_ref, cols_ref,
        result_ref, normal_ref, second_ref, ffn_ref, before_ref, part_ref,
    ):
        second = normed_ref[...] + (a_ref[...].astype(F32) + b_ref[...].astype(F32)) + bias_ref[4:5, :]
        normal, inverse = normalize(second)
        gain = gain_ref[1:2, :]
        result_ref[...] = normal * gain + bias_ref[5:6, :]
        normal_ref[...] = normal
        grad_second = normalize_back(grad_ref[...] * gain, normal, inverse)
        second_ref[...] = grad_second
        ffn = grad_second.astype(BF16)
        ffn_ref[...] = ffn
        before = (dot_nt(ffn, down_ref[...]) * slope_ref[...]).astype(BF16)
        before_ref[...] = before
        part_ref[...] = dot_nt(before, cols_ref[:, :hidden]).astype(BF16)

    result, normal2, grad_second, grad_ffn, grad_before, partial_sum = fused(
        turn,
        [
            (full, F32), (full, F32), (full, F32), (full, BF16),
            ((count, hidden), BF16), (full, BF16),
        ],
        normed, half_sum, other_sum, biases, gains, grad_all, w_down, slope, cols,
        name="cross_turn",
    )
    half_sum = settle(partial_sum, net.hop(partial_sum, lo))
    other_sum = net.hop(half_sum, hi)

    def attend_back(
        second_ref, a_ref, b_ref, normal_ref, inverse_ref, gain_ref, out_w_ref, chance_ref,
        q_ref, have_ref, late_ref,
        normed_ref, mixed_ref, attn_ref, grad_q_ref, keep_ref, send_ref,
    ):
        grad_normed = second_ref[...] + (a_ref[...].astype(F32) + b_ref[...].astype(F32))
        normed_ref[...] = grad_normed
        grad_mixed = normalize_back(
            grad_normed * gain_ref[0:1, :], normal_ref[...], inverse_ref[...]
        )
        mixed_ref[...] = grad_mixed
        attn = grad_mixed.astype(BF16)
        attn_ref[...] = attn
        grad = dot_nt(attn, out_w_ref[...]).astype(BF16)
        grads = stack_heads(jnp.concatenate([jnp.zeros_like(grad), grad], 1), heads, part)
        q = q_ref[...]
        spread = stack_heads(jnp.concatenate([q, jnp.zeros_like(q)], 1), heads, 0)
        kv = jnp.concatenate([have_ref[...], late_ref[...]], 0)
        chance = chance_ref[...]
        slopes = dot_nt(grads, kv)
        slopes = slopes - jnp.sum(slopes * chance, axis=1, keepdims=True)
        tilt = (chance * slopes).astype(BF16)
        grad_q = merge_heads(dot(tilt, kv), heads, 0)[:, :part] * SCALE
        grad_q_ref[...] = grad_q.astype(BF16)
        grad_kv = dot_tn(tilt, spread) * SCALE + dot_tn(chance.astype(BF16), grads)
        keep_ref[...] = grad_kv[: seen // 2]
        send_ref[...] = grad_kv[seen // 2 :]

    grad_normed, grad_mixed, grad_attn, grad_q, keep, send = fused(
        attend_back,
        [
            (full, F32), (full, F32), (full, BF16), (flat, BF16),
            ((seen // 2, 2 * part), F32), ((seen // 2, 2 * part), F32),
        ],
        grad_second, half_sum, other_sum, normal1, inverse1, gains, w_out, chance,
        queries, have, late,
        name="cross_attend_back",
    )
    other = net.hop(send, 0)
    for b in up[::-1]:
        size = keep.shape[0] // 2
        total = keep + other
        keep, other = total[:size], net.hop(total[size:], b)

    def project_back(grad_q_ref, keep_ref, other_ref, cols_ref, grad_ref, back_ref):
        grad_kv = (keep_ref[...] + other_ref[...]).astype(BF16)
        grad_q = grad_q_ref[...]
        grad_ref[...] = jnp.concatenate([grad_kv, grad_q], 1)
        back = dot_nt(grad_kv, cols_ref[:, hidden : hidden + 2 * part]) + dot_nt(
            grad_q, cols_ref[:, hidden + 2 * part : hidden + 3 * part]
        )
        back_ref[...] = back.astype(BF16)

    grad_kvq, back = fused(
        project_back,
        [((count, 3 * part), BF16), (full, BF16)],
        grad_q, keep, other, cols,
        name="cross_project_back",
    )
    half_sum = settle(back, net.hop(back, lo))
    grad_in = grad_mixed + settle(half_sum, net.hop(half_sum, hi), F32)
    mine = lambda values: lax.dynamic_slice_in_dim(values, member * own, own, 0)

    def feed_grads(normed_ref, before_ref, active_ref, ffn_ref, up_ref, down_ref):
        up_ref[...] = dot_tn(normed_ref[...], before_ref[...]).astype(BF16)
        down_ref[...] = dot_tn(active_ref[...], ffn_ref[...]).astype(BF16)

    grad_up, grad_down = fused(
        feed_grads,
        [((width, hidden), BF16), (w_down.shape, BF16)],
        normed_low, grad_before, active, grad_ffn,
        name="cross_feed_grads",
    )

    def attend_grads(
        low_ref, grad_ref, context_ref, attn_ref, in_ref, onehot_ref, rest_ref, out_ref
    ):
        table = dot_tn(in_ref[...].astype(BF16), onehot_ref[...])
        rest_ref[...] = jnp.concatenate(
            [
                dot_tn(low_ref[...], grad_ref[...]),
                table,
                jnp.zeros((width, part - table.shape[1]), F32),
            ],
            1,
        ).astype(BF16)
        out_ref[...] = dot_tn(context_ref[...], attn_ref[...]).astype(BF16)

    rest, grad_wout = fused(
        attend_grads,
        [((width, width), BF16), (w_out.shape, BF16)],
        hidden_low, grad_kvq, context, grad_attn, grad_in, onehot,
        name="cross_attend_grads",
    )
    grads = grad_up, rest, grad_wout, grad_down

    def small_sums(
        member_ref, grad_ref, attn_ref, normed_ref, ffn_ref, result_grad_ref, normal1_ref,
        normal2_ref, before_ref, out_ref,
    ):
        member = member_ref[0]
        rows = lax.broadcasted_iota(jnp.int32, full, 0) // own == member
        ours = lambda values: jnp.sum(jnp.where(rows, values, 0.0), axis=0, keepdims=True)
        every = lambda values: jnp.sum(values.astype(F32), axis=0, keepdims=True)

        def spread(values):
            return jnp.concatenate([jnp.where(member == j, values, 0.0) for j in range(TP)], 1)

        sums = every(grad_ref[...])
        grad_normed, grad_result = normed_ref[...], result_grad_ref[...]
        out_ref[...] = jnp.zeros_like(out_ref)
        out_ref[0:1, :] = spread(sums[:, 2 * part :])
        out_ref[1:2, :] = spread(sums[:, part : 2 * part])
        out_ref[2:3, :] = ours(attn_ref[...].astype(F32))
        out_ref[3:4, :] = ours(grad_normed)
        out_ref[4:5, :] = ours(ffn_ref[...].astype(F32))
        out_ref[5:6, :] = ours(grad_result)
        out_ref[6:7, :] = ours(grad_normed * normal1_ref[...])
        out_ref[7:8, :] = ours(grad_result * normal2_ref[...])
        up_sums = every(before_ref[...])
        per = hidden // width
        for j in range(TP):
            for k in range(per):
                at = 8 + j * per + k
                out_ref[at : at + 1, :] = jnp.where(
                    member == j, up_sums[:, k * width : (k + 1) * width], 0.0
                )

    lines = 8 + hidden * TP // width
    small = pl.pallas_call(
        small_sums,
        out_shape=jax.ShapeDtypeStruct((lines, width), F32),
        in_specs=[pl.BlockSpec(memory_space=pltpu.SMEM)]
        + [pl.BlockSpec(memory_space=pltpu.VMEM)] * 8,
        name="cross_small_sums",
        compiler_params=pltpu.CompilerParams(vmem_limit_bytes=8 << 20),
        cost_estimate=work(2),
    )(member.reshape(1), grad_kvq, grad_attn, grad_normed, grad_ffn, grad_all, normal1, normal2,
      grad_before)
    return mine(result), mine(grad_in), grads, small


def places_of(ids, slots, seq_ids, table_rows):
    all_slots = jnp.arange(seq_ids.shape[0], dtype=jnp.int32)
    earlier = (seq_ids[None, :] == ids[:, None]) & (all_slots[None, :] < slots[:, None])
    places = jnp.sum(earlier.astype(jnp.int32), axis=1)
    rows = jnp.arange(table_rows, dtype=jnp.int32)
    return (places[:, None] == rows[None, :]).astype(BF16)


def shards(
    count, tokens, seq_ids, w_qkv, w_out, w_up, w_down, biases, up_bias, norm_gains, pos_table, cotangent
):
    net = Net(count)
    rows_here, width = tokens.shape
    segs_here = rows_here // SEG
    share, hidden = biases.shape[2], up_bias.shape[1]
    half = width // 2
    lo, hi = net.bits - 2, net.bits - 1
    planes = count // TP

    order = list(range(1, net.bits - 2)) + [0]
    masks = [0]
    for b in order:
        masks = masks + [m | 1 << b for m in masks]
    slots = jnp.arange(seq_ids.shape[0], dtype=jnp.int32).reshape(TP, planes, segs_here)
    key_slots = jnp.take(slots, (net.me & (planes - 1)) ^ jnp.array(masks, jnp.int32), axis=1)
    row_slots = key_slots[:, 0].reshape(-1)
    key_ids = seq_ids[key_slots.transpose(1, 0, 2).reshape(-1)]
    row_ids = seq_ids[row_slots]
    allowed = (row_ids[:, None] == key_ids[None, :]).astype(F32)
    onehot = places_of(row_ids, row_slots, seq_ids, pos_table.shape[0])

    grad_rows = cotangent.reshape(segs_here, SEG, width)
    table = pos_table.T
    small = jnp.concatenate(
        [v.reshape(-1, share) for v in (biases, norm_gains, up_bias)], 0
    )
    if share % 8:
        first_packed = packed = None
    else:
        first_packed = pack_first(w_qkv, table, biases, norm_gains, up_bias)
        packed = stack_columns(width, w_out[0], w_up[0])
    shares_down = w_down[0]
    cross_shares = (w_qkv[1], w_out[1], w_up[1], w_down[1])

    get_qkv = Task(gather_first(net, w_qkv[0], table, small, first_packed))
    window([], [get_qkv])
    shares_down, *cross_shares = window([shares_down, *cross_shares], [get_qkv])
    packed = tie(packed, *cross_shares)[0] if packed is not None else None
    get_middle = Task(gather_middle(net, w_out[0], w_up[0], packed))
    window([], [get_qkv])
    (shares_down,) = window([shares_down], [get_qkv, get_middle])
    tokens, *cross_shares = window([tokens, *cross_shares], [get_qkv])
    *weights_qkv, table, small = get_qkv.get()
    small = small.astype(F32)
    narrow = small[:, :16].transpose(1, 0, 2).reshape(16, width)
    long = small[:, 16:].reshape(count, 2, -1).transpose(1, 0, 2).reshape(2, 1, -1)
    biases0, gains0, up_bias0 = narrow[:6], narrow[12:14], long[0, 0]
    params1 = narrow[6:12], narrow[14:], long[1]

    allowed, onehot, biases0, gains0, up_bias0, *params1 = tie(
        allowed, onehot, biases0, gains0, up_bias0, *params1
    )

    def project(n):
        shift = jnp.concatenate(
            [
                biases0[0, n * half : (n + 1) * half],
                jnp.zeros((half,), F32),
                biases0[1, n * half : (n + 1) * half],
            ]
        )
        return (dot(tokens, weights_qkv[n]) + shift).astype(BF16)

    left = project(0)
    left, shares_down, *cross_shares = window([left, shares_down, *cross_shares], [get_middle])
    get_down = Task(gather_down(net, shares_down))
    get_cross = Task(cross_weight_steps(net, *cross_shares))
    context = segment_attend(left, 0)
    context, tokens = window([context, tokens], [get_middle, get_down, get_cross])
    right = project(1)
    (right,) = window([right], [get_down, get_cross])
    context = segment_attend(right, 1, context)
    qkv = [left, right]
    (context,) = window([context], [get_middle, get_down])
    (context,) = window([context], [get_middle])
    w_out0, w_up0 = get_middle.get()
    normed, normal1, inverse1, normed_low, active, slope = feed_up(
        tokens, context, w_out0, w_up0, biases0, gains0, up_bias0[None, :]
    )
    active, slope, normed = window([active, slope, normed], [get_down, get_cross])
    (normed,) = window([normed], [get_down])
    w_down0 = get_down.get()
    result0, firsts, normal2, inverse2 = feed_down(normed, active, w_down0, biases0, gains0)
    (firsts,) = window([firsts], [get_cross])
    firsts, *weights1 = window([firsts, *get_cross.get()], [])
    firsts = firsts.reshape(segs_here, width)

    own_onehot = lax.dynamic_slice_in_dim(onehot, (net.me >> lo) * segs_here, segs_here, 0)
    cross_in = firsts + dot_nt(own_onehot, table)
    result1, grad_cross, grads1, small1 = cross_encoder(
        net,
        cross_in,
        grad_rows[:, 0, :].astype(F32),
        weights1,
        params1,
        allowed,
        onehot,
    )
    layer_out = put_firsts(result0, result1)

    ways, back_ways = link_orders(net)
    grad_ffn, grad_before, grad_mixed, grad_attn, grad_context, small0 = tail_backward(
        cotangent, grad_cross, (normal1, inverse1, slope, normal2, inverse2), w_out0, w_up0, w_down0,
        gains0,
    )
    grad_ffn, grad_before, grad_attn, grad_context, *grads1 = tie(
        grad_ffn, grad_before, grad_attn, grad_context, *grads1
    )
    red_cross = Task(cross_grad_steps(net, *grads1, ways))
    grad_down = dot_tn(active, grad_ffn).astype(BF16)
    grad_down, grad_before, grad_attn, grad_context = window(
        [grad_down, grad_before, grad_attn, grad_context], [red_cross]
    )
    red_down = Task(reduce_steps(net, [grad_down], back_ways + [lo, hi]))
    grad_up = dot_tn(normed_low, grad_before).astype(BF16)
    grad_out = dot_tn(context, grad_attn).astype(BF16)
    grad_up, grad_out, grad_context = window([grad_up, grad_out, grad_context], [red_down])
    red_up = Task(reduce_steps(net, [grad_up], ways + [lo, hi]))
    back_left, sums_left = segment_attend_back(qkv[0], grad_context, 0)
    grad_left = dot_tn(tokens, back_left).astype(BF16)
    back_left, grad_left, grad_context = window(
        [back_left, grad_left, grad_context], [red_cross, red_up]
    )
    back_right, sums_right = segment_attend_back(qkv[1], grad_context, 1)
    grad_right = dot_tn(tokens, back_right).astype(BF16)
    grad_right, grad_left, grad_out, back_right = window(
        [grad_right, grad_left, grad_out, back_right], [red_down, red_up, red_cross]
    )
    red_left = Task(reduce_steps(net, [grad_left, grad_out], ways + [lo, hi]))
    red_right = Task(reduce_steps(net, [grad_right], back_ways + [lo, hi]))
    grad_tokens = grad_mixed + dot_nt(back_left, weights_qkv[0]) + dot_nt(back_right, weights_qkv[1])
    (grad_tokens, sums_left, sums_right) = window(
        [grad_tokens.astype(BF16), sums_left, sums_right], [red_down, red_up, red_left, red_right]
    )

    sums = [jnp.sum(v, axis=(0, 1)).reshape(3, half) for v in (sums_left, sums_right)]
    ends = [jnp.concatenate([v[n] for v in sums]) for n in (0, 2)]
    small0 = jnp.concatenate([jnp.stack(ends), small0[2:]])
    red_small = Task(total_steps(net, jnp.stack([small0, small1])))
    for _ in range(net.bits):
        window([], [red_right, red_left, red_up, red_small, red_down])

    small = red_small.get()
    narrow = lax.dynamic_slice_in_dim(small[:, :8], net.me * share, share, 2)
    long = lax.dynamic_slice_in_dim(small[:, 8:].reshape(2, -1), net.me * hidden, hidden, 1)
    (grad_down0,) = red_down.get()
    (grad_up0,) = red_up.get()
    grad_left0, grad_out0 = red_left.get()
    halves = [r.reshape(-1, 3, half) for r in (grad_left0, red_right.get()[0])]
    grad_qkv0 = jnp.stack(halves, 2).reshape(share, -1)
    shares1 = red_cross.get()
    return (
        layer_out,
        grad_tokens,
        jnp.stack([grad_qkv0, shares1[0]]),
        jnp.stack([grad_out0, shares1[1]]),
        jnp.stack([grad_up0, shares1[2]]),
        jnp.stack([grad_down0, shares1[3]]),
        narrow[:, :6],
        long,
        narrow[:, 6:],
        shares1[4][:, : pos_table.shape[0]].T,
    )


def solution(mesh):
    count = mesh.shape["ctx"] * mesh.shape["wa"]
    in_specs = (
        P(AXES, None),
        P(),
        P(None, AXES, None),
        P(None, AXES, None),
        P(None, AXES, None),
        P(None, AXES, None),
        P(None, None, AXES),
        P(None, AXES),
        P(None, None, AXES),
        P(None, AXES),
        P(AXES, None),
    )
    out_specs = (
        P(AXES, None),
        P(AXES, None),
        P(None, AXES, None),
        P(None, AXES, None),
        P(None, AXES, None),
        P(None, AXES, None),
        P(None, None, AXES),
        P(None, AXES),
        P(None, None, AXES),
        P(None, AXES),
    )
    return jax.shard_map(
        partial(shards, count), mesh=mesh, in_specs=in_specs, out_specs=out_specs, check_vma=False
    )
```

```python
from functools import partial

import jax
import jax.numpy as jnp
from jax import lax
from jax.experimental import pallas as pl
from jax.experimental.pallas import tpu as pltpu
from jax.sharding import PartitionSpec as P

HDIM = 64
SEG = 128
TP = 4
AXES = ("ctx", "wa")
F32 = jnp.float32
BF16 = jnp.bfloat16
SCALE = HDIM ** (-0.5)


def work(microseconds):
    return pl.CostEstimate(flops=microseconds * 10**9, transcendentals=0, bytes_accessed=0)


def dot(a, b, dims=((1,), (0,))):
    return lax.dot_general(a, b, (dims, ((), ())), preferred_element_type=F32)


def normalize(values):
    center = values - jnp.mean(values, axis=-1, keepdims=True)
    spread = jnp.mean(center * center, axis=-1, keepdims=True)
    inverse = lax.rsqrt(spread + 1e-05)
    return center * inverse, inverse


def normalize_back(grad, normal, inverse):
    return inverse * (
        grad
        - jnp.mean(grad, axis=-1, keepdims=True)
        - normal * jnp.mean(grad * normal, axis=-1, keepdims=True)
    )


def gelu_pair(values):
    phi = 0.5 * (1.0 + lax.erf(values * 0.7071067811865476))
    density = jnp.exp(-0.5 * values * values) * 0.3989422804014327
    return values * phi, phi + values * density


class Net:
    def __init__(self, count):
        self.count = count
        self.bits = count.bit_length() - 1
        self.me = lax.axis_index(AXES)

    def bit(self, b):
        return (self.me >> b) & 1

    def hop(self, value, b):
        return lax.ppermute(value, AXES, [(i, i ^ (1 << b)) for i in range(self.count)])

    def grow(self, value, b, axis):
        other = self.hop(value, b)
        return jnp.where(
            self.bit(b) == 0,
            jnp.concatenate([value, other], axis),
            jnp.concatenate([other, value], axis),
        )

    def pick(self, value, which, axis):
        return lax.dynamic_slice_in_dim(value, which, 1, axis)


def tie(*values):
    return lax.optimization_barrier(values)


def place_blocks(net, parts, blocks, shapes):
    arrays = [part[0] for part in parts]

    lists = [list(masks) for _, masks, _ in parts]
    table = net.me ^ jnp.array(lists, jnp.int32)

    def body(owner_ref, *refs):
        sources = refs[: len(parts)]
        targets = refs[len(parts) : len(parts) + len(shapes)]
        sem = refs[-1]
        for n, (source, (array, masks, half)) in enumerate(zip(sources, parts)):

            def move(j, carry, n=n, source=source, half=half):
                owner = owner_ref[n, j]
                for row, rows, lane, lanes, which, to_row, to_lane in blocks(half):
                    which, lead = which if isinstance(which, tuple) else (which, ())
                    to = lead + (owner, pl.ds(to_row, rows), pl.ds(to_lane, lanes))
                    pltpu.make_async_copy(
                        source.at[j, pl.ds(row, rows), pl.ds(lane, lanes)], targets[which].at[to], sem
                    ).start()
                return carry

            lax.fori_loop(0, len(masks), move, 0)
        for target in targets:
            pltpu.make_async_copy(target, target, sem).wait()

    return pl.pallas_call(
        body,
        out_shape=[jax.ShapeDtypeStruct(shape, BF16) for shape in shapes],
        in_specs=[pl.BlockSpec(memory_space=pltpu.SMEM)]
        + [pl.BlockSpec(memory_space=pl.ANY)] * len(parts),
        out_specs=[pl.BlockSpec(memory_space=pltpu.VMEM)] * len(shapes),
        scratch_shapes=[pltpu.SemaphoreType.DMA],
        name="place_blocks",
        cost_estimate=work(3),
        compiler_params=pltpu.CompilerParams(vmem_limit_bytes=16 << 20),
    )(table, *arrays)


def link_orders(net):
    mid = list(range(1, net.bits - 2))
    return mid, mid[::-1]


class Task:
    def __init__(self, steps):
        self.steps, self.flight, self.result = steps, None, None
        self.advance(None)

    def advance(self, arrived):
        try:
            self.flight = list(self.steps.send(arrived))
        except StopIteration as stop:
            self.flight, self.result = [], stop.value

    def get(self):
        while self.flight:
            self.advance(self.flight)
        return self.result


def window(values, tasks):
    done = tie(*values, *[f for task in tasks for f in task.flight])
    at = len(values)
    for task in tasks:
        size = len(task.flight)
        if size:
            task.advance(list(done[at : at + size]))
        at += size
    return done[: len(values)]


def gather_steps(net, have, high, early=False):
    have, masks = have[None], [0]
    for b in high:
        (other,) = yield [net.hop(have, b)]
        have = jnp.concatenate([have, other], 0)
        masks = masks + [m ^ (1 << b) for m in masks]
    cut = have.shape[2] // 2
    halves = [have[:, :, :cut], have[:, :, cut:]]
    orders = link_orders(net)
    lists = [masks, masks]
    for step in range(len(orders[0]) - 1):
        others = yield [net.hop(h, o[step]) for h, o in zip(halves, orders)]
        halves = [jnp.concatenate([h, o], 0) for h, o in zip(halves, others)]
        lists = [l + [m ^ (1 << o[step]) for m in l] for l, o in zip(lists, orders)]
    last = [o[-1] for o in orders]
    if early:
        arrived = yield [net.hop(h, b) for h, b in zip(halves, last)] + [
            net.hop(h, 0) for h in halves
        ]
        late, early_core = arrived[:2], arrived[2:]
        late_core = yield [net.hop(h, 0) for h in late]
    else:
        late = yield [net.hop(h, b) for h, b in zip(halves, last)]
        arrived = yield [net.hop(h, 0) for h in halves + late]
        early_core, late_core = arrived[:2], arrived[2:]
    core = [c for pair in zip(early_core, late_core) for c in pair]
    parts = []
    for n in (0, 1):
        late_list = [m ^ (1 << last[n]) for m in lists[n]]
        parts.append((halves[n], lists[n], n))
        parts.append((core[2 * n], [m ^ 1 for m in lists[n]], n))
        parts.append((late[n], late_list, n))
        parts.append((core[2 * n + 1], [m ^ 1 for m in late_list], n))
    return parts


def stack_columns(width, *shares):
    pieces = []
    for share in shares:
        for at in range(0, share.shape[1], width):
            pieces.append(share[:, at : at + width])
    return jnp.concatenate(pieces, 0)


def flat_rows(out):
    return out.reshape(-1, out.shape[2])


def pack_first(w_qkv, table, biases, gains, up_bias):
    rows, width = w_qkv.shape[1], w_qkv.shape[2] // 3
    share = biases.shape[2]
    groups = up_bias.shape[1] // share

    def body(qkv_ref, table_ref, bias_ref, gain_ref, up_ref, out_ref):
        for i in range(3):
            out_ref[i * rows : (i + 1) * rows, :] = qkv_ref[0, :, i * width : (i + 1) * width]
        up = up_ref[...].astype(F32)
        small = jnp.concatenate(
            [bias_ref[e].astype(F32) for e in (0, 1)]
            + [gain_ref[e].astype(F32) for e in (0, 1)]
            + [up[e : e + 1, k * share : (k + 1) * share] for e in (0, 1) for k in range(groups)],
            0,
        )
        small = jnp.concatenate([small, jnp.zeros((24, 128 - share), F32)], 1)
        table = table_ref[...].astype(F32)
        out_ref[3 * rows :, :] = jnp.concatenate(
            [v[i : i + 8] for v in (table, small) for i in (0, 8, 16)], 1
        ).astype(BF16)

    return pl.pallas_call(
        body, out_shape=jax.ShapeDtypeStruct((3 * rows + 8, width), BF16), name="pack_first",
        cost_estimate=work(2),
    )(w_qkv, table, biases, gains, up_bias)


def gather_first(net, w_qkv, table, small, packed):
    rows, width = w_qkv.shape[0], w_qkv.shape[1] // 3
    half = width // 2
    if packed is None:
        cube = lax.all_gather(w_qkv, AXES, axis=0, tiled=True).reshape(width, 3, 2, half)
        return (
            cube[:, :, 0].reshape(width, -1),
            cube[:, :, 1].reshape(width, -1),
            lax.all_gather(table, AXES, axis=0, tiled=True),
            lax.all_gather(small, AXES, axis=0),
        )
    parts = yield from gather_steps(net, packed, (net.bits - 1, net.bits - 2), True)
    left, right, table, small = place_blocks(
        net,
        parts,
        lambda h: [(i * rows, rows, 0, half, h, 0, i * half) for i in range(3)]
        + [(3 * rows, 8, i * 128, 128, 2 + h, i * 8, 0) for i in range(3)],
        [(net.count, rows, 3 * half)] * 2 + [(net.count, 24, 128)] * 2,
    )
    return flat_rows(left), flat_rows(right), flat_rows(table), small[:, :, :rows]


def gather_middle(net, w_out, w_up, packed):
    rows, width = w_out.shape
    if packed is None:
        return [lax.all_gather(w, AXES, axis=0, tiled=True) for w in (w_out, w_up)]
    parts = yield from gather_steps(net, packed, (net.bits - 1, net.bits - 2))
    columns = w_up.shape[1] // width
    half = width // 2
    out, up = place_blocks(
        net,
        parts,
        lambda h: [(0, rows, 0, half, 0, 0, h * half)]
        + [((i + 1) * rows, rows, 0, half, 1, 0, i * width + h * half) for i in range(columns)],
        [(net.count,) + w.shape for w in (w_out, w_up)],
    )
    return flat_rows(out), flat_rows(up)


def gather_down(net, w_down):
    rows, width = w_down.shape
    if rows % 32:
        return lax.all_gather(w_down, AXES, axis=0, tiled=True)
    parts = yield from gather_steps(net, w_down, (net.bits - 1, net.bits - 2))
    half = width // 2
    (down,) = place_blocks(
        net, parts, lambda h: [(0, rows, 0, half, 0, 0, h * half)], [(net.count, rows, width)]
    )
    return flat_rows(down)


def settle(keep, other, dtype=BF16):
    return (keep.astype(F32) + other.astype(F32)).astype(dtype)


def reduce_steps(net, grads, order):
    axis = lambda b: net.bits - 1 - b
    cubes = [g.reshape((2,) * net.bits + (g.shape[0] // net.count, g.shape[1])) for g in grads]
    widths = [g.shape[1] for g in grads]
    join = lambda values: jnp.concatenate(values, -1) if len(values) > 1 else values[0]
    arrived = yield [net.hop(net.pick(c, 1 - net.bit(0), axis(0)), 0) for c in cubes]
    pairs = [(net.pick(c, net.bit(0), axis(0)), f) for c, f in zip(cubes, arrived)]
    for b in order:
        if isinstance(b, tuple):
            if len(pairs) != 2:
                keep, other = join([k for k, _ in pairs]), join([f for _, f in pairs])
                cut = keep.shape[-1] // 256 * 128
                pairs = [(keep[..., :cut], other[..., :cut]), (keep[..., cut:], other[..., cut:])]
            sides = lambda turn: [
                settle(net.pick(k, t, axis(x)), net.pick(f, t, axis(x)))
                for (k, f), x in zip(pairs, b)
                for t in [net.bit(x) ^ turn]
            ]
            sent, kept = sides(1), sides(0)
            arrived = yield [net.hop(v, x) for v, x in zip(sent, b)]
            pairs = list(zip(kept, arrived))
            continue
        side = lambda which: join(
            [settle(net.pick(k, which, axis(b)), net.pick(f, which, axis(b))) for k, f in pairs]
        )
        sent, kept = side(1 - net.bit(b)), side(net.bit(b))
        (other,) = yield [net.hop(sent, b)]
        pairs = [(kept, other)]
    whole = settle(*pairs[0], F32)
    whole = whole.reshape(whole.shape[-2:])
    out, at = [], 0
    for w in widths:
        out.append(whole[:, at : at + w])
        at += w
    return out


def ordered(net, value, other, b, axis):
    return jnp.where(
        net.bit(b) == 0,
        jnp.concatenate([value, other], axis),
        jnp.concatenate([other, value], axis),
    )


def trade_pair(net, value, b, axis):
    return net.hop(net.pick(value, 1 - net.bit(b), axis), b), net.pick(value, net.bit(b), axis)


def dot_nt(a, b):
    return dot(a, b, ((1,), (1,)))


def dot_tn(a, b):
    return dot(a, b, ((0,), (0,)))


def pick_lanes(mask, values):
    return jnp.where(mask, values, jnp.zeros_like(values))


def head_masks(rows):
    lane = lax.broadcasted_iota(jnp.int32, (rows, 2 * HDIM), 1)
    return lane < HDIM, lane >= HDIM


def chance_of(keys, queries):
    scores = dot_nt(keys, queries) * SCALE
    raised = jnp.exp(scores - jnp.max(scores, axis=0, keepdims=True))
    return raised * (1.0 / jnp.sum(raised, axis=0, keepdims=True))


def attend_forward_body(heads, qkv_ref, out_ref):
    width = heads * HDIM
    for at in range(0, width, 2 * HDIM):
        queries, keys, values = [qkv_ref[:, n * width + at : n * width + at + 128] for n in range(3)]
        total = 0.0
        for mask in head_masks(SEG):
            chance = chance_of(pick_lanes(mask, keys), queries).astype(BF16)
            total = total + dot_tn(pick_lanes(mask, values), chance)
        out_ref[:, at : at + 128] = total.T.astype(BF16)


def attend_backward_body(heads, qkv_ref, grad_ref, out_ref, sums_ref):
    width = heads * HDIM
    for at in range(0, width, 2 * HDIM):
        queries, keys, values = [qkv_ref[:, n * width + at : n * width + at + 128] for n in range(3)]
        grad = grad_ref[:, at : at + 128]
        totals = [0.0, 0.0, 0.0]
        for mask in head_masks(SEG):
            own_keys = pick_lanes(mask, keys)
            chance = chance_of(own_keys, queries)
            slope = dot_nt(pick_lanes(mask, values), grad)
            slope = slope - jnp.sum(slope * chance, axis=0, keepdims=True)
            tilt = (chance * slope).astype(BF16)
            totals[0] = totals[0] + dot_tn(tilt, own_keys)
            totals[1] = totals[1] + dot(tilt, pick_lanes(mask, queries))
            totals[2] = totals[2] + dot(chance.astype(BF16), pick_lanes(mask, grad))
        for n, (total, scale) in enumerate(zip(totals, (SCALE, SCALE, 1.0))):
            low = (total * scale).astype(BF16)
            out_ref[:, n * width + at : n * width + at + 128] = low
            sums_ref[0, :, n * width + at : n * width + at + 128] = jnp.sum(
                low.astype(F32), axis=0, keepdims=True
            )


def segment_attend(qkv, half, context=None):
    rows, width = qkv.shape[0], qkv.shape[1] // 3

    def body(*refs):
        attend_forward_body(width // HDIM, refs[0], refs[-1])

    return pl.pallas_call(
        body,
        out_shape=jax.ShapeDtypeStruct((rows, 2 * width), BF16),
        grid=(rows // SEG,),
        in_specs=[pl.BlockSpec((SEG, 3 * width), lambda i: (i, 0))]
        + [pl.BlockSpec(memory_space=pl.ANY)] * half,
        out_specs=pl.BlockSpec((SEG, width), lambda i: (i, half)),
        input_output_aliases={1: 0} if half else {},
        name="segment_attend",
        compiler_params=pltpu.CompilerParams(vmem_limit_bytes=12 << 20),
        cost_estimate=work(10),
    )(*([qkv, context] if half else [qkv]))


def segment_attend_back(qkv, grad, half):
    rows, width = qkv.shape[0], qkv.shape[1] // 3
    return pl.pallas_call(
        partial(attend_backward_body, width // HDIM),
        out_shape=(
            jax.ShapeDtypeStruct((rows, 3 * width), BF16),
            jax.ShapeDtypeStruct((rows // SEG, 1, 3 * width), F32),
        ),
        grid=(rows // SEG,),
        in_specs=[
            pl.BlockSpec((SEG, 3 * width), lambda i: (i, 0)),
            pl.BlockSpec((SEG, width), lambda i: (i, half)),
        ],
        out_specs=(
            pl.BlockSpec((SEG, 3 * width), lambda i: (i, 0)),
            pl.BlockSpec((1, 1, 3 * width), lambda i: (i, 0, 0)),
        ),
        name="segment_attend_back",
        compiler_params=pltpu.CompilerParams(vmem_limit_bytes=16 << 20),
        cost_estimate=work(12),
    )(qkv, grad)


BLOCK = 256


def row_block(width):
    return pl.BlockSpec((BLOCK, width), lambda i: (i, 0))


def whole(shape):
    return pl.BlockSpec(
        shape, lambda i: (0,) * len(shape), pipeline_mode=pl.Buffered(1)
    )


def feed_up(tokens, context, w_out, w_up, biases, gains, up_bias):
    rows, width = tokens.shape
    hidden = w_up.shape[1]

    def body(
        tokens_ref, context_ref, out_ref, up_ref, bias_ref, gain_ref, up_bias_ref,
        normed_ref, normal_ref, inverse_ref, low_ref, active_ref, slope_ref,
    ):
        mixed = tokens_ref[...].astype(F32) + dot(context_ref[...], out_ref[...]) + bias_ref[2:3, :]
        normal, inverse = normalize(mixed)
        normal_ref[...] = normal.astype(BF16)
        inverse_ref[...] = inverse
        normed = normal * gain_ref[0:1, :] + bias_ref[3:4, :]
        normed_ref[...] = normed
        low = normed.astype(BF16)
        low_ref[...] = low
        for at in range(0, hidden, width):
            part = slice(at, at + width)
            active, slope = gelu_pair(dot(low, up_ref[:, part]) + up_bias_ref[:, part])
            active_ref[:, part] = active.astype(BF16)
            slope_ref[:, part] = slope.astype(BF16)

    outs = [(width, F32), (width, BF16), (1, F32), (width, BF16), (hidden, BF16), (hidden, BF16)]
    return pl.pallas_call(
        body,
        grid=(rows // BLOCK,),
        out_shape=[jax.ShapeDtypeStruct((rows, w), t) for w, t in outs],
        in_specs=[row_block(width)] * 2
        + [whole(v.shape) for v in (w_out, w_up, biases, gains, up_bias)],
        out_specs=[row_block(w) for w, _ in outs],
        name="feed_up",
        compiler_params=pltpu.CompilerParams(vmem_limit_bytes=36 << 20),
        cost_estimate=work(18),
    )(tokens, context, w_out, w_up, biases, gains, up_bias)


def feed_down(normed, active, w_down, biases, gains):
    rows, width = normed.shape
    per = BLOCK // SEG

    def body(
        normed_ref, active_ref, down_ref, bias_ref, gain_ref,
        result_ref, first_ref, normal_ref, inverse_ref,
    ):
        second = normed_ref[...] + dot(active_ref[...], down_ref[...]) + bias_ref[4:5, :]
        normal, inverse = normalize(second)
        normal_ref[...] = normal.astype(BF16)
        inverse_ref[...] = inverse
        result = normal * gain_ref[1:2, :] + bias_ref[5:6, :]
        result_ref[...] = result.astype(BF16)
        for k in range(per):
            first_ref[0, k : k + 1, :] = result[k * SEG : k * SEG + 1]

    return pl.pallas_call(
        body,
        grid=(rows // BLOCK,),
        out_shape=[
            jax.ShapeDtypeStruct((rows, width), BF16),
            jax.ShapeDtypeStruct((rows // BLOCK, per, width), F32),
            jax.ShapeDtypeStruct((rows, width), BF16),
            jax.ShapeDtypeStruct((rows, 1), F32),
        ],
        in_specs=[row_block(width), row_block(active.shape[1])]
        + [whole(v.shape) for v in (w_down, biases, gains)],
        out_specs=[
            row_block(width), pl.BlockSpec((1, per, width), lambda i: (i, 0, 0)), row_block(width),
            row_block(1),
        ],
        name="feed_down",
        compiler_params=pltpu.CompilerParams(vmem_limit_bytes=28 << 20),
        cost_estimate=work(11),
    )(normed, active, w_down, biases, gains)


def tail_backward(cotangent, firsts, kept, w_out, w_up, w_down, gains):
    normal1, inverse1, slope, normal2, inverse2 = kept
    rows, width = cotangent.shape
    hidden = w_up.shape[1]
    per = BLOCK // SEG
    lines = 8 + hidden // width

    def body(
        cotangent_ref, first_ref, normal1_ref, inverse1_ref, slope_ref, normal2_ref, inverse2_ref,
        out_ref, up_ref, down_ref, gain_ref,
        ffn_ref, before_ref, mixed_ref, attn_ref, context_ref, sums_ref,
    ):
        grad = cotangent_ref[...].astype(F32)
        row = lax.broadcasted_iota(jnp.int32, (BLOCK, 1), 0)
        for k in range(per):
            grad = jnp.where(row == k * SEG, first_ref[0, k : k + 1, :], grad)
        normal2 = normal2_ref[...].astype(F32)
        grad_second = normalize_back(grad * gain_ref[1:2, :], normal2, inverse2_ref[...])
        ffn = grad_second.astype(BF16)
        ffn_ref[...] = ffn
        grad_normed = grad_second
        up_sums = []
        for at in range(0, hidden, width):
            part = slice(at, at + width)
            before = dot_nt(ffn, down_ref[part, :]) * slope_ref[:, part].astype(F32)
            before = before.astype(BF16)
            before_ref[:, part] = before
            up_sums.append(before)
            grad_normed = grad_normed + dot_nt(before, up_ref[:, part])
        normal1 = normal1_ref[...].astype(F32)
        grad_mixed = normalize_back(grad_normed * gain_ref[0:1, :], normal1, inverse1_ref[...])
        mixed_ref[...] = grad_mixed
        attn = grad_mixed.astype(BF16)
        attn_ref[...] = attn
        context_ref[...] = dot_nt(attn, out_ref[...]).astype(BF16)

        @pl.when(pl.program_id(0) == 0)
        def _():
            sums_ref[...] = jnp.zeros_like(sums_ref)

        values = [attn, grad_normed, ffn, grad, grad_normed * normal1, grad * normal2] + up_sums
        for n, value in enumerate(values):
            sums_ref[n + 2 : n + 3, :] += jnp.sum(value.astype(F32), axis=0, keepdims=True)

    return pl.pallas_call(
        body,
        grid=(rows // BLOCK,),
        out_shape=[
            jax.ShapeDtypeStruct((rows, width), BF16),
            jax.ShapeDtypeStruct((rows, hidden), BF16),
            jax.ShapeDtypeStruct((rows, width), F32),
            jax.ShapeDtypeStruct((rows, width), BF16),
            jax.ShapeDtypeStruct((rows, width), BF16),
            jax.ShapeDtypeStruct((lines, width), F32),
        ],
        in_specs=[
            row_block(width),
            pl.BlockSpec((1, per, width), lambda i: (i, 0, 0)),
            row_block(width), row_block(1), row_block(hidden), row_block(width), row_block(1),
        ]
        + [whole(v.shape) for v in (w_out, w_up, w_down, gains)],
        out_specs=[
            row_block(width), row_block(hidden), row_block(width), row_block(width),
            row_block(width), pl.BlockSpec((lines, width), lambda i: (0, 0)),
        ],
        name="tail_backward",
        compiler_params=pltpu.CompilerParams(vmem_limit_bytes=36 << 20),
        cost_estimate=work(24),
    )(
        cotangent, firsts.reshape(-1, per, width), normal1, inverse1, slope, normal2, inverse2,
        w_out, w_up, w_down, gains,
    )


def put_firsts(values, firsts):
    rows, width = values.shape

    def body(old_ref, first_ref, out_ref):
        row = lax.broadcasted_iota(jnp.int32, (16, 1), 0)
        old = old_ref[...].astype(F32)
        out_ref[...] = jnp.where(row == 0, first_ref[0], old).astype(BF16)

    block = pl.BlockSpec((16, width), lambda i: (i * (SEG // 16), 0))
    return pl.pallas_call(
        body,
        grid=(rows // SEG,),
        out_shape=jax.ShapeDtypeStruct(values.shape, BF16),
        in_specs=[block, pl.BlockSpec((1, 1, width), lambda i: (i, 0, 0))],
        out_specs=block,
        input_output_aliases={0: 0},
        name="put_firsts",
        compiler_params=pltpu.CompilerParams(vmem_limit_bytes=4 << 20),
        cost_estimate=work(4),
    )(values, firsts[:, None, :])


def cross_weight_steps(net, w_qkv, w_out, w_up, w_down):
    rows, width = w_out.shape
    hi, lo = net.bits - 1, net.bits - 2
    part = width // TP
    planes = net.count // TP
    cube = w_qkv.reshape(rows, 3, TP, part)
    ups = w_up.reshape(rows, TP, -1)
    hidden = ups.shape[2]
    assert hidden == width
    kvq = jnp.concatenate([cube[:, 1], cube[:, 2], cube[:, 0], jnp.zeros_like(cube[:, 0])], 2)
    cols = jnp.stack([ups, kvq]).transpose(2, 0, 1, 3).reshape(2, 2, 2 * rows, width)
    for b, axis in ((hi, 0), (lo, 1)):
        flight, keep = trade_pair(net, cols, b, axis)
        (other,) = yield [flight]
        cols = ordered(net, keep, other, b, axis)
    have = jnp.concatenate([cols.reshape(-1, width), w_out, w_down], 0)
    if rows % 8:
        value = have[None]
        for b in range(net.bits - 2):
            (other,) = yield [net.hop(value, b)]
            value = ordered(net, value, other, b, 0)
        cols = value[:, : 8 * rows].reshape(planes, TP, 2, rows, width).transpose(1, 0, 3, 2, 4)
        return (
            cols.reshape(width, 2 * width),
            value[:, 8 * rows : 9 * rows].reshape(part, width),
            value[:, 9 * rows :].reshape(hidden, width),
        )
    parts = yield from gather_steps(net, have, ())
    parts = [(array, [m & (planes - 1) for m in masks], h) for array, masks, h in parts]
    half = width // 2
    plane = Net.__new__(Net)
    plane.me = net.me & (planes - 1)
    outs = place_blocks(
        plane,
        parts,
        lambda h: [
            ((2 * t + k) * rows, rows, 0, half, (0, (t,)), 0, k * width + h * half)
            for t in range(TP)
            for k in (0, 1)
        ]
        + [
            (8 * rows, rows, 0, half, 1, 0, h * half),
            (9 * rows, 4 * rows, 0, half, 2, 0, h * half),
        ],
        [(TP, planes, rows, 2 * width), (planes, rows, width), (planes, 4 * rows, width)],
    )
    return outs[0].reshape(width, 2 * width), flat_rows(outs[1]), flat_rows(outs[2])


def cross_grad_steps(net, ups, rest, grad_out, grad_down, order):
    hi, lo = net.bits - 1, net.bits - 2
    plane = net.bits - 2
    planes = net.count // TP
    width = ups.shape[0]
    rows = width // net.count
    part = width // TP
    pair = jnp.stack([ups.reshape(TP, planes, rows, width), rest.reshape(TP, planes, rows, width)])
    whole = jnp.concatenate(
        [
            pair.transpose(2, 1, 0, 3, 4).reshape(planes, 8 * rows, width),
            grad_out.reshape(planes, rows, width),
            grad_down.reshape(planes, 4 * rows, width),
        ],
        1,
    ).reshape((2,) * plane + (13 * rows, width))
    axis = lambda b: plane - 1 - b
    (other,) = yield [net.hop(net.pick(whole, 1 - net.bit(0), axis(0)), 0)]
    kept = net.pick(whole, net.bit(0), axis(0))
    for b in order:
        side = lambda which: settle(net.pick(kept, which, axis(b)), net.pick(other, which, axis(b)))
        sent, kept = side(1 - net.bit(b)), side(net.bit(b))
        (other,) = yield [net.hop(sent, b)]
    whole = settle(kept, other).reshape(13 * rows, width)
    cols = whole[: 8 * rows].reshape(2, 2, 2 * rows, width)
    for b, at in ((hi, 0), (lo, 1)):
        flight, keep = trade_pair(net, cols, b, at)
        (back,) = yield [flight]
        cols = ordered(net, keep, back, b, at)
    whole, cols = yield [whole, cols]
    cols = cols.reshape(TP, 2, rows, width).transpose(1, 2, 0, 3).astype(F32)
    deep = whole[8 * rows :].astype(F32)
    pieces = [cols[1, :, :, n * part : (n + 1) * part].reshape(rows, width) for n in (2, 0, 1)]
    return (
        jnp.concatenate(pieces, 1),
        deep[:rows],
        cols[0].reshape(rows, -1),
        deep[rows:],
        cols[1, :, 0, 3 * part :],
    )


def lanes_between(values, first, last):
    lane = lax.broadcasted_iota(jnp.int32, values.shape, values.ndim - 1)
    return jnp.where((lane >= first) & (lane < last), values, jnp.zeros_like(values))


def stack_heads(values, heads, first):
    return jnp.concatenate(
        [lanes_between(values, first + h * HDIM, first + (h + 1) * HDIM) for h in range(heads)], 0
    )


def merge_heads(values, heads, first):
    rows = values.shape[0] // heads
    return sum(
        lanes_between(values[h * rows : (h + 1) * rows], first + h * HDIM, first + (h + 1) * HDIM)
        for h in range(heads)
    )


def fused(body, outs, *args, name):
    return pl.pallas_call(
        body, out_shape=[jax.ShapeDtypeStruct(shape, dtype) for shape, dtype in outs], name=name,
        compiler_params=pltpu.CompilerParams(vmem_limit_bytes=32 << 20),
        cost_estimate=work(3),
    )(*args)


def cross_encoder(net, cross_in, grad_own, weights, params, allowed, onehot):
    cols, w_out, w_down = weights
    own, width = cross_in.shape
    part, hidden = w_out.shape[0], w_down.shape[0]
    plane = net.bits - 2
    hi, lo = net.bits - 1, net.bits - 2
    member = net.me >> lo
    up = list(range(1, plane))
    heads = part // HDIM
    biases, gains, up_bias = params
    row = lambda n: biases[n : n + 1]
    slab = lambda vector, size: lax.dynamic_slice_in_dim(vector, member * size, size, 1)
    bias_kv = jnp.concatenate([jnp.zeros((1, part), F32), slab(row(1), part)], 1)
    bias_q = slab(row(0), part)
    bias_up = slab(up_bias.reshape(1, -1), hidden)
    both = jnp.concatenate([cross_in, grad_own], 0)[None]
    both = net.grow(net.grow(both, lo, 0), hi, 0)
    count = TP * own
    full, wide, flat = (count, width), (count, 2 * part), (count, part)

    def project(x_ref, cols_ref, bias_kv_ref, bias_q_ref, hidden_ref, grad_ref, low_ref, kv_ref, q_ref):
        values = jnp.concatenate([x_ref[t, :own, :] for t in range(TP)], 0)
        hidden_ref[...] = values
        grad_ref[...] = jnp.concatenate([x_ref[t, own:, :] for t in range(TP)], 0)
        low = values.astype(BF16)
        low_ref[...] = low
        kv = dot(low, cols_ref[:, hidden : hidden + 2 * part]) + bias_kv_ref[...]
        kv_ref[...] = kv.astype(BF16)
        q_ref[...] = (dot(low, cols_ref[:, hidden + 2 * part : hidden + 3 * part]) + bias_q_ref[...]).astype(BF16)

    hidden_all, grad_all, hidden_low, kv, queries = fused(
        project,
        [(full, F32), (full, F32), (full, BF16), (wide, BF16), (flat, BF16)],
        both, cols, bias_kv, bias_q,
        name="cross_project",
    )
    have = kv
    for b in up:
        have = jnp.concatenate([have, net.hop(have, b)], 0)
    late = net.hop(have, 0)
    seen = 2 * have.shape[0]

    def attend(q_ref, have_ref, late_ref, allowed_ref, out_w_ref, chance_ref, context_ref, part_ref):
        kv = jnp.concatenate([have_ref[...], late_ref[...]], 0)
        q = q_ref[...]
        spread = stack_heads(jnp.concatenate([q, jnp.zeros_like(q)], 1), heads, 0)
        scores = dot_nt(spread, kv) * SCALE
        scores = jnp.where(jnp.concatenate([allowed_ref[...]] * heads, 0) > 0.5, scores, -1e30)
        raised = jnp.exp(scores - jnp.max(scores, axis=1, keepdims=True))
        chance = raised * (1.0 / jnp.sum(raised, axis=1, keepdims=True))
        chance_ref[...] = chance
        context = merge_heads(dot(chance.astype(BF16), kv), heads, part)[:, part:].astype(BF16)
        context_ref[...] = context
        part_ref[...] = dot(context, out_w_ref[...]).astype(BF16)

    chance, context, partial_sum = fused(
        attend,
        [((heads * count, seen), F32), (flat, BF16), (full, BF16)],
        queries, have, late, allowed, w_out,
        name="cross_attend",
    )
    half_sum = settle(partial_sum, net.hop(partial_sum, lo))
    other_sum = net.hop(half_sum, hi)

    def feed(
        x_ref, a_ref, b_ref, bias_ref, gain_ref, cols_ref, bias_up_ref, down_ref,
        normed_ref, normal_ref, inverse_ref, low_ref, active_ref, slope_ref, part_ref,
    ):
        mixed = x_ref[...] + (a_ref[...].astype(F32) + b_ref[...].astype(F32)) + bias_ref[2:3, :]
        normal, inverse = normalize(mixed)
        normed = normal * gain_ref[0:1, :] + bias_ref[3:4, :]
        low = normed.astype(BF16)
        active, slope = gelu_pair(dot(low, cols_ref[:, :hidden]) + bias_up_ref[...])
        active = active.astype(BF16)
        normed_ref[...] = normed
        normal_ref[...] = normal
        inverse_ref[...] = inverse
        low_ref[...] = low
        active_ref[...] = active
        slope_ref[...] = slope
        part_ref[...] = dot(active, down_ref[...]).astype(BF16)

    normed, normal1, inverse1, normed_low, active, slope, partial_sum = fused(
        feed,
        [
            (full, F32), (full, F32), ((count, 1), F32), (full, BF16),
            ((count, hidden), BF16), ((count, hidden), F32), (full, BF16),
        ],
        hidden_all, half_sum, other_sum, biases, gains, cols, bias_up, w_down,
        name="cross_feed",
    )
    half_sum = settle(partial_sum, net.hop(partial_sum, lo))
    other_sum = net.hop(half_sum, hi)

    def turn(
        normed_ref, a_ref, b_ref, bias_ref, gain_ref, grad_ref, down_ref, slope_ref, cols_ref,
        result_ref, normal_ref, second_ref, ffn_ref, before_ref, part_ref,
    ):
        second = normed_ref[...] + (a_ref[...].astype(F32) + b_ref[...].astype(F32)) + bias_ref[4:5, :]
        normal, inverse = normalize(second)
        gain = gain_ref[1:2, :]
        result_ref[...] = normal * gain + bias_ref[5:6, :]
        normal_ref[...] = normal
        grad_second = normalize_back(grad_ref[...] * gain, normal, inverse)
        second_ref[...] = grad_second
        ffn = grad_second.astype(BF16)
        ffn_ref[...] = ffn
        before = (dot_nt(ffn, down_ref[...]) * slope_ref[...]).astype(BF16)
        before_ref[...] = before
        part_ref[...] = dot_nt(before, cols_ref[:, :hidden]).astype(BF16)

    result, normal2, grad_second, grad_ffn, grad_before, partial_sum = fused(
        turn,
        [
            (full, F32), (full, F32), (full, F32), (full, BF16),
            ((count, hidden), BF16), (full, BF16),
        ],
        normed, half_sum, other_sum, biases, gains, grad_all, w_down, slope, cols,
        name="cross_turn",
    )
    half_sum = settle(partial_sum, net.hop(partial_sum, lo))
    other_sum = net.hop(half_sum, hi)

    def attend_back(
        second_ref, a_ref, b_ref, normal_ref, inverse_ref, gain_ref, out_w_ref, chance_ref,
        q_ref, have_ref, late_ref,
        normed_ref, mixed_ref, attn_ref, grad_q_ref, keep_ref, send_ref,
    ):
        grad_normed = second_ref[...] + (a_ref[...].astype(F32) + b_ref[...].astype(F32))
        normed_ref[...] = grad_normed
        grad_mixed = normalize_back(
            grad_normed * gain_ref[0:1, :], normal_ref[...], inverse_ref[...]
        )
        mixed_ref[...] = grad_mixed
        attn = grad_mixed.astype(BF16)
        attn_ref[...] = attn
        grad = dot_nt(attn, out_w_ref[...]).astype(BF16)
        grads = stack_heads(jnp.concatenate([jnp.zeros_like(grad), grad], 1), heads, part)
        q = q_ref[...]
        spread = stack_heads(jnp.concatenate([q, jnp.zeros_like(q)], 1), heads, 0)
        kv = jnp.concatenate([have_ref[...], late_ref[...]], 0)
        chance = chance_ref[...]
        slopes = dot_nt(grads, kv)
        slopes = slopes - jnp.sum(slopes * chance, axis=1, keepdims=True)
        tilt = (chance * slopes).astype(BF16)
        grad_q = merge_heads(dot(tilt, kv), heads, 0)[:, :part] * SCALE
        grad_q_ref[...] = grad_q.astype(BF16)
        grad_kv = dot_tn(tilt, spread) * SCALE + dot_tn(chance.astype(BF16), grads)
        keep_ref[...] = grad_kv[: seen // 2]
        send_ref[...] = grad_kv[seen // 2 :]

    grad_normed, grad_mixed, grad_attn, grad_q, keep, send = fused(
        attend_back,
        [
            (full, F32), (full, F32), (full, BF16), (flat, BF16),
            ((seen // 2, 2 * part), F32), ((seen // 2, 2 * part), F32),
        ],
        grad_second, half_sum, other_sum, normal1, inverse1, gains, w_out, chance,
        queries, have, late,
        name="cross_attend_back",
    )
    other = net.hop(send, 0)
    for b in up[::-1]:
        size = keep.shape[0] // 2
        total = keep + other
        keep, other = total[:size], net.hop(total[size:], b)

    def project_back(grad_q_ref, keep_ref, other_ref, cols_ref, grad_ref, back_ref):
        grad_kv = (keep_ref[...] + other_ref[...]).astype(BF16)
        grad_q = grad_q_ref[...]
        grad_ref[...] = jnp.concatenate([grad_kv, grad_q], 1)
        back = dot_nt(grad_kv, cols_ref[:, hidden : hidden + 2 * part]) + dot_nt(
            grad_q, cols_ref[:, hidden + 2 * part : hidden + 3 * part]
        )
        back_ref[...] = back.astype(BF16)

    grad_kvq, back = fused(
        project_back,
        [((count, 3 * part), BF16), (full, BF16)],
        grad_q, keep, other, cols,
        name="cross_project_back",
    )
    half_sum = settle(back, net.hop(back, lo))
    grad_in = grad_mixed + settle(half_sum, net.hop(half_sum, hi), F32)
    mine = lambda values: lax.dynamic_slice_in_dim(values, member * own, own, 0)

    def feed_grads(normed_ref, before_ref, active_ref, ffn_ref, up_ref, down_ref):
        up_ref[...] = dot_tn(normed_ref[...], before_ref[...]).astype(BF16)
        down_ref[...] = dot_tn(active_ref[...], ffn_ref[...]).astype(BF16)

    grad_up, grad_down = fused(
        feed_grads,
        [((width, hidden), BF16), (w_down.shape, BF16)],
        normed_low, grad_before, active, grad_ffn,
        name="cross_feed_grads",
    )

    def attend_grads(
        low_ref, grad_ref, context_ref, attn_ref, in_ref, onehot_ref, rest_ref, out_ref
    ):
        table = dot_tn(in_ref[...].astype(BF16), onehot_ref[...])
        rest_ref[...] = jnp.concatenate(
            [
                dot_tn(low_ref[...], grad_ref[...]),
                table,
                jnp.zeros((width, part - table.shape[1]), F32),
            ],
            1,
        ).astype(BF16)
        out_ref[...] = dot_tn(context_ref[...], attn_ref[...]).astype(BF16)

    rest, grad_wout = fused(
        attend_grads,
        [((width, width), BF16), (w_out.shape, BF16)],
        hidden_low, grad_kvq, context, grad_attn, grad_in, onehot,
        name="cross_attend_grads",
    )
    grads = grad_up, rest, grad_wout, grad_down

    def small_sums(
        member_ref, grad_ref, attn_ref, normed_ref, ffn_ref, result_grad_ref, normal1_ref,
        normal2_ref, before_ref, out_ref,
    ):
        member = member_ref[0]
        rows = lax.broadcasted_iota(jnp.int32, full, 0) // own == member
        ours = lambda values: jnp.sum(jnp.where(rows, values, 0.0), axis=0, keepdims=True)
        every = lambda values: jnp.sum(values.astype(F32), axis=0, keepdims=True)

        def spread(values):
            return jnp.concatenate([jnp.where(member == j, values, 0.0) for j in range(TP)], 1)

        sums = every(grad_ref[...])
        grad_normed, grad_result = normed_ref[...], result_grad_ref[...]
        out_ref[...] = jnp.zeros_like(out_ref)
        out_ref[0:1, :] = spread(sums[:, 2 * part :])
        out_ref[1:2, :] = spread(sums[:, part : 2 * part])
        out_ref[2:3, :] = ours(attn_ref[...].astype(F32))
        out_ref[3:4, :] = ours(grad_normed)
        out_ref[4:5, :] = ours(ffn_ref[...].astype(F32))
        out_ref[5:6, :] = ours(grad_result)
        out_ref[6:7, :] = ours(grad_normed * normal1_ref[...])
        out_ref[7:8, :] = ours(grad_result * normal2_ref[...])
        up_sums = every(before_ref[...])
        per = hidden // width
        for j in range(TP):
            for k in range(per):
                at = 8 + j * per + k
                out_ref[at : at + 1, :] = jnp.where(
                    member == j, up_sums[:, k * width : (k + 1) * width], 0.0
                )

    lines = 8 + hidden * TP // width
    small = pl.pallas_call(
        small_sums,
        out_shape=jax.ShapeDtypeStruct((lines, width), F32),
        in_specs=[pl.BlockSpec(memory_space=pltpu.SMEM)]
        + [pl.BlockSpec(memory_space=pltpu.VMEM)] * 8,
        name="cross_small_sums",
        compiler_params=pltpu.CompilerParams(vmem_limit_bytes=8 << 20),
        cost_estimate=work(2),
    )(member.reshape(1), grad_kvq, grad_attn, grad_normed, grad_ffn, grad_all, normal1, normal2,
      grad_before)
    return mine(result), mine(grad_in), grads, small


def places_of(ids, slots, seq_ids, table_rows):
    all_slots = jnp.arange(seq_ids.shape[0], dtype=jnp.int32)
    earlier = (seq_ids[None, :] == ids[:, None]) & (all_slots[None, :] < slots[:, None])
    places = jnp.sum(earlier.astype(jnp.int32), axis=1)
    rows = jnp.arange(table_rows, dtype=jnp.int32)
    return (places[:, None] == rows[None, :]).astype(BF16)


def shards(
    count, tokens, seq_ids, w_qkv, w_out, w_up, w_down, biases, up_bias, norm_gains, pos_table, cotangent
):
    net = Net(count)
    rows_here, width = tokens.shape
    segs_here = rows_here // SEG
    share, hidden = biases.shape[2], up_bias.shape[1]
    half = width // 2
    lo, hi = net.bits - 2, net.bits - 1
    planes = count // TP

    order = list(range(1, net.bits - 2)) + [0]
    masks = [0]
    for b in order:
        masks = masks + [m | 1 << b for m in masks]
    slots = jnp.arange(seq_ids.shape[0], dtype=jnp.int32).reshape(TP, planes, segs_here)
    key_slots = jnp.take(slots, (net.me & (planes - 1)) ^ jnp.array(masks, jnp.int32), axis=1)
    row_slots = key_slots[:, 0].reshape(-1)
    key_ids = seq_ids[key_slots.transpose(1, 0, 2).reshape(-1)]
    row_ids = seq_ids[row_slots]
    allowed = (row_ids[:, None] == key_ids[None, :]).astype(F32)
    onehot = places_of(row_ids, row_slots, seq_ids, pos_table.shape[0])

    grad_rows = cotangent.reshape(segs_here, SEG, width)
    table = pos_table.T
    small = jnp.concatenate(
        [v.reshape(-1, share) for v in (biases, norm_gains, up_bias)], 0
    )
    if share % 8:
        first_packed = packed = None
    else:
        first_packed = pack_first(w_qkv, table, biases, norm_gains, up_bias)
        packed = stack_columns(width, w_out[0], w_up[0])
    shares_down = w_down[0]
    cross_shares = (w_qkv[1], w_out[1], w_up[1], w_down[1])

    get_qkv = Task(gather_first(net, w_qkv[0], table, small, first_packed))
    window([], [get_qkv])
    shares_down, *cross_shares = window([shares_down, *cross_shares], [get_qkv])
    packed = tie(packed, *cross_shares)[0] if packed is not None else None
    get_middle = Task(gather_middle(net, w_out[0], w_up[0], packed))
    window([], [get_qkv])
    (shares_down,) = window([shares_down], [get_qkv, get_middle])
    tokens, *cross_shares = window([tokens, *cross_shares], [get_qkv])
    *weights_qkv, table, small = get_qkv.get()
    small = small.astype(F32)
    narrow = small[:, :16].transpose(1, 0, 2).reshape(16, width)
    long = small[:, 16:].reshape(count, 2, -1).transpose(1, 0, 2).reshape(2, 1, -1)
    biases0, gains0, up_bias0 = narrow[:6], narrow[12:14], long[0, 0]
    params1 = narrow[6:12], narrow[14:], long[1]

    allowed, onehot, biases0, gains0, up_bias0, *params1 = tie(
        allowed, onehot, biases0, gains0, up_bias0, *params1
    )

    def project(n):
        shift = jnp.concatenate(
            [
                biases0[0, n * half : (n + 1) * half],
                jnp.zeros((half,), F32),
                biases0[1, n * half : (n + 1) * half],
            ]
        )
        return (dot(tokens, weights_qkv[n]) + shift).astype(BF16)

    left = project(0)
    left, shares_down, *cross_shares = window([left, shares_down, *cross_shares], [get_middle])
    get_down = Task(gather_down(net, shares_down))
    get_cross = Task(cross_weight_steps(net, *cross_shares))
    context = segment_attend(left, 0)
    context, tokens = window([context, tokens], [get_middle, get_down, get_cross])
    right = project(1)
    (right,) = window([right], [get_down, get_cross])
    context = segment_attend(right, 1, context)
    qkv = [left, right]
    (context,) = window([context], [get_middle, get_down])
    (context,) = window([context], [get_middle])
    w_out0, w_up0 = get_middle.get()
    normed, normal1, inverse1, normed_low, active, slope = feed_up(
        tokens, context, w_out0, w_up0, biases0, gains0, up_bias0[None, :]
    )
    active, slope, normed = window([active, slope, normed], [get_down, get_cross])
    (normed,) = window([normed], [get_down])
    w_down0 = get_down.get()
    result0, firsts, normal2, inverse2 = feed_down(normed, active, w_down0, biases0, gains0)
    (firsts,) = window([firsts], [get_cross])
    firsts, *weights1 = window([firsts, *get_cross.get()], [])
    firsts = firsts.reshape(segs_here, width)

    own_onehot = lax.dynamic_slice_in_dim(onehot, (net.me >> lo) * segs_here, segs_here, 0)
    cross_in = firsts + dot_nt(own_onehot, table)
    result1, grad_cross, grads1, small1 = cross_encoder(
        net,
        cross_in,
        grad_rows[:, 0, :].astype(F32),
        weights1,
        params1,
        allowed,
        onehot,
    )
    layer_out = put_firsts(result0, result1)

    ways, back_ways = link_orders(net)
    grad_ffn, grad_before, grad_mixed, grad_attn, grad_context, small0 = tail_backward(
        cotangent, grad_cross, (normal1, inverse1, slope, normal2, inverse2), w_out0, w_up0, w_down0,
        gains0,
    )
    grad_ffn, grad_before, grad_attn, grad_context, *grads1 = tie(
        grad_ffn, grad_before, grad_attn, grad_context, *grads1
    )
    red_cross = Task(cross_grad_steps(net, *grads1, ways))
    grad_down = dot_tn(active, grad_ffn).astype(BF16)
    grad_down, grad_before, grad_attn, grad_context = window(
        [grad_down, grad_before, grad_attn, grad_context], [red_cross]
    )
    red_down = Task(reduce_steps(net, [grad_down], back_ways + [lo, hi]))
    grad_up = dot_tn(normed_low, grad_before).astype(BF16)
    grad_out = dot_tn(context, grad_attn).astype(BF16)
    grad_up, grad_out, grad_context = window([grad_up, grad_out, grad_context], [red_down])
    red_up = Task(reduce_steps(net, [grad_up], ways + [lo, hi]))
    back_left, sums_left = segment_attend_back(qkv[0], grad_context, 0)
    grad_left = dot_tn(tokens, back_left).astype(BF16)
    back_left, grad_left, grad_context = window(
        [back_left, grad_left, grad_context], [red_cross, red_up]
    )
    back_right, sums_right = segment_attend_back(qkv[1], grad_context, 1)
    grad_right = dot_tn(tokens, back_right).astype(BF16)
    grad_right, grad_left, grad_out, back_right, sums_left, sums_right = window(
        [grad_right, grad_left, grad_out, back_right, sums_left, sums_right], [red_down, red_up]
    )
    sums = [jnp.sum(v, axis=(0, 1)).reshape(3, half) for v in (sums_left, sums_right)]
    ends = [jnp.concatenate([v[n] for v in sums]) for n in (0, 2)]
    small0 = jnp.concatenate([jnp.stack(ends), small0[2:]])
    small = jnp.stack([small0, small1])
    narrow = small[:, :8].reshape(16, width).T
    long = small[:, 8:].reshape(2, count, -1, share).transpose(1, 3, 0, 2).reshape(width, -1)
    small = jnp.concatenate([narrow, long], 1)
    small = jnp.pad(small, ((0, 0), (0, 128 - small.shape[1]))).astype(BF16)
    red_left = Task(reduce_steps(net, [grad_left, grad_out, small], ways + [lo, hi]))
    red_right = Task(reduce_steps(net, [grad_right], back_ways + [lo, hi]))
    grad_tokens = grad_mixed + dot_nt(back_left, weights_qkv[0]) + dot_nt(back_right, weights_qkv[1])
    (grad_tokens,) = window(
        [grad_tokens.astype(BF16)], [red_left, red_right, red_down, red_up, red_cross]
    )
    for _ in range(net.bits):
        window([], [red_left, red_right, red_down, red_up, red_cross])

    grad_left0, grad_out0, small = red_left.get()
    narrow = small[:, :16].T.reshape(2, 8, share)
    long = small[:, 16 : 16 + 2 * (hidden // share)]
    long = long.reshape(share, 2, -1).transpose(1, 2, 0).reshape(2, -1)
    (grad_down0,) = red_down.get()
    (grad_up0,) = red_up.get()
    halves = [r.reshape(-1, 3, half) for r in (grad_left0, red_right.get()[0])]
    grad_qkv0 = jnp.stack(halves, 2).reshape(share, -1)
    shares1 = red_cross.get()
    return (
        layer_out,
        grad_tokens,
        jnp.stack([grad_qkv0, shares1[0]]),
        jnp.stack([grad_out0, shares1[1]]),
        jnp.stack([grad_up0, shares1[2]]),
        jnp.stack([grad_down0, shares1[3]]),
        narrow[:, :6],
        long,
        narrow[:, 6:],
        shares1[4][:, : pos_table.shape[0]].T,
    )


def solution(mesh):
    count = mesh.shape["ctx"] * mesh.shape["wa"]
    in_specs = (
        P(AXES, None),
        P(),
        P(None, AXES, None),
        P(None, AXES, None),
        P(None, AXES, None),
        P(None, AXES, None),
        P(None, None, AXES),
        P(None, AXES),
        P(None, None, AXES),
        P(None, AXES),
        P(AXES, None),
    )
    out_specs = (
        P(AXES, None),
        P(AXES, None),
        P(None, AXES, None),
        P(None, AXES, None),
        P(None, AXES, None),
        P(None, AXES, None),
        P(None, None, AXES),
        P(None, AXES),
        P(None, None, AXES),
        P(None, AXES),
    )
    return jax.shard_map(
        partial(shards, count), mesh=mesh, in_specs=in_specs, out_specs=out_specs, check_vma=False
    )
```

```python
from functools import partial

import jax
import jax.numpy as jnp
from jax import lax
from jax.experimental import pallas as pl
from jax.experimental.pallas import tpu as pltpu
from jax.sharding import PartitionSpec as P

HDIM = 64
SEG = 128
TP = 4
AXES = ("ctx", "wa")
F32 = jnp.float32
BF16 = jnp.bfloat16
SCALE = HDIM ** (-0.5)


def work(microseconds):
    return pl.CostEstimate(flops=microseconds * 10**9, transcendentals=0, bytes_accessed=0)


def dot(a, b, dims=((1,), (0,))):
    return lax.dot_general(a, b, (dims, ((), ())), preferred_element_type=F32)


def normalize(values):
    center = values - jnp.mean(values, axis=-1, keepdims=True)
    spread = jnp.mean(center * center, axis=-1, keepdims=True)
    inverse = lax.rsqrt(spread + 1e-05)
    return center * inverse, inverse


def normalize_back(grad, normal, inverse):
    return inverse * (
        grad
        - jnp.mean(grad, axis=-1, keepdims=True)
        - normal * jnp.mean(grad * normal, axis=-1, keepdims=True)
    )


def gelu_pair(values):
    phi = 0.5 * (1.0 + lax.erf(values * 0.7071067811865476))
    density = jnp.exp(-0.5 * values * values) * 0.3989422804014327
    return values * phi, phi + values * density


class Net:
    def __init__(self, count):
        self.count = count
        self.bits = count.bit_length() - 1
        self.me = lax.axis_index(AXES)

    def bit(self, b):
        return (self.me >> b) & 1

    def hop(self, value, b):
        return lax.ppermute(value, AXES, [(i, i ^ (1 << b)) for i in range(self.count)])

    def grow(self, value, b, axis):
        other = self.hop(value, b)
        return jnp.where(
            self.bit(b) == 0,
            jnp.concatenate([value, other], axis),
            jnp.concatenate([other, value], axis),
        )

    def pick(self, value, which, axis):
        return lax.dynamic_slice_in_dim(value, which, 1, axis)


def tie(*values):
    return lax.optimization_barrier(values)


def place_blocks(net, parts, blocks, shapes):
    arrays = [part[0] for part in parts]

    lists = [list(masks) for _, masks, _ in parts]
    table = net.me ^ jnp.array(lists, jnp.int32)

    def body(owner_ref, *refs):
        sources = refs[: len(parts)]
        targets = refs[len(parts) : len(parts) + len(shapes)]
        sem = refs[-1]
        for n, (source, (array, masks, half)) in enumerate(zip(sources, parts)):

            def move(j, carry, n=n, source=source, half=half):
                owner = owner_ref[n, j]
                for row, rows, lane, lanes, which, to_row, to_lane in blocks(half):
                    which, lead = which if isinstance(which, tuple) else (which, ())
                    to = lead + (owner, pl.ds(to_row, rows), pl.ds(to_lane, lanes))
                    pltpu.make_async_copy(
                        source.at[j, pl.ds(row, rows), pl.ds(lane, lanes)], targets[which].at[to], sem
                    ).start()
                return carry

            lax.fori_loop(0, len(masks), move, 0)
        for target in targets:
            pltpu.make_async_copy(target, target, sem).wait()

    return pl.pallas_call(
        body,
        out_shape=[jax.ShapeDtypeStruct(shape, BF16) for shape in shapes],
        in_specs=[pl.BlockSpec(memory_space=pltpu.SMEM)]
        + [pl.BlockSpec(memory_space=pl.ANY)] * len(parts),
        out_specs=[pl.BlockSpec(memory_space=pltpu.VMEM)] * len(shapes),
        scratch_shapes=[pltpu.SemaphoreType.DMA],
        name="place_blocks",
        cost_estimate=work(3),
        compiler_params=pltpu.CompilerParams(vmem_limit_bytes=16 << 20),
    )(table, *arrays)


def link_orders(net):
    mid = list(range(1, net.bits - 2))
    return mid, mid[::-1]


class Task:
    def __init__(self, steps):
        self.steps, self.flight, self.result = steps, None, None
        self.advance(None)

    def advance(self, arrived):
        try:
            self.flight = list(self.steps.send(arrived))
        except StopIteration as stop:
            self.flight, self.result = [], stop.value

    def get(self):
        while self.flight:
            self.advance(self.flight)
        return self.result


def window(values, tasks):
    done = tie(*values, *[f for task in tasks for f in task.flight])
    at = len(values)
    for task in tasks:
        size = len(task.flight)
        if size:
            task.advance(list(done[at : at + size]))
        at += size
    return done[: len(values)]


def gather_steps(net, have, high, early=False):
    have, masks = have[None], [0]
    for b in high:
        (other,) = yield [net.hop(have, b)]
        have = jnp.concatenate([have, other], 0)
        masks = masks + [m ^ (1 << b) for m in masks]
    cut = have.shape[2] // 2
    halves = [have[:, :, :cut], have[:, :, cut:]]
    orders = link_orders(net)
    lists = [masks, masks]
    for step in range(len(orders[0]) - 1):
        others = yield [net.hop(h, o[step]) for h, o in zip(halves, orders)]
        halves = [jnp.concatenate([h, o], 0) for h, o in zip(halves, others)]
        lists = [l + [m ^ (1 << o[step]) for m in l] for l, o in zip(lists, orders)]
    last = [o[-1] for o in orders]
    if early:
        arrived = yield [net.hop(h, b) for h, b in zip(halves, last)] + [
            net.hop(h, 0) for h in halves
        ]
        late, early_core = arrived[:2], arrived[2:]
        late_core = yield [net.hop(h, 0) for h in late]
    else:
        late = yield [net.hop(h, b) for h, b in zip(halves, last)]
        arrived = yield [net.hop(h, 0) for h in halves + late]
        early_core, late_core = arrived[:2], arrived[2:]
    core = [c for pair in zip(early_core, late_core) for c in pair]
    parts = []
    for n in (0, 1):
        late_list = [m ^ (1 << last[n]) for m in lists[n]]
        parts.append((halves[n], lists[n], n))
        parts.append((core[2 * n], [m ^ 1 for m in lists[n]], n))
        parts.append((late[n], late_list, n))
        parts.append((core[2 * n + 1], [m ^ 1 for m in late_list], n))
    return parts


def stack_columns(width, *shares):
    pieces = []
    for share in shares:
        for at in range(0, share.shape[1], width):
            pieces.append(share[:, at : at + width])
    return jnp.concatenate(pieces, 0)


def flat_rows(out):
    return out.reshape(-1, out.shape[2])


def pack_first(w_qkv, table, biases, gains, up_bias):
    rows, width = w_qkv.shape[1], w_qkv.shape[2] // 3
    share = biases.shape[2]
    groups = up_bias.shape[1] // share

    def body(qkv_ref, table_ref, bias_ref, gain_ref, up_ref, out_ref):
        for i in range(3):
            out_ref[i * rows : (i + 1) * rows, :] = qkv_ref[0, :, i * width : (i + 1) * width]
        up = up_ref[...].astype(F32)
        small = jnp.concatenate(
            [bias_ref[e].astype(F32) for e in (0, 1)]
            + [gain_ref[e].astype(F32) for e in (0, 1)]
            + [up[e : e + 1, k * share : (k + 1) * share] for e in (0, 1) for k in range(groups)],
            0,
        )
        small = jnp.concatenate([small, jnp.zeros((24, 128 - share), F32)], 1)
        table = table_ref[...].astype(F32)
        out_ref[3 * rows :, :] = jnp.concatenate(
            [v[i : i + 8] for v in (table, small) for i in (0, 8, 16)], 1
        ).astype(BF16)

    return pl.pallas_call(
        body, out_shape=jax.ShapeDtypeStruct((3 * rows + 8, width), BF16), name="pack_first",
        cost_estimate=work(2),
    )(w_qkv, table, biases, gains, up_bias)


def gather_first(net, w_qkv, table, small, packed):
    rows, width = w_qkv.shape[0], w_qkv.shape[1] // 3
    half = width // 2
    if packed is None:
        cube = lax.all_gather(w_qkv, AXES, axis=0, tiled=True).reshape(width, 3, 2, half)
        return (
            cube[:, :, 0].reshape(width, -1),
            cube[:, :, 1].reshape(width, -1),
            lax.all_gather(table, AXES, axis=0, tiled=True),
            lax.all_gather(small, AXES, axis=0),
        )
    parts = yield from gather_steps(net, packed, (net.bits - 1, net.bits - 2), True)
    left, right, table, small = place_blocks(
        net,
        parts,
        lambda h: [(i * rows, rows, 0, half, h, 0, i * half) for i in range(3)]
        + [(3 * rows, 8, i * 128, 128, 2 + h, i * 8, 0) for i in range(3)],
        [(net.count, rows, 3 * half)] * 2 + [(net.count, 24, 128)] * 2,
    )
    return flat_rows(left), flat_rows(right), flat_rows(table), small[:, :, :rows]


def gather_middle(net, w_out, w_up, packed):
    rows, width = w_out.shape
    if packed is None:
        return [lax.all_gather(w, AXES, axis=0, tiled=True) for w in (w_out, w_up)]
    parts = yield from gather_steps(net, packed, (net.bits - 1, net.bits - 2))
    columns = w_up.shape[1] // width
    half = width // 2
    out, up = place_blocks(
        net,
        parts,
        lambda h: [(0, rows, 0, half, 0, 0, h * half)]
        + [((i + 1) * rows, rows, 0, half, 1, 0, i * width + h * half) for i in range(columns)],
        [(net.count,) + w.shape for w in (w_out, w_up)],
    )
    return flat_rows(out), flat_rows(up)


def gather_down(net, w_down):
    rows, width = w_down.shape
    if rows % 32:
        return lax.all_gather(w_down, AXES, axis=0, tiled=True)
    parts = yield from gather_steps(net, w_down, (net.bits - 1, net.bits - 2))
    half = width // 2
    (down,) = place_blocks(
        net, parts, lambda h: [(0, rows, 0, half, 0, 0, h * half)], [(net.count, rows, width)]
    )
    return flat_rows(down)


def settle(keep, other, dtype=BF16):
    return (keep.astype(F32) + other.astype(F32)).astype(dtype)


def reduce_steps(net, grads, order):
    axis = lambda b: net.bits - 1 - b
    cubes = [g.reshape((2,) * net.bits + (g.shape[0] // net.count, g.shape[1])) for g in grads]
    widths = [g.shape[1] for g in grads]
    join = lambda values: jnp.concatenate(values, -1) if len(values) > 1 else values[0]
    arrived = yield [net.hop(net.pick(c, 1 - net.bit(0), axis(0)), 0) for c in cubes]
    pairs = [(net.pick(c, net.bit(0), axis(0)), f) for c, f in zip(cubes, arrived)]
    for b in order:
        if isinstance(b, tuple):
            if len(pairs) != 2:
                keep, other = join([k for k, _ in pairs]), join([f for _, f in pairs])
                cut = keep.shape[-1] // 256 * 128
                pairs = [(keep[..., :cut], other[..., :cut]), (keep[..., cut:], other[..., cut:])]
            sides = lambda turn: [
                settle(net.pick(k, t, axis(x)), net.pick(f, t, axis(x)))
                for (k, f), x in zip(pairs, b)
                for t in [net.bit(x) ^ turn]
            ]
            sent, kept = sides(1), sides(0)
            arrived = yield [net.hop(v, x) for v, x in zip(sent, b)]
            pairs = list(zip(kept, arrived))
            continue
        side = lambda which: join(
            [settle(net.pick(k, which, axis(b)), net.pick(f, which, axis(b))) for k, f in pairs]
        )
        sent, kept = side(1 - net.bit(b)), side(net.bit(b))
        (other,) = yield [net.hop(sent, b)]
        pairs = [(kept, other)]
    whole = settle(*pairs[0], F32)
    whole = whole.reshape(whole.shape[-2:])
    out, at = [], 0
    for w in widths:
        out.append(whole[:, at : at + w])
        at += w
    return out


def ordered(net, value, other, b, axis):
    return jnp.where(
        net.bit(b) == 0,
        jnp.concatenate([value, other], axis),
        jnp.concatenate([other, value], axis),
    )


def trade_pair(net, value, b, axis):
    return net.hop(net.pick(value, 1 - net.bit(b), axis), b), net.pick(value, net.bit(b), axis)


def dot_nt(a, b):
    return dot(a, b, ((1,), (1,)))


def dot_tn(a, b):
    return dot(a, b, ((0,), (0,)))


def pick_lanes(mask, values):
    return jnp.where(mask, values, jnp.zeros_like(values))


def head_masks(rows):
    lane = lax.broadcasted_iota(jnp.int32, (rows, 2 * HDIM), 1)
    return lane < HDIM, lane >= HDIM


def chance_of(keys, queries):
    scores = dot_nt(keys, queries) * SCALE
    raised = jnp.exp(scores - jnp.max(scores, axis=0, keepdims=True))
    return raised * (1.0 / jnp.sum(raised, axis=0, keepdims=True))


def attend_forward_body(heads, qkv_ref, out_ref):
    width = heads * HDIM
    for at in range(0, width, 2 * HDIM):
        queries, keys, values = [qkv_ref[:, n * width + at : n * width + at + 128] for n in range(3)]
        total = 0.0
        for mask in head_masks(SEG):
            chance = chance_of(pick_lanes(mask, keys), queries).astype(BF16)
            total = total + dot_tn(pick_lanes(mask, values), chance)
        out_ref[:, at : at + 128] = total.T.astype(BF16)


def attend_backward_body(heads, qkv_ref, grad_ref, out_ref, sums_ref):
    width = heads * HDIM
    for at in range(0, width, 2 * HDIM):
        queries, keys, values = [qkv_ref[:, n * width + at : n * width + at + 128] for n in range(3)]
        grad = grad_ref[:, at : at + 128]
        totals = [0.0, 0.0, 0.0]
        for mask in head_masks(SEG):
            own_keys = pick_lanes(mask, keys)
            chance = chance_of(own_keys, queries)
            slope = dot_nt(pick_lanes(mask, values), grad)
            slope = slope - jnp.sum(slope * chance, axis=0, keepdims=True)
            tilt = (chance * slope).astype(BF16)
            totals[0] = totals[0] + dot_tn(tilt, own_keys)
            totals[1] = totals[1] + dot(tilt, pick_lanes(mask, queries))
            totals[2] = totals[2] + dot(chance.astype(BF16), pick_lanes(mask, grad))
        for n, (total, scale) in enumerate(zip(totals, (SCALE, SCALE, 1.0))):
            low = (total * scale).astype(BF16)
            out_ref[:, n * width + at : n * width + at + 128] = low
            sums_ref[0, :, n * width + at : n * width + at + 128] = jnp.sum(
                low.astype(F32), axis=0, keepdims=True
            )


def segment_attend(qkv, half, context=None):
    rows, width = qkv.shape[0], qkv.shape[1] // 3

    def body(*refs):
        attend_forward_body(width // HDIM, refs[0], refs[-1])

    return pl.pallas_call(
        body,
        out_shape=jax.ShapeDtypeStruct((rows, 2 * width), BF16),
        grid=(rows // SEG,),
        in_specs=[pl.BlockSpec((SEG, 3 * width), lambda i: (i, 0))]
        + [pl.BlockSpec(memory_space=pl.ANY)] * half,
        out_specs=pl.BlockSpec((SEG, width), lambda i: (i, half)),
        input_output_aliases={1: 0} if half else {},
        name="segment_attend",
        compiler_params=pltpu.CompilerParams(vmem_limit_bytes=12 << 20),
        cost_estimate=work(10),
    )(*([qkv, context] if half else [qkv]))


def segment_attend_back(qkv, grad, half):
    rows, width = qkv.shape[0], qkv.shape[1] // 3
    return pl.pallas_call(
        partial(attend_backward_body, width // HDIM),
        out_shape=(
            jax.ShapeDtypeStruct((rows, 3 * width), BF16),
            jax.ShapeDtypeStruct((rows // SEG, 1, 3 * width), F32),
        ),
        grid=(rows // SEG,),
        in_specs=[
            pl.BlockSpec((SEG, 3 * width), lambda i: (i, 0)),
            pl.BlockSpec((SEG, width), lambda i: (i, half)),
        ],
        out_specs=(
            pl.BlockSpec((SEG, 3 * width), lambda i: (i, 0)),
            pl.BlockSpec((1, 1, 3 * width), lambda i: (i, 0, 0)),
        ),
        name="segment_attend_back",
        compiler_params=pltpu.CompilerParams(vmem_limit_bytes=16 << 20),
        cost_estimate=work(12),
    )(qkv, grad)


BLOCK = 256


def row_block(width):
    return pl.BlockSpec((BLOCK, width), lambda i: (i, 0))


def whole(shape):
    return pl.BlockSpec(
        shape, lambda i: (0,) * len(shape), pipeline_mode=pl.Buffered(1)
    )


def feed_up(tokens, context, w_out, w_up, biases, gains, up_bias):
    rows, width = tokens.shape
    hidden = w_up.shape[1]

    def body(
        tokens_ref, context_ref, out_ref, up_ref, bias_ref, gain_ref, up_bias_ref,
        normed_ref, normal_ref, inverse_ref, low_ref, active_ref, slope_ref,
    ):
        mixed = tokens_ref[...].astype(F32) + dot(context_ref[...], out_ref[...]) + bias_ref[2:3, :]
        normal, inverse = normalize(mixed)
        normal_ref[...] = normal.astype(BF16)
        inverse_ref[...] = inverse
        normed = normal * gain_ref[0:1, :] + bias_ref[3:4, :]
        normed_ref[...] = normed
        low = normed.astype(BF16)
        low_ref[...] = low
        for at in range(0, hidden, width):
            part = slice(at, at + width)
            active, slope = gelu_pair(dot(low, up_ref[:, part]) + up_bias_ref[:, part])
            active_ref[:, part] = active.astype(BF16)
            slope_ref[:, part] = slope.astype(BF16)

    outs = [(width, F32), (width, BF16), (1, F32), (width, BF16), (hidden, BF16), (hidden, BF16)]
    return pl.pallas_call(
        body,
        grid=(rows // BLOCK,),
        out_shape=[jax.ShapeDtypeStruct((rows, w), t) for w, t in outs],
        in_specs=[row_block(width)] * 2
        + [whole(v.shape) for v in (w_out, w_up, biases, gains, up_bias)],
        out_specs=[row_block(w) for w, _ in outs],
        name="feed_up",
        compiler_params=pltpu.CompilerParams(vmem_limit_bytes=36 << 20),
        cost_estimate=work(18),
    )(tokens, context, w_out, w_up, biases, gains, up_bias)


def feed_down(normed, active, w_down, biases, gains):
    rows, width = normed.shape
    per = BLOCK // SEG

    def body(
        normed_ref, active_ref, down_ref, bias_ref, gain_ref,
        result_ref, first_ref, normal_ref, inverse_ref,
    ):
        second = normed_ref[...] + dot(active_ref[...], down_ref[...]) + bias_ref[4:5, :]
        normal, inverse = normalize(second)
        normal_ref[...] = normal.astype(BF16)
        inverse_ref[...] = inverse
        result = normal * gain_ref[1:2, :] + bias_ref[5:6, :]
        result_ref[...] = result.astype(BF16)
        for k in range(per):
            first_ref[0, k : k + 1, :] = result[k * SEG : k * SEG + 1]

    return pl.pallas_call(
        body,
        grid=(rows // BLOCK,),
        out_shape=[
            jax.ShapeDtypeStruct((rows, width), BF16),
            jax.ShapeDtypeStruct((rows // BLOCK, per, width), F32),
            jax.ShapeDtypeStruct((rows, width), BF16),
            jax.ShapeDtypeStruct((rows, 1), F32),
        ],
        in_specs=[row_block(width), row_block(active.shape[1])]
        + [whole(v.shape) for v in (w_down, biases, gains)],
        out_specs=[
            row_block(width), pl.BlockSpec((1, per, width), lambda i: (i, 0, 0)), row_block(width),
            row_block(1),
        ],
        name="feed_down",
        compiler_params=pltpu.CompilerParams(vmem_limit_bytes=28 << 20),
        cost_estimate=work(11),
    )(normed, active, w_down, biases, gains)


def tail_backward(cotangent, firsts, kept, w_out, w_up, w_down, gains):
    normal1, inverse1, slope, normal2, inverse2 = kept
    rows, width = cotangent.shape
    hidden = w_up.shape[1]
    per = BLOCK // SEG
    lines = 8 + hidden // width

    def body(
        cotangent_ref, first_ref, normal1_ref, inverse1_ref, slope_ref, normal2_ref, inverse2_ref,
        out_ref, up_ref, down_ref, gain_ref,
        ffn_ref, before_ref, mixed_ref, attn_ref, context_ref, sums_ref,
    ):
        grad = cotangent_ref[...].astype(F32)
        row = lax.broadcasted_iota(jnp.int32, (BLOCK, 1), 0)
        for k in range(per):
            grad = jnp.where(row == k * SEG, first_ref[0, k : k + 1, :], grad)
        normal2 = normal2_ref[...].astype(F32)
        grad_second = normalize_back(grad * gain_ref[1:2, :], normal2, inverse2_ref[...])
        ffn = grad_second.astype(BF16)
        ffn_ref[...] = ffn
        grad_normed = grad_second
        up_sums = []
        for at in range(0, hidden, width):
            part = slice(at, at + width)
            before = dot_nt(ffn, down_ref[part, :]) * slope_ref[:, part].astype(F32)
            before = before.astype(BF16)
            before_ref[:, part] = before
            up_sums.append(before)
            grad_normed = grad_normed + dot_nt(before, up_ref[:, part])
        normal1 = normal1_ref[...].astype(F32)
        grad_mixed = normalize_back(grad_normed * gain_ref[0:1, :], normal1, inverse1_ref[...])
        mixed_ref[...] = grad_mixed
        attn = grad_mixed.astype(BF16)
        attn_ref[...] = attn
        context_ref[...] = dot_nt(attn, out_ref[...]).astype(BF16)

        @pl.when(pl.program_id(0) == 0)
        def _():
            sums_ref[...] = jnp.zeros_like(sums_ref)

        values = [attn, grad_normed, ffn, grad, grad_normed * normal1, grad * normal2] + up_sums
        for n, value in enumerate(values):
            sums_ref[n + 2 : n + 3, :] += jnp.sum(value.astype(F32), axis=0, keepdims=True)

    return pl.pallas_call(
        body,
        grid=(rows // BLOCK,),
        out_shape=[
            jax.ShapeDtypeStruct((rows, width), BF16),
            jax.ShapeDtypeStruct((rows, hidden), BF16),
            jax.ShapeDtypeStruct((rows, width), F32),
            jax.ShapeDtypeStruct((rows, width), BF16),
            jax.ShapeDtypeStruct((rows, width), BF16),
            jax.ShapeDtypeStruct((lines, width), F32),
        ],
        in_specs=[
            row_block(width),
            pl.BlockSpec((1, per, width), lambda i: (i, 0, 0)),
            row_block(width), row_block(1), row_block(hidden), row_block(width), row_block(1),
        ]
        + [whole(v.shape) for v in (w_out, w_up, w_down, gains)],
        out_specs=[
            row_block(width), row_block(hidden), row_block(width), row_block(width),
            row_block(width), pl.BlockSpec((lines, width), lambda i: (0, 0)),
        ],
        name="tail_backward",
        compiler_params=pltpu.CompilerParams(vmem_limit_bytes=36 << 20),
        cost_estimate=work(24),
    )(
        cotangent, firsts.reshape(-1, per, width), normal1, inverse1, slope, normal2, inverse2,
        w_out, w_up, w_down, gains,
    )


def put_firsts(values, firsts):
    rows, width = values.shape

    def body(old_ref, first_ref, out_ref):
        row = lax.broadcasted_iota(jnp.int32, (16, 1), 0)
        old = old_ref[...].astype(F32)
        out_ref[...] = jnp.where(row == 0, first_ref[0], old).astype(BF16)

    block = pl.BlockSpec((16, width), lambda i: (i * (SEG // 16), 0))
    return pl.pallas_call(
        body,
        grid=(rows // SEG,),
        out_shape=jax.ShapeDtypeStruct(values.shape, BF16),
        in_specs=[block, pl.BlockSpec((1, 1, width), lambda i: (i, 0, 0))],
        out_specs=block,
        input_output_aliases={0: 0},
        name="put_firsts",
        compiler_params=pltpu.CompilerParams(vmem_limit_bytes=4 << 20),
        cost_estimate=work(4),
    )(values, firsts[:, None, :])


def cross_weight_steps(net, w_qkv, w_out, w_up, w_down):
    rows, width = w_out.shape
    hi, lo = net.bits - 1, net.bits - 2
    part = width // TP
    planes = net.count // TP
    cube = w_qkv.reshape(rows, 3, TP, part)
    ups = w_up.reshape(rows, TP, -1)
    hidden = ups.shape[2]
    assert hidden == width
    kvq = jnp.concatenate([cube[:, 1], cube[:, 2], cube[:, 0], jnp.zeros_like(cube[:, 0])], 2)
    cols = jnp.stack([ups, kvq]).transpose(2, 0, 1, 3).reshape(2, 2, 2 * rows, width)
    for b, axis in ((hi, 0), (lo, 1)):
        flight, keep = trade_pair(net, cols, b, axis)
        (other,) = yield [flight]
        cols = ordered(net, keep, other, b, axis)
    have = jnp.concatenate([cols.reshape(-1, width), w_out, w_down], 0)
    if rows % 8:
        value = have[None]
        for b in range(net.bits - 2):
            (other,) = yield [net.hop(value, b)]
            value = ordered(net, value, other, b, 0)
        cols = value[:, : 8 * rows].reshape(planes, TP, 2, rows, width).transpose(1, 0, 3, 2, 4)
        return (
            cols.reshape(width, 2 * width),
            value[:, 8 * rows : 9 * rows].reshape(part, width),
            value[:, 9 * rows :].reshape(hidden, width),
        )
    parts = yield from gather_steps(net, have, ())
    parts = [(array, [m & (planes - 1) for m in masks], h) for array, masks, h in parts]
    half = width // 2
    plane = Net.__new__(Net)
    plane.me = net.me & (planes - 1)
    outs = place_blocks(
        plane,
        parts,
        lambda h: [
            ((2 * t + k) * rows, rows, 0, half, (0, (t,)), 0, k * width + h * half)
            for t in range(TP)
            for k in (0, 1)
        ]
        + [
            (8 * rows, rows, 0, half, 1, 0, h * half),
            (9 * rows, 4 * rows, 0, half, 2, 0, h * half),
        ],
        [(TP, planes, rows, 2 * width), (planes, rows, width), (planes, 4 * rows, width)],
    )
    return outs[0].reshape(width, 2 * width), flat_rows(outs[1]), flat_rows(outs[2])


def cross_grad_steps(net, ups, rest, grad_out, grad_down, order):
    hi, lo = net.bits - 1, net.bits - 2
    plane = net.bits - 2
    planes = net.count // TP
    width = ups.shape[0]
    rows = width // net.count
    part = width // TP
    pair = jnp.stack([ups.reshape(TP, planes, rows, width), rest.reshape(TP, planes, rows, width)])
    whole = jnp.concatenate(
        [
            pair.transpose(2, 1, 0, 3, 4).reshape(planes, 8 * rows, width),
            grad_out.reshape(planes, rows, width),
            grad_down.reshape(planes, 4 * rows, width),
        ],
        1,
    ).reshape((2,) * plane + (13 * rows, width))
    axis = lambda b: plane - 1 - b
    (other,) = yield [net.hop(net.pick(whole, 1 - net.bit(0), axis(0)), 0)]
    kept = net.pick(whole, net.bit(0), axis(0))
    for b in order:
        side = lambda which: settle(net.pick(kept, which, axis(b)), net.pick(other, which, axis(b)))
        sent, kept = side(1 - net.bit(b)), side(net.bit(b))
        (other,) = yield [net.hop(sent, b)]
    whole = settle(kept, other).reshape(13 * rows, width)
    cols = whole[: 8 * rows].reshape(2, 2, 2 * rows, width)
    for b, at in ((hi, 0), (lo, 1)):
        flight, keep = trade_pair(net, cols, b, at)
        (back,) = yield [flight]
        cols = ordered(net, keep, back, b, at)
    whole, cols = yield [whole, cols]
    cols = cols.reshape(TP, 2, rows, width).transpose(1, 2, 0, 3).astype(F32)
    deep = whole[8 * rows :].astype(F32)
    pieces = [cols[1, :, :, n * part : (n + 1) * part].reshape(rows, width) for n in (2, 0, 1)]
    return (
        jnp.concatenate(pieces, 1),
        deep[:rows],
        cols[0].reshape(rows, -1),
        deep[rows:],
        cols[1, :, 0, 3 * part :],
    )


def lanes_between(values, first, last):
    lane = lax.broadcasted_iota(jnp.int32, values.shape, values.ndim - 1)
    return jnp.where((lane >= first) & (lane < last), values, jnp.zeros_like(values))


def stack_heads(values, heads, first):
    return jnp.concatenate(
        [lanes_between(values, first + h * HDIM, first + (h + 1) * HDIM) for h in range(heads)], 0
    )


def merge_heads(values, heads, first):
    rows = values.shape[0] // heads
    return sum(
        lanes_between(values[h * rows : (h + 1) * rows], first + h * HDIM, first + (h + 1) * HDIM)
        for h in range(heads)
    )


def fused(body, outs, *args, name):
    return pl.pallas_call(
        body, out_shape=[jax.ShapeDtypeStruct(shape, dtype) for shape, dtype in outs], name=name,
        compiler_params=pltpu.CompilerParams(vmem_limit_bytes=32 << 20),
        cost_estimate=work(3),
    )(*args)


def cross_encoder(net, cross_in, grad_own, weights, params, allowed, onehot):
    cols, w_out, w_down = weights
    own, width = cross_in.shape
    part, hidden = w_out.shape[0], w_down.shape[0]
    plane = net.bits - 2
    hi, lo = net.bits - 1, net.bits - 2
    member = net.me >> lo
    up = list(range(1, plane))
    heads = part // HDIM
    biases, gains, up_bias = params
    row = lambda n: biases[n : n + 1]
    slab = lambda vector, size: lax.dynamic_slice_in_dim(vector, member * size, size, 1)
    bias_kv = jnp.concatenate([jnp.zeros((1, part), F32), slab(row(1), part)], 1)
    bias_q = slab(row(0), part)
    bias_up = slab(up_bias.reshape(1, -1), hidden)
    both = jnp.concatenate([cross_in, grad_own], 0)[None]
    both = net.grow(net.grow(both, lo, 0), hi, 0)
    count = TP * own
    full, wide, flat = (count, width), (count, 2 * part), (count, part)

    def project(x_ref, cols_ref, bias_kv_ref, bias_q_ref, hidden_ref, grad_ref, low_ref, kv_ref, q_ref):
        values = jnp.concatenate([x_ref[t, :own, :] for t in range(TP)], 0)
        hidden_ref[...] = values
        grad_ref[...] = jnp.concatenate([x_ref[t, own:, :] for t in range(TP)], 0)
        low = values.astype(BF16)
        low_ref[...] = low
        kv = dot(low, cols_ref[:, hidden : hidden + 2 * part]) + bias_kv_ref[...]
        kv_ref[...] = kv.astype(BF16)
        q_ref[...] = (dot(low, cols_ref[:, hidden + 2 * part : hidden + 3 * part]) + bias_q_ref[...]).astype(BF16)

    hidden_all, grad_all, hidden_low, kv, queries = fused(
        project,
        [(full, F32), (full, F32), (full, BF16), (wide, BF16), (flat, BF16)],
        both, cols, bias_kv, bias_q,
        name="cross_project",
    )
    have = kv
    for b in up:
        have = jnp.concatenate([have, net.hop(have, b)], 0)
    late = net.hop(have, 0)
    seen = 2 * have.shape[0]

    def attend(q_ref, have_ref, late_ref, allowed_ref, out_w_ref, chance_ref, context_ref, part_ref):
        kv = jnp.concatenate([have_ref[...], late_ref[...]], 0)
        q = q_ref[...]
        spread = stack_heads(jnp.concatenate([q, jnp.zeros_like(q)], 1), heads, 0)
        scores = dot_nt(spread, kv) * SCALE
        scores = jnp.where(jnp.concatenate([allowed_ref[...]] * heads, 0) > 0.5, scores, -1e30)
        raised = jnp.exp(scores - jnp.max(scores, axis=1, keepdims=True))
        chance = raised * (1.0 / jnp.sum(raised, axis=1, keepdims=True))
        chance_ref[...] = chance
        context = merge_heads(dot(chance.astype(BF16), kv), heads, part)[:, part:].astype(BF16)
        context_ref[...] = context
        part_ref[...] = dot(context, out_w_ref[...]).astype(BF16)

    chance, context, partial_sum = fused(
        attend,
        [((heads * count, seen), F32), (flat, BF16), (full, BF16)],
        queries, have, late, allowed, w_out,
        name="cross_attend",
    )
    half_sum = settle(partial_sum, net.hop(partial_sum, lo))
    other_sum = net.hop(half_sum, hi)

    def feed(
        x_ref, a_ref, b_ref, bias_ref, gain_ref, cols_ref, bias_up_ref, down_ref,
        normed_ref, normal_ref, inverse_ref, low_ref, active_ref, slope_ref, part_ref,
    ):
        mixed = x_ref[...] + (a_ref[...].astype(F32) + b_ref[...].astype(F32)) + bias_ref[2:3, :]
        normal, inverse = normalize(mixed)
        normed = normal * gain_ref[0:1, :] + bias_ref[3:4, :]
        low = normed.astype(BF16)
        active, slope = gelu_pair(dot(low, cols_ref[:, :hidden]) + bias_up_ref[...])
        active = active.astype(BF16)
        normed_ref[...] = normed
        normal_ref[...] = normal
        inverse_ref[...] = inverse
        low_ref[...] = low
        active_ref[...] = active
        slope_ref[...] = slope
        part_ref[...] = dot(active, down_ref[...]).astype(BF16)

    normed, normal1, inverse1, normed_low, active, slope, partial_sum = fused(
        feed,
        [
            (full, F32), (full, F32), ((count, 1), F32), (full, BF16),
            ((count, hidden), BF16), ((count, hidden), F32), (full, BF16),
        ],
        hidden_all, half_sum, other_sum, biases, gains, cols, bias_up, w_down,
        name="cross_feed",
    )
    half_sum = settle(partial_sum, net.hop(partial_sum, lo))
    other_sum = net.hop(half_sum, hi)

    def turn(
        normed_ref, a_ref, b_ref, bias_ref, gain_ref, grad_ref, down_ref, slope_ref, cols_ref,
        result_ref, normal_ref, second_ref, ffn_ref, before_ref, part_ref,
    ):
        second = normed_ref[...] + (a_ref[...].astype(F32) + b_ref[...].astype(F32)) + bias_ref[4:5, :]
        normal, inverse = normalize(second)
        gain = gain_ref[1:2, :]
        result_ref[...] = normal * gain + bias_ref[5:6, :]
        normal_ref[...] = normal
        grad_second = normalize_back(grad_ref[...] * gain, normal, inverse)
        second_ref[...] = grad_second
        ffn = grad_second.astype(BF16)
        ffn_ref[...] = ffn
        before = (dot_nt(ffn, down_ref[...]) * slope_ref[...]).astype(BF16)
        before_ref[...] = before
        part_ref[...] = dot_nt(before, cols_ref[:, :hidden]).astype(BF16)

    result, normal2, grad_second, grad_ffn, grad_before, partial_sum = fused(
        turn,
        [
            (full, F32), (full, F32), (full, F32), (full, BF16),
            ((count, hidden), BF16), (full, BF16),
        ],
        normed, half_sum, other_sum, biases, gains, grad_all, w_down, slope, cols,
        name="cross_turn",
    )
    half_sum = settle(partial_sum, net.hop(partial_sum, lo))
    other_sum = net.hop(half_sum, hi)

    def attend_back(
        second_ref, a_ref, b_ref, normal_ref, inverse_ref, gain_ref, out_w_ref, chance_ref,
        q_ref, have_ref, late_ref,
        normed_ref, mixed_ref, attn_ref, grad_q_ref, keep_ref, send_ref,
    ):
        grad_normed = second_ref[...] + (a_ref[...].astype(F32) + b_ref[...].astype(F32))
        normed_ref[...] = grad_normed
        grad_mixed = normalize_back(
            grad_normed * gain_ref[0:1, :], normal_ref[...], inverse_ref[...]
        )
        mixed_ref[...] = grad_mixed
        attn = grad_mixed.astype(BF16)
        attn_ref[...] = attn
        grad = dot_nt(attn, out_w_ref[...]).astype(BF16)
        grads = stack_heads(jnp.concatenate([jnp.zeros_like(grad), grad], 1), heads, part)
        q = q_ref[...]
        spread = stack_heads(jnp.concatenate([q, jnp.zeros_like(q)], 1), heads, 0)
        kv = jnp.concatenate([have_ref[...], late_ref[...]], 0)
        chance = chance_ref[...]
        slopes = dot_nt(grads, kv)
        slopes = slopes - jnp.sum(slopes * chance, axis=1, keepdims=True)
        tilt = (chance * slopes).astype(BF16)
        grad_q = merge_heads(dot(tilt, kv), heads, 0)[:, :part] * SCALE
        grad_q_ref[...] = grad_q.astype(BF16)
        grad_kv = dot_tn(tilt, spread) * SCALE + dot_tn(chance.astype(BF16), grads)
        keep_ref[...] = grad_kv[: seen // 2]
        send_ref[...] = grad_kv[seen // 2 :]

    grad_normed, grad_mixed, grad_attn, grad_q, keep, send = fused(
        attend_back,
        [
            (full, F32), (full, F32), (full, BF16), (flat, BF16),
            ((seen // 2, 2 * part), F32), ((seen // 2, 2 * part), F32),
        ],
        grad_second, half_sum, other_sum, normal1, inverse1, gains, w_out, chance,
        queries, have, late,
        name="cross_attend_back",
    )
    other = net.hop(send, 0)
    for b in up[::-1]:
        size = keep.shape[0] // 2
        total = keep + other
        keep, other = total[:size], net.hop(total[size:], b)

    def project_back(grad_q_ref, keep_ref, other_ref, cols_ref, grad_ref, back_ref):
        grad_kv = (keep_ref[...] + other_ref[...]).astype(BF16)
        grad_q = grad_q_ref[...]
        grad_ref[...] = jnp.concatenate([grad_kv, grad_q], 1)
        back = dot_nt(grad_kv, cols_ref[:, hidden : hidden + 2 * part]) + dot_nt(
            grad_q, cols_ref[:, hidden + 2 * part : hidden + 3 * part]
        )
        back_ref[...] = back.astype(BF16)

    grad_kvq, back = fused(
        project_back,
        [((count, 3 * part), BF16), (full, BF16)],
        grad_q, keep, other, cols,
        name="cross_project_back",
    )
    half_sum = settle(back, net.hop(back, lo))
    grad_in = grad_mixed + settle(half_sum, net.hop(half_sum, hi), F32)
    mine = lambda values: lax.dynamic_slice_in_dim(values, member * own, own, 0)

    def feed_grads(normed_ref, before_ref, active_ref, ffn_ref, up_ref, down_ref):
        up_ref[...] = dot_tn(normed_ref[...], before_ref[...]).astype(BF16)
        down_ref[...] = dot_tn(active_ref[...], ffn_ref[...]).astype(BF16)

    grad_up, grad_down = fused(
        feed_grads,
        [((width, hidden), BF16), (w_down.shape, BF16)],
        normed_low, grad_before, active, grad_ffn,
        name="cross_feed_grads",
    )

    def attend_grads(
        low_ref, grad_ref, context_ref, attn_ref, in_ref, onehot_ref, rest_ref, out_ref
    ):
        table = dot_tn(in_ref[...].astype(BF16), onehot_ref[...])
        rest_ref[...] = jnp.concatenate(
            [
                dot_tn(low_ref[...], grad_ref[...]),
                table,
                jnp.zeros((width, part - table.shape[1]), F32),
            ],
            1,
        ).astype(BF16)
        out_ref[...] = dot_tn(context_ref[...], attn_ref[...]).astype(BF16)

    rest, grad_wout = fused(
        attend_grads,
        [((width, width), BF16), (w_out.shape, BF16)],
        hidden_low, grad_kvq, context, grad_attn, grad_in, onehot,
        name="cross_attend_grads",
    )
    grads = grad_up, rest, grad_wout, grad_down

    def small_sums(
        member_ref, grad_ref, attn_ref, normed_ref, ffn_ref, result_grad_ref, normal1_ref,
        normal2_ref, before_ref, out_ref,
    ):
        member = member_ref[0]
        rows = lax.broadcasted_iota(jnp.int32, full, 0) // own == member
        ours = lambda values: jnp.sum(jnp.where(rows, values, 0.0), axis=0, keepdims=True)
        every = lambda values: jnp.sum(values.astype(F32), axis=0, keepdims=True)

        def spread(values):
            return jnp.concatenate([jnp.where(member == j, values, 0.0) for j in range(TP)], 1)

        sums = every(grad_ref[...])
        grad_normed, grad_result = normed_ref[...], result_grad_ref[...]
        out_ref[...] = jnp.zeros_like(out_ref)
        out_ref[0:1, :] = spread(sums[:, 2 * part :])
        out_ref[1:2, :] = spread(sums[:, part : 2 * part])
        out_ref[2:3, :] = ours(attn_ref[...].astype(F32))
        out_ref[3:4, :] = ours(grad_normed)
        out_ref[4:5, :] = ours(ffn_ref[...].astype(F32))
        out_ref[5:6, :] = ours(grad_result)
        out_ref[6:7, :] = ours(grad_normed * normal1_ref[...])
        out_ref[7:8, :] = ours(grad_result * normal2_ref[...])
        up_sums = every(before_ref[...])
        per = hidden // width
        for j in range(TP):
            for k in range(per):
                at = 8 + j * per + k
                out_ref[at : at + 1, :] = jnp.where(
                    member == j, up_sums[:, k * width : (k + 1) * width], 0.0
                )

    lines = 8 + hidden * TP // width
    small = pl.pallas_call(
        small_sums,
        out_shape=jax.ShapeDtypeStruct((lines, width), F32),
        in_specs=[pl.BlockSpec(memory_space=pltpu.SMEM)]
        + [pl.BlockSpec(memory_space=pltpu.VMEM)] * 8,
        name="cross_small_sums",
        compiler_params=pltpu.CompilerParams(vmem_limit_bytes=8 << 20),
        cost_estimate=work(2),
    )(member.reshape(1), grad_kvq, grad_attn, grad_normed, grad_ffn, grad_all, normal1, normal2,
      grad_before)
    return mine(result), mine(grad_in), grads, small


def places_of(ids, slots, seq_ids, table_rows):
    all_slots = jnp.arange(seq_ids.shape[0], dtype=jnp.int32)
    earlier = (seq_ids[None, :] == ids[:, None]) & (all_slots[None, :] < slots[:, None])
    places = jnp.sum(earlier.astype(jnp.int32), axis=1)
    rows = jnp.arange(table_rows, dtype=jnp.int32)
    return (places[:, None] == rows[None, :]).astype(BF16)


def shards(
    count, tokens, seq_ids, w_qkv, w_out, w_up, w_down, biases, up_bias, norm_gains, pos_table, cotangent
):
    net = Net(count)
    rows_here, width = tokens.shape
    segs_here = rows_here // SEG
    share, hidden = biases.shape[2], up_bias.shape[1]
    half = width // 2
    lo, hi = net.bits - 2, net.bits - 1
    planes = count // TP

    order = list(range(1, net.bits - 2)) + [0]
    masks = [0]
    for b in order:
        masks = masks + [m | 1 << b for m in masks]
    slots = jnp.arange(seq_ids.shape[0], dtype=jnp.int32).reshape(TP, planes, segs_here)
    key_slots = jnp.take(slots, (net.me & (planes - 1)) ^ jnp.array(masks, jnp.int32), axis=1)
    row_slots = key_slots[:, 0].reshape(-1)
    key_ids = seq_ids[key_slots.transpose(1, 0, 2).reshape(-1)]
    row_ids = seq_ids[row_slots]
    allowed = (row_ids[:, None] == key_ids[None, :]).astype(F32)
    onehot = places_of(row_ids, row_slots, seq_ids, pos_table.shape[0])

    grad_rows = cotangent.reshape(segs_here, SEG, width)
    table = pos_table.T
    small = jnp.concatenate(
        [v.reshape(-1, share) for v in (biases, norm_gains, up_bias)], 0
    )
    if share % 8:
        first_packed = packed = None
    else:
        first_packed = pack_first(w_qkv, table, biases, norm_gains, up_bias)
        packed = stack_columns(width, w_out[0], w_up[0])
    shares_down = w_down[0]
    cross_shares = (w_qkv[1], w_out[1], w_up[1], w_down[1])

    get_qkv = Task(gather_first(net, w_qkv[0], table, small, first_packed))
    window([], [get_qkv])
    shares_down, *cross_shares = window([shares_down, *cross_shares], [get_qkv])
    packed = tie(packed, *cross_shares)[0] if packed is not None else None
    get_middle = Task(gather_middle(net, w_out[0], w_up[0], packed))
    window([], [get_qkv])
    (shares_down,) = window([shares_down], [get_qkv, get_middle])
    tokens, *cross_shares = window([tokens, *cross_shares], [get_qkv])
    *weights_qkv, table, small = get_qkv.get()
    small = small.astype(F32)
    narrow = small[:, :16].transpose(1, 0, 2).reshape(16, width)
    long = small[:, 16:].reshape(count, 2, -1).transpose(1, 0, 2).reshape(2, 1, -1)
    biases0, gains0, up_bias0 = narrow[:6], narrow[12:14], long[0, 0]
    params1 = narrow[6:12], narrow[14:], long[1]

    allowed, onehot, biases0, gains0, up_bias0, *params1 = tie(
        allowed, onehot, biases0, gains0, up_bias0, *params1
    )

    def project(n):
        shift = jnp.concatenate(
            [
                biases0[0, n * half : (n + 1) * half],
                jnp.zeros((half,), F32),
                biases0[1, n * half : (n + 1) * half],
            ]
        )
        return (dot(tokens, weights_qkv[n]) + shift).astype(BF16)

    left = project(0)
    left, shares_down, *cross_shares = window([left, shares_down, *cross_shares], [get_middle])
    get_down = Task(gather_down(net, shares_down))
    get_cross = Task(cross_weight_steps(net, *cross_shares))
    context = segment_attend(left, 0)
    context, tokens = window([context, tokens], [get_middle, get_down, get_cross])
    right = project(1)
    (right,) = window([right], [get_down, get_cross])
    context = segment_attend(right, 1, context)
    qkv = [left, right]
    (context,) = window([context], [get_middle, get_down])
    (context,) = window([context], [get_middle])
    w_out0, w_up0 = get_middle.get()
    normed, normal1, inverse1, normed_low, active, slope = feed_up(
        tokens, context, w_out0, w_up0, biases0, gains0, up_bias0[None, :]
    )
    active, slope, normed = window([active, slope, normed], [get_down, get_cross])
    (normed,) = window([normed], [get_down])
    w_down0 = get_down.get()
    result0, firsts, normal2, inverse2 = feed_down(normed, active, w_down0, biases0, gains0)
    (firsts,) = window([firsts], [get_cross])
    weights1 = get_cross.get()
    firsts = firsts.reshape(segs_here, width)

    own_onehot = lax.dynamic_slice_in_dim(onehot, (net.me >> lo) * segs_here, segs_here, 0)
    cross_in = firsts + dot_nt(own_onehot, table)
    result1, grad_cross, grads1, small1 = cross_encoder(
        net,
        cross_in,
        grad_rows[:, 0, :].astype(F32),
        weights1,
        params1,
        allowed,
        onehot,
    )
    layer_out = put_firsts(result0, result1)

    ways, back_ways = link_orders(net)
    grad_ffn, grad_before, grad_mixed, grad_attn, grad_context, small0 = tail_backward(
        cotangent, grad_cross, (normal1, inverse1, slope, normal2, inverse2), w_out0, w_up0, w_down0,
        gains0,
    )
    grad_ffn, grad_before, grad_attn, grad_context, *grads1 = tie(
        grad_ffn, grad_before, grad_attn, grad_context, *grads1
    )
    red_cross = Task(cross_grad_steps(net, *grads1, ways))
    grad_down = dot_tn(active, grad_ffn).astype(BF16)
    grad_down, grad_before, grad_attn, grad_context = window(
        [grad_down, grad_before, grad_attn, grad_context], [red_cross]
    )
    red_down = Task(reduce_steps(net, [grad_down], back_ways + [lo, hi]))
    grad_up = dot_tn(normed_low, grad_before).astype(BF16)
    grad_out = dot_tn(context, grad_attn).astype(BF16)
    grad_up, grad_out, grad_context = window([grad_up, grad_out, grad_context], [red_down])
    red_up = Task(reduce_steps(net, [grad_up], ways + [lo, hi]))
    back_left, sums_left = segment_attend_back(qkv[0], grad_context, 0)
    grad_left = dot_tn(tokens, back_left).astype(BF16)
    back_left, grad_left, grad_context = window(
        [back_left, grad_left, grad_context], [red_cross, red_up]
    )
    back_right, sums_right = segment_attend_back(qkv[1], grad_context, 1)
    grad_right = dot_tn(tokens, back_right).astype(BF16)
    grad_right, grad_left, grad_out, back_right, sums_left, sums_right = window(
        [grad_right, grad_left, grad_out, back_right, sums_left, sums_right], [red_down, red_up]
    )
    sums = [jnp.sum(v, axis=(0, 1)).reshape(3, half) for v in (sums_left, sums_right)]
    ends = [jnp.concatenate([v[n] for v in sums]) for n in (0, 2)]
    small0 = jnp.concatenate([jnp.stack(ends), small0[2:]])
    small = jnp.stack([small0, small1])
    narrow = small[:, :8].reshape(16, width).T
    long = small[:, 8:].reshape(2, count, -1, share).transpose(1, 3, 0, 2).reshape(width, -1)
    small = jnp.concatenate([narrow, long], 1)
    small = jnp.pad(small, ((0, 0), (0, 128 - small.shape[1]))).astype(BF16)
    red_qkv = Task(
        reduce_steps(
            net, [grad_left, grad_right, grad_out, small], list(zip(back_ways, ways)) + [lo, hi]
        )
    )
    grad_tokens = grad_mixed + dot_nt(back_left, weights_qkv[0]) + dot_nt(back_right, weights_qkv[1])
    (grad_tokens,) = window(
        [grad_tokens.astype(BF16)], [red_qkv, red_down, red_up, red_cross]
    )
    for _ in range(net.bits):
        window([], [red_qkv, red_down, red_up, red_cross])

    grad_left0, grad_right0, grad_out0, small = red_qkv.get()
    narrow = small[:, :16].T.reshape(2, 8, share)
    long = small[:, 16 : 16 + 2 * (hidden // share)]
    long = long.reshape(share, 2, -1).transpose(1, 2, 0).reshape(2, -1)
    (grad_down0,) = red_down.get()
    (grad_up0,) = red_up.get()
    halves = [r.reshape(-1, 3, half) for r in (grad_left0, grad_right0)]
    grad_qkv0 = jnp.stack(halves, 2).reshape(share, -1)
    shares1 = red_cross.get()
    return (
        layer_out,
        grad_tokens,
        jnp.stack([grad_qkv0, shares1[0]]),
        jnp.stack([grad_out0, shares1[1]]),
        jnp.stack([grad_up0, shares1[2]]),
        jnp.stack([grad_down0, shares1[3]]),
        narrow[:, :6],
        long,
        narrow[:, 6:],
        shares1[4][:, : pos_table.shape[0]].T,
    )


def solution(mesh):
    count = mesh.shape["ctx"] * mesh.shape["wa"]
    in_specs = (
        P(AXES, None),
        P(),
        P(None, AXES, None),
        P(None, AXES, None),
        P(None, AXES, None),
        P(None, AXES, None),
        P(None, None, AXES),
        P(None, AXES),
        P(None, None, AXES),
        P(None, AXES),
        P(AXES, None),
    )
    out_specs = (
        P(AXES, None),
        P(AXES, None),
        P(None, AXES, None),
        P(None, AXES, None),
        P(None, AXES, None),
        P(None, AXES, None),
        P(None, None, AXES),
        P(None, AXES),
        P(None, None, AXES),
        P(None, AXES),
    )
    return jax.shard_map(
        partial(shards, count), mesh=mesh, in_specs=in_specs, out_specs=out_specs, check_vma=False
    )
```

```python
from functools import partial

import jax
import jax.numpy as jnp
from jax import lax
from jax.experimental import pallas as pl
from jax.experimental.pallas import tpu as pltpu
from jax.sharding import PartitionSpec as P

HDIM = 64
SEG = 128
TP = 4
AXES = ("ctx", "wa")
F32 = jnp.float32
BF16 = jnp.bfloat16
SCALE = HDIM ** (-0.5)


def work(microseconds):
    return pl.CostEstimate(flops=microseconds * 10**9, transcendentals=0, bytes_accessed=0)


def dot(a, b, dims=((1,), (0,))):
    return lax.dot_general(a, b, (dims, ((), ())), preferred_element_type=F32)


def normalize(values):
    center = values - jnp.mean(values, axis=-1, keepdims=True)
    spread = jnp.mean(center * center, axis=-1, keepdims=True)
    inverse = lax.rsqrt(spread + 1e-05)
    return center * inverse, inverse


def normalize_back(grad, normal, inverse):
    return inverse * (
        grad
        - jnp.mean(grad, axis=-1, keepdims=True)
        - normal * jnp.mean(grad * normal, axis=-1, keepdims=True)
    )


def gelu_pair(values):
    phi = 0.5 * (1.0 + lax.erf(values * 0.7071067811865476))
    density = jnp.exp(-0.5 * values * values) * 0.3989422804014327
    return values * phi, phi + values * density


class Net:
    def __init__(self, count):
        self.count = count
        self.bits = count.bit_length() - 1
        self.me = lax.axis_index(AXES)

    def bit(self, b):
        return (self.me >> b) & 1

    def hop(self, value, b):
        return lax.ppermute(value, AXES, [(i, i ^ (1 << b)) for i in range(self.count)])

    def grow(self, value, b, axis):
        other = self.hop(value, b)
        return jnp.where(
            self.bit(b) == 0,
            jnp.concatenate([value, other], axis),
            jnp.concatenate([other, value], axis),
        )

    def pick(self, value, which, axis):
        return lax.dynamic_slice_in_dim(value, which, 1, axis)


def tie(*values):
    return lax.optimization_barrier(values)


def place_blocks(net, parts, blocks, shapes):
    arrays = [part[0] for part in parts]

    lists = [list(masks) for _, masks, _ in parts]
    table = net.me ^ jnp.array(lists, jnp.int32)

    def body(owner_ref, *refs):
        sources = refs[: len(parts)]
        targets = refs[len(parts) : len(parts) + len(shapes)]
        sem = refs[-1]
        for n, (source, (array, masks, half)) in enumerate(zip(sources, parts)):

            def move(j, carry, n=n, source=source, half=half):
                owner = owner_ref[n, j]
                for row, rows, lane, lanes, which, to_row, to_lane in blocks(half):
                    which, lead = which if isinstance(which, tuple) else (which, ())
                    to = lead + (owner, pl.ds(to_row, rows), pl.ds(to_lane, lanes))
                    pltpu.make_async_copy(
                        source.at[j, pl.ds(row, rows), pl.ds(lane, lanes)], targets[which].at[to], sem
                    ).start()
                return carry

            lax.fori_loop(0, len(masks), move, 0)
        for target in targets:
            pltpu.make_async_copy(target, target, sem).wait()

    return pl.pallas_call(
        body,
        out_shape=[jax.ShapeDtypeStruct(shape, BF16) for shape in shapes],
        in_specs=[pl.BlockSpec(memory_space=pltpu.SMEM)]
        + [pl.BlockSpec(memory_space=pl.ANY)] * len(parts),
        out_specs=[pl.BlockSpec(memory_space=pltpu.VMEM)] * len(shapes),
        scratch_shapes=[pltpu.SemaphoreType.DMA],
        name="place_blocks",
        cost_estimate=work(3),
        compiler_params=pltpu.CompilerParams(vmem_limit_bytes=16 << 20),
    )(table, *arrays)


def link_orders(net):
    mid = list(range(1, net.bits - 2))
    return mid, mid[::-1]


class Task:
    def __init__(self, steps):
        self.steps, self.flight, self.result = steps, None, None
        self.advance(None)

    def advance(self, arrived):
        try:
            self.flight = list(self.steps.send(arrived))
        except StopIteration as stop:
            self.flight, self.result = [], stop.value

    def get(self):
        while self.flight:
            self.advance(self.flight)
        return self.result


def window(values, tasks):
    done = tie(*values, *[f for task in tasks for f in task.flight])
    at = len(values)
    for task in tasks:
        size = len(task.flight)
        if size:
            task.advance(list(done[at : at + size]))
        at += size
    return done[: len(values)]


def gather_steps(net, have, high, early=False):
    have, masks = have[None], [0]
    for b in high:
        (other,) = yield [net.hop(have, b)]
        have = jnp.concatenate([have, other], 0)
        masks = masks + [m ^ (1 << b) for m in masks]
    cut = have.shape[2] // 2
    halves = [have[:, :, :cut], have[:, :, cut:]]
    orders = link_orders(net)
    lists = [masks, masks]
    for step in range(len(orders[0]) - 1):
        others = yield [net.hop(h, o[step]) for h, o in zip(halves, orders)]
        halves = [jnp.concatenate([h, o], 0) for h, o in zip(halves, others)]
        lists = [l + [m ^ (1 << o[step]) for m in l] for l, o in zip(lists, orders)]
    last = [o[-1] for o in orders]
    if early:
        arrived = yield [net.hop(h, b) for h, b in zip(halves, last)] + [
            net.hop(h, 0) for h in halves
        ]
        late, early_core = arrived[:2], arrived[2:]
        late_core = yield [net.hop(h, 0) for h in late]
    else:
        late = yield [net.hop(h, b) for h, b in zip(halves, last)]
        arrived = yield [net.hop(h, 0) for h in halves + late]
        early_core, late_core = arrived[:2], arrived[2:]
    core = [c for pair in zip(early_core, late_core) for c in pair]
    parts = []
    for n in (0, 1):
        late_list = [m ^ (1 << last[n]) for m in lists[n]]
        parts.append((halves[n], lists[n], n))
        parts.append((core[2 * n], [m ^ 1 for m in lists[n]], n))
        parts.append((late[n], late_list, n))
        parts.append((core[2 * n + 1], [m ^ 1 for m in late_list], n))
    return parts


def stack_columns(width, *shares):
    pieces = []
    for share in shares:
        for at in range(0, share.shape[1], width):
            pieces.append(share[:, at : at + width])
    return jnp.concatenate(pieces, 0)


def flat_rows(out):
    return out.reshape(-1, out.shape[2])


def pack_first(w_qkv, table, biases, gains, up_bias):
    rows, width = w_qkv.shape[1], w_qkv.shape[2] // 3
    share = biases.shape[2]
    groups = up_bias.shape[1] // share

    def body(qkv_ref, table_ref, bias_ref, gain_ref, up_ref, out_ref):
        for i in range(3):
            out_ref[i * rows : (i + 1) * rows, :] = qkv_ref[0, :, i * width : (i + 1) * width]
        up = up_ref[...].astype(F32)
        small = jnp.concatenate(
            [bias_ref[e].astype(F32) for e in (0, 1)]
            + [gain_ref[e].astype(F32) for e in (0, 1)]
            + [up[e : e + 1, k * share : (k + 1) * share] for e in (0, 1) for k in range(groups)],
            0,
        )
        small = jnp.concatenate([small, jnp.zeros((24, 128 - share), F32)], 1)
        table = table_ref[...].astype(F32)
        out_ref[3 * rows :, :] = jnp.concatenate(
            [v[i : i + 8] for v in (table, small) for i in (0, 8, 16)], 1
        ).astype(BF16)

    return pl.pallas_call(
        body, out_shape=jax.ShapeDtypeStruct((3 * rows + 8, width), BF16), name="pack_first",
        cost_estimate=work(2),
    )(w_qkv, table, biases, gains, up_bias)


def gather_first(net, w_qkv, table, small, packed):
    rows, width = w_qkv.shape[0], w_qkv.shape[1] // 3
    half = width // 2
    if packed is None:
        cube = lax.all_gather(w_qkv, AXES, axis=0, tiled=True).reshape(width, 3, 2, half)
        return (
            cube[:, :, 0].reshape(width, -1),
            cube[:, :, 1].reshape(width, -1),
            lax.all_gather(table, AXES, axis=0, tiled=True),
            lax.all_gather(small, AXES, axis=0),
        )
    parts = yield from gather_steps(net, packed, (net.bits - 1, net.bits - 2), True)
    left, right, table, small = place_blocks(
        net,
        parts,
        lambda h: [(i * rows, rows, 0, half, h, 0, i * half) for i in range(3)]
        + [(3 * rows, 8, i * 128, 128, 2 + h, i * 8, 0) for i in range(3)],
        [(net.count, rows, 3 * half)] * 2 + [(net.count, 24, 128)] * 2,
    )
    return flat_rows(left), flat_rows(right), flat_rows(table), small[:, :, :rows]


def gather_middle(net, w_out, w_up, packed):
    rows, width = w_out.shape
    if packed is None:
        return [lax.all_gather(w, AXES, axis=0, tiled=True) for w in (w_out, w_up)]
    parts = yield from gather_steps(net, packed, (net.bits - 1, net.bits - 2))
    columns = w_up.shape[1] // width
    half = width // 2
    out, up = place_blocks(
        net,
        parts,
        lambda h: [(0, rows, 0, half, 0, 0, h * half)]
        + [((i + 1) * rows, rows, 0, half, 1, 0, i * width + h * half) for i in range(columns)],
        [(net.count,) + w.shape for w in (w_out, w_up)],
    )
    return flat_rows(out), flat_rows(up)


def gather_down(net, w_down):
    rows, width = w_down.shape
    if rows % 32:
        return lax.all_gather(w_down, AXES, axis=0, tiled=True)
    parts = yield from gather_steps(net, w_down, (net.bits - 1, net.bits - 2))
    half = width // 2
    (down,) = place_blocks(
        net, parts, lambda h: [(0, rows, 0, half, 0, 0, h * half)], [(net.count, rows, width)]
    )
    return flat_rows(down)


def settle(keep, other, dtype=BF16):
    return (keep.astype(F32) + other.astype(F32)).astype(dtype)


def reduce_steps(net, grads, order):
    axis = lambda b: net.bits - 1 - b
    cubes = [g.reshape((2,) * net.bits + (g.shape[0] // net.count, g.shape[1])) for g in grads]
    widths = [g.shape[1] for g in grads]
    join = lambda values: jnp.concatenate(values, -1) if len(values) > 1 else values[0]
    arrived = yield [net.hop(net.pick(c, 1 - net.bit(0), axis(0)), 0) for c in cubes]
    pairs = [(net.pick(c, net.bit(0), axis(0)), f) for c, f in zip(cubes, arrived)]
    for b in order:
        if isinstance(b, tuple):
            if len(pairs) != 2:
                keep, other = join([k for k, _ in pairs]), join([f for _, f in pairs])
                cut = keep.shape[-1] // 256 * 128
                pairs = [(keep[..., :cut], other[..., :cut]), (keep[..., cut:], other[..., cut:])]
            sides = lambda turn: [
                settle(net.pick(k, t, axis(x)), net.pick(f, t, axis(x)))
                for (k, f), x in zip(pairs, b)
                for t in [net.bit(x) ^ turn]
            ]
            sent, kept = sides(1), sides(0)
            arrived = yield [net.hop(v, x) for v, x in zip(sent, b)]
            pairs = list(zip(kept, arrived))
            continue
        side = lambda which: join(
            [settle(net.pick(k, which, axis(b)), net.pick(f, which, axis(b))) for k, f in pairs]
        )
        sent, kept = side(1 - net.bit(b)), side(net.bit(b))
        (other,) = yield [net.hop(sent, b)]
        pairs = [(kept, other)]
    whole = settle(*pairs[0], F32)
    whole = whole.reshape(whole.shape[-2:])
    out, at = [], 0
    for w in widths:
        out.append(whole[:, at : at + w])
        at += w
    return out


def ordered(net, value, other, b, axis):
    return jnp.where(
        net.bit(b) == 0,
        jnp.concatenate([value, other], axis),
        jnp.concatenate([other, value], axis),
    )


def trade_pair(net, value, b, axis):
    return net.hop(net.pick(value, 1 - net.bit(b), axis), b), net.pick(value, net.bit(b), axis)


def dot_nt(a, b):
    return dot(a, b, ((1,), (1,)))


def dot_tn(a, b):
    return dot(a, b, ((0,), (0,)))


def pick_lanes(mask, values):
    return jnp.where(mask, values, jnp.zeros_like(values))


def head_masks(rows):
    lane = lax.broadcasted_iota(jnp.int32, (rows, 2 * HDIM), 1)
    return lane < HDIM, lane >= HDIM


def chance_of(keys, queries):
    scores = dot_nt(keys, queries) * SCALE
    raised = jnp.exp(scores - jnp.max(scores, axis=0, keepdims=True))
    return raised * (1.0 / jnp.sum(raised, axis=0, keepdims=True))


def attend_forward_body(heads, qkv_ref, out_ref):
    width = heads * HDIM
    for at in range(0, width, 2 * HDIM):
        queries, keys, values = [qkv_ref[:, n * width + at : n * width + at + 128] for n in range(3)]
        total = 0.0
        for mask in head_masks(SEG):
            chance = chance_of(pick_lanes(mask, keys), queries).astype(BF16)
            total = total + dot_tn(pick_lanes(mask, values), chance)
        out_ref[:, at : at + 128] = total.T.astype(BF16)


def attend_backward_body(heads, qkv_ref, grad_ref, out_ref, sums_ref):
    width = heads * HDIM
    for at in range(0, width, 2 * HDIM):
        queries, keys, values = [qkv_ref[:, n * width + at : n * width + at + 128] for n in range(3)]
        grad = grad_ref[:, at : at + 128]
        totals = [0.0, 0.0, 0.0]
        for mask in head_masks(SEG):
            own_keys = pick_lanes(mask, keys)
            chance = chance_of(own_keys, queries)
            slope = dot_nt(pick_lanes(mask, values), grad)
            slope = slope - jnp.sum(slope * chance, axis=0, keepdims=True)
            tilt = (chance * slope).astype(BF16)
            totals[0] = totals[0] + dot_tn(tilt, own_keys)
            totals[1] = totals[1] + dot(tilt, pick_lanes(mask, queries))
            totals[2] = totals[2] + dot(chance.astype(BF16), pick_lanes(mask, grad))
        for n, (total, scale) in enumerate(zip(totals, (SCALE, SCALE, 1.0))):
            low = (total * scale).astype(BF16)
            out_ref[:, n * width + at : n * width + at + 128] = low
            sums_ref[0, :, n * width + at : n * width + at + 128] = jnp.sum(
                low.astype(F32), axis=0, keepdims=True
            )


def segment_attend(qkv, half, context=None):
    rows, width = qkv.shape[0], qkv.shape[1] // 3

    def body(*refs):
        attend_forward_body(width // HDIM, refs[0], refs[-1])

    return pl.pallas_call(
        body,
        out_shape=jax.ShapeDtypeStruct((rows, 2 * width), BF16),
        grid=(rows // SEG,),
        in_specs=[pl.BlockSpec((SEG, 3 * width), lambda i: (i, 0))]
        + [pl.BlockSpec(memory_space=pl.ANY)] * half,
        out_specs=pl.BlockSpec((SEG, width), lambda i: (i, half)),
        input_output_aliases={1: 0} if half else {},
        name="segment_attend",
        compiler_params=pltpu.CompilerParams(vmem_limit_bytes=12 << 20),
        cost_estimate=work(10),
    )(*([qkv, context] if half else [qkv]))


def segment_attend_back(qkv, grad, half):
    rows, width = qkv.shape[0], qkv.shape[1] // 3
    return pl.pallas_call(
        partial(attend_backward_body, width // HDIM),
        out_shape=(
            jax.ShapeDtypeStruct((rows, 3 * width), BF16),
            jax.ShapeDtypeStruct((rows // SEG, 1, 3 * width), F32),
        ),
        grid=(rows // SEG,),
        in_specs=[
            pl.BlockSpec((SEG, 3 * width), lambda i: (i, 0)),
            pl.BlockSpec((SEG, width), lambda i: (i, half)),
        ],
        out_specs=(
            pl.BlockSpec((SEG, 3 * width), lambda i: (i, 0)),
            pl.BlockSpec((1, 1, 3 * width), lambda i: (i, 0, 0)),
        ),
        name="segment_attend_back",
        compiler_params=pltpu.CompilerParams(vmem_limit_bytes=16 << 20),
        cost_estimate=work(12),
    )(qkv, grad)


BLOCK = 256


def row_block(width):
    return pl.BlockSpec((BLOCK, width), lambda i: (i, 0))


def whole(shape):
    return pl.BlockSpec(
        shape, lambda i: (0,) * len(shape), pipeline_mode=pl.Buffered(1)
    )


def feed_up(tokens, context, w_out, w_up, biases, gains, up_bias):
    rows, width = tokens.shape
    hidden = w_up.shape[1]

    def body(
        tokens_ref, context_ref, out_ref, up_ref, bias_ref, gain_ref, up_bias_ref,
        normed_ref, normal_ref, inverse_ref, low_ref, active_ref, slope_ref,
    ):
        mixed = tokens_ref[...].astype(F32) + dot(context_ref[...], out_ref[...]) + bias_ref[2:3, :]
        normal, inverse = normalize(mixed)
        normal_ref[...] = normal.astype(BF16)
        inverse_ref[...] = inverse
        normed = normal * gain_ref[0:1, :] + bias_ref[3:4, :]
        normed_ref[...] = normed
        low = normed.astype(BF16)
        low_ref[...] = low
        for at in range(0, hidden, width):
            part = slice(at, at + width)
            active, slope = gelu_pair(dot(low, up_ref[:, part]) + up_bias_ref[:, part])
            active_ref[:, part] = active.astype(BF16)
            slope_ref[:, part] = slope.astype(BF16)

    outs = [(width, F32), (width, BF16), (1, F32), (width, BF16), (hidden, BF16), (hidden, BF16)]
    return pl.pallas_call(
        body,
        grid=(rows // BLOCK,),
        out_shape=[jax.ShapeDtypeStruct((rows, w), t) for w, t in outs],
        in_specs=[row_block(width)] * 2
        + [whole(v.shape) for v in (w_out, w_up, biases, gains, up_bias)],
        out_specs=[row_block(w) for w, _ in outs],
        name="feed_up",
        compiler_params=pltpu.CompilerParams(vmem_limit_bytes=36 << 20),
        cost_estimate=work(18),
    )(tokens, context, w_out, w_up, biases, gains, up_bias)


def feed_down(normed, active, w_down, biases, gains):
    rows, width = normed.shape
    per = BLOCK // SEG

    def body(
        normed_ref, active_ref, down_ref, bias_ref, gain_ref,
        result_ref, first_ref, normal_ref, inverse_ref,
    ):
        second = normed_ref[...] + dot(active_ref[...], down_ref[...]) + bias_ref[4:5, :]
        normal, inverse = normalize(second)
        normal_ref[...] = normal.astype(BF16)
        inverse_ref[...] = inverse
        result = normal * gain_ref[1:2, :] + bias_ref[5:6, :]
        result_ref[...] = result.astype(BF16)
        for k in range(per):
            first_ref[0, k : k + 1, :] = result[k * SEG : k * SEG + 1]

    return pl.pallas_call(
        body,
        grid=(rows // BLOCK,),
        out_shape=[
            jax.ShapeDtypeStruct((rows, width), BF16),
            jax.ShapeDtypeStruct((rows // BLOCK, per, width), F32),
            jax.ShapeDtypeStruct((rows, width), BF16),
            jax.ShapeDtypeStruct((rows, 1), F32),
        ],
        in_specs=[row_block(width), row_block(active.shape[1])]
        + [whole(v.shape) for v in (w_down, biases, gains)],
        out_specs=[
            row_block(width), pl.BlockSpec((1, per, width), lambda i: (i, 0, 0)), row_block(width),
            row_block(1),
        ],
        name="feed_down",
        compiler_params=pltpu.CompilerParams(vmem_limit_bytes=28 << 20),
        cost_estimate=work(11),
    )(normed, active, w_down, biases, gains)


def tail_backward(cotangent, firsts, kept, w_out, w_up, w_down, gains):
    normal1, inverse1, slope, normal2, inverse2 = kept
    rows, width = cotangent.shape
    hidden = w_up.shape[1]
    per = BLOCK // SEG
    lines = 8 + hidden // width

    def body(
        cotangent_ref, first_ref, normal1_ref, inverse1_ref, slope_ref, normal2_ref, inverse2_ref,
        out_ref, up_ref, down_ref, gain_ref,
        ffn_ref, before_ref, mixed_ref, attn_ref, context_ref, sums_ref,
    ):
        grad = cotangent_ref[...].astype(F32)
        row = lax.broadcasted_iota(jnp.int32, (BLOCK, 1), 0)
        for k in range(per):
            grad = jnp.where(row == k * SEG, first_ref[0, k : k + 1, :], grad)
        normal2 = normal2_ref[...].astype(F32)
        grad_second = normalize_back(grad * gain_ref[1:2, :], normal2, inverse2_ref[...])
        ffn = grad_second.astype(BF16)
        ffn_ref[...] = ffn
        grad_normed = grad_second
        up_sums = []
        for at in range(0, hidden, width):
            part = slice(at, at + width)
            before = dot_nt(ffn, down_ref[part, :]) * slope_ref[:, part].astype(F32)
            before = before.astype(BF16)
            before_ref[:, part] = before
            up_sums.append(before)
            grad_normed = grad_normed + dot_nt(before, up_ref[:, part])
        normal1 = normal1_ref[...].astype(F32)
        grad_mixed = normalize_back(grad_normed * gain_ref[0:1, :], normal1, inverse1_ref[...])
        mixed_ref[...] = grad_mixed
        attn = grad_mixed.astype(BF16)
        attn_ref[...] = attn
        context_ref[...] = dot_nt(attn, out_ref[...]).astype(BF16)

        @pl.when(pl.program_id(0) == 0)
        def _():
            sums_ref[...] = jnp.zeros_like(sums_ref)

        values = [attn, grad_normed, ffn, grad, grad_normed * normal1, grad * normal2] + up_sums
        for n, value in enumerate(values):
            sums_ref[n + 2 : n + 3, :] += jnp.sum(value.astype(F32), axis=0, keepdims=True)

    return pl.pallas_call(
        body,
        grid=(rows // BLOCK,),
        out_shape=[
            jax.ShapeDtypeStruct((rows, width), BF16),
            jax.ShapeDtypeStruct((rows, hidden), BF16),
            jax.ShapeDtypeStruct((rows, width), F32),
            jax.ShapeDtypeStruct((rows, width), BF16),
            jax.ShapeDtypeStruct((rows, width), BF16),
            jax.ShapeDtypeStruct((lines, width), F32),
        ],
        in_specs=[
            row_block(width),
            pl.BlockSpec((1, per, width), lambda i: (i, 0, 0)),
            row_block(width), row_block(1), row_block(hidden), row_block(width), row_block(1),
        ]
        + [whole(v.shape) for v in (w_out, w_up, w_down, gains)],
        out_specs=[
            row_block(width), row_block(hidden), row_block(width), row_block(width),
            row_block(width), pl.BlockSpec((lines, width), lambda i: (0, 0)),
        ],
        name="tail_backward",
        compiler_params=pltpu.CompilerParams(vmem_limit_bytes=36 << 20),
        cost_estimate=work(24),
    )(
        cotangent, firsts.reshape(-1, per, width), normal1, inverse1, slope, normal2, inverse2,
        w_out, w_up, w_down, gains,
    )


def put_firsts(values, firsts):
    rows, width = values.shape

    def body(old_ref, first_ref, out_ref):
        row = lax.broadcasted_iota(jnp.int32, (16, 1), 0)
        old = old_ref[...].astype(F32)
        out_ref[...] = jnp.where(row == 0, first_ref[0], old).astype(BF16)

    block = pl.BlockSpec((16, width), lambda i: (i * (SEG // 16), 0))
    return pl.pallas_call(
        body,
        grid=(rows // SEG,),
        out_shape=jax.ShapeDtypeStruct(values.shape, BF16),
        in_specs=[block, pl.BlockSpec((1, 1, width), lambda i: (i, 0, 0))],
        out_specs=block,
        input_output_aliases={0: 0},
        name="put_firsts",
        compiler_params=pltpu.CompilerParams(vmem_limit_bytes=4 << 20),
        cost_estimate=work(4),
    )(values, firsts[:, None, :])


def cross_weight_steps(net, w_qkv, w_out, w_up, w_down):
    rows, width = w_out.shape
    hi, lo = net.bits - 1, net.bits - 2
    part = width // TP
    planes = net.count // TP
    cube = w_qkv.reshape(rows, 3, TP, part)
    ups = w_up.reshape(rows, TP, -1)
    hidden = ups.shape[2]
    assert hidden == width
    kvq = jnp.concatenate([cube[:, 1], cube[:, 2], cube[:, 0], jnp.zeros_like(cube[:, 0])], 2)
    cols = jnp.stack([ups, kvq]).transpose(2, 0, 1, 3).reshape(2, 2, 2 * rows, width)
    for b, axis in ((hi, 0), (lo, 1)):
        flight, keep = trade_pair(net, cols, b, axis)
        (other,) = yield [flight]
        cols = ordered(net, keep, other, b, axis)
    have = jnp.concatenate([cols.reshape(-1, width), w_out, w_down], 0)
    if rows % 8:
        value = have[None]
        for b in range(net.bits - 2):
            (other,) = yield [net.hop(value, b)]
            value = ordered(net, value, other, b, 0)
        cols = value[:, : 8 * rows].reshape(planes, TP, 2, rows, width).transpose(1, 0, 3, 2, 4)
        return (
            cols.reshape(width, 2 * width),
            value[:, 8 * rows : 9 * rows].reshape(part, width),
            value[:, 9 * rows :].reshape(hidden, width),
        )
    parts = yield from gather_steps(net, have, ())
    parts = [(array, [m & (planes - 1) for m in masks], h) for array, masks, h in parts]
    half = width // 2
    plane = Net.__new__(Net)
    plane.me = net.me & (planes - 1)
    outs = place_blocks(
        plane,
        parts,
        lambda h: [
            ((2 * t + k) * rows, rows, 0, half, (0, (t,)), 0, k * width + h * half)
            for t in range(TP)
            for k in (0, 1)
        ]
        + [
            (8 * rows, rows, 0, half, 1, 0, h * half),
            (9 * rows, 4 * rows, 0, half, 2, 0, h * half),
        ],
        [(TP, planes, rows, 2 * width), (planes, rows, width), (planes, 4 * rows, width)],
    )
    return outs[0].reshape(width, 2 * width), flat_rows(outs[1]), flat_rows(outs[2])


def cross_grad_steps(net, ups, rest, grad_out, grad_down, order):
    hi, lo = net.bits - 1, net.bits - 2
    plane = net.bits - 2
    planes = net.count // TP
    width = ups.shape[0]
    rows = width // net.count
    part = width // TP
    pair = jnp.stack([ups.reshape(TP, planes, rows, width), rest.reshape(TP, planes, rows, width)])
    whole = jnp.concatenate(
        [
            pair.transpose(2, 1, 0, 3, 4).reshape(planes, 8 * rows, width),
            grad_out.reshape(planes, rows, width),
            grad_down.reshape(planes, 4 * rows, width),
        ],
        1,
    ).reshape((2,) * plane + (13 * rows, width))
    axis = lambda b: plane - 1 - b
    (other,) = yield [net.hop(net.pick(whole, 1 - net.bit(0), axis(0)), 0)]
    kept = net.pick(whole, net.bit(0), axis(0))
    for b in order:
        side = lambda which: settle(net.pick(kept, which, axis(b)), net.pick(other, which, axis(b)))
        sent, kept = side(1 - net.bit(b)), side(net.bit(b))
        (other,) = yield [net.hop(sent, b)]
    whole = settle(kept, other).reshape(13 * rows, width)
    cols = whole[: 8 * rows].reshape(2, 2, 2 * rows, width)
    for b, at in ((hi, 0), (lo, 1)):
        flight, keep = trade_pair(net, cols, b, at)
        (back,) = yield [flight]
        cols = ordered(net, keep, back, b, at)
    whole, cols = yield [whole, cols]
    cols = cols.reshape(TP, 2, rows, width).transpose(1, 2, 0, 3).astype(F32)
    deep = whole[8 * rows :].astype(F32)
    pieces = [cols[1, :, :, n * part : (n + 1) * part].reshape(rows, width) for n in (2, 0, 1)]
    return (
        jnp.concatenate(pieces, 1),
        deep[:rows],
        cols[0].reshape(rows, -1),
        deep[rows:],
        cols[1, :, 0, 3 * part :],
    )


def lanes_between(values, first, last):
    lane = lax.broadcasted_iota(jnp.int32, values.shape, values.ndim - 1)
    return jnp.where((lane >= first) & (lane < last), values, jnp.zeros_like(values))


def stack_heads(values, heads, first):
    return jnp.concatenate(
        [lanes_between(values, first + h * HDIM, first + (h + 1) * HDIM) for h in range(heads)], 0
    )


def merge_heads(values, heads, first):
    rows = values.shape[0] // heads
    return sum(
        lanes_between(values[h * rows : (h + 1) * rows], first + h * HDIM, first + (h + 1) * HDIM)
        for h in range(heads)
    )


def fused(body, outs, *args, name):
    return pl.pallas_call(
        body, out_shape=[jax.ShapeDtypeStruct(shape, dtype) for shape, dtype in outs], name=name,
        compiler_params=pltpu.CompilerParams(vmem_limit_bytes=32 << 20),
        cost_estimate=work(3),
    )(*args)


def cross_encoder(net, cross_in, grad_own, weights, params, allowed, onehot):
    cols, w_out, w_down = weights
    own, width = cross_in.shape
    part, hidden = w_out.shape[0], w_down.shape[0]
    plane = net.bits - 2
    hi, lo = net.bits - 1, net.bits - 2
    member = net.me >> lo
    up = list(range(1, plane))
    heads = part // HDIM
    biases, gains, up_bias = params
    row = lambda n: biases[n : n + 1]
    slab = lambda vector, size: lax.dynamic_slice_in_dim(vector, member * size, size, 1)
    bias_kv = jnp.concatenate([jnp.zeros((1, part), F32), slab(row(1), part)], 1)
    bias_q = slab(row(0), part)
    bias_up = slab(up_bias.reshape(1, -1), hidden)
    both = jnp.concatenate([cross_in, grad_own], 0)[None]
    both = net.grow(net.grow(both, lo, 0), hi, 0)
    count = TP * own
    full, wide, flat = (count, width), (count, 2 * part), (count, part)

    def project(x_ref, cols_ref, bias_kv_ref, bias_q_ref, hidden_ref, grad_ref, low_ref, kv_ref, q_ref):
        values = jnp.concatenate([x_ref[t, :own, :] for t in range(TP)], 0)
        hidden_ref[...] = values
        grad_ref[...] = jnp.concatenate([x_ref[t, own:, :] for t in range(TP)], 0)
        low = values.astype(BF16)
        low_ref[...] = low
        kv = dot(low, cols_ref[:, hidden : hidden + 2 * part]) + bias_kv_ref[...]
        kv_ref[...] = kv.astype(BF16)
        q_ref[...] = (dot(low, cols_ref[:, hidden + 2 * part : hidden + 3 * part]) + bias_q_ref[...]).astype(BF16)

    hidden_all, grad_all, hidden_low, kv, queries = fused(
        project,
        [(full, F32), (full, F32), (full, BF16), (wide, BF16), (flat, BF16)],
        both, cols, bias_kv, bias_q,
        name="cross_project",
    )
    have = kv
    for b in up:
        have = jnp.concatenate([have, net.hop(have, b)], 0)
    late = net.hop(have, 0)
    seen = 2 * have.shape[0]

    def attend(q_ref, have_ref, late_ref, allowed_ref, out_w_ref, chance_ref, context_ref, part_ref):
        kv = jnp.concatenate([have_ref[...], late_ref[...]], 0)
        q = q_ref[...]
        spread = stack_heads(jnp.concatenate([q, jnp.zeros_like(q)], 1), heads, 0)
        scores = dot_nt(spread, kv) * SCALE
        scores = jnp.where(jnp.concatenate([allowed_ref[...]] * heads, 0) > 0.5, scores, -1e30)
        raised = jnp.exp(scores - jnp.max(scores, axis=1, keepdims=True))
        chance = raised * (1.0 / jnp.sum(raised, axis=1, keepdims=True))
        chance_ref[...] = chance
        context = merge_heads(dot(chance.astype(BF16), kv), heads, part)[:, part:].astype(BF16)
        context_ref[...] = context
        part_ref[...] = dot(context, out_w_ref[...]).astype(BF16)

    chance, context, partial_sum = fused(
        attend,
        [((heads * count, seen), F32), (flat, BF16), (full, BF16)],
        queries, have, late, allowed, w_out,
        name="cross_attend",
    )
    half_sum = settle(partial_sum, net.hop(partial_sum, lo))
    other_sum = net.hop(half_sum, hi)

    def feed(
        x_ref, a_ref, b_ref, bias_ref, gain_ref, cols_ref, bias_up_ref, down_ref,
        normed_ref, normal_ref, inverse_ref, low_ref, active_ref, slope_ref, part_ref,
    ):
        mixed = x_ref[...] + (a_ref[...].astype(F32) + b_ref[...].astype(F32)) + bias_ref[2:3, :]
        normal, inverse = normalize(mixed)
        normed = normal * gain_ref[0:1, :] + bias_ref[3:4, :]
        low = normed.astype(BF16)
        active, slope = gelu_pair(dot(low, cols_ref[:, :hidden]) + bias_up_ref[...])
        active = active.astype(BF16)
        normed_ref[...] = normed
        normal_ref[...] = normal
        inverse_ref[...] = inverse
        low_ref[...] = low
        active_ref[...] = active
        slope_ref[...] = slope
        part_ref[...] = dot(active, down_ref[...]).astype(BF16)

    normed, normal1, inverse1, normed_low, active, slope, partial_sum = fused(
        feed,
        [
            (full, F32), (full, F32), ((count, 1), F32), (full, BF16),
            ((count, hidden), BF16), ((count, hidden), F32), (full, BF16),
        ],
        hidden_all, half_sum, other_sum, biases, gains, cols, bias_up, w_down,
        name="cross_feed",
    )
    half_sum = settle(partial_sum, net.hop(partial_sum, lo))
    other_sum = net.hop(half_sum, hi)

    def turn(
        normed_ref, a_ref, b_ref, bias_ref, gain_ref, grad_ref, down_ref, slope_ref, cols_ref,
        result_ref, normal_ref, second_ref, ffn_ref, before_ref, part_ref,
    ):
        second = normed_ref[...] + (a_ref[...].astype(F32) + b_ref[...].astype(F32)) + bias_ref[4:5, :]
        normal, inverse = normalize(second)
        gain = gain_ref[1:2, :]
        result_ref[...] = normal * gain + bias_ref[5:6, :]
        normal_ref[...] = normal
        grad_second = normalize_back(grad_ref[...] * gain, normal, inverse)
        second_ref[...] = grad_second
        ffn = grad_second.astype(BF16)
        ffn_ref[...] = ffn
        before = (dot_nt(ffn, down_ref[...]) * slope_ref[...]).astype(BF16)
        before_ref[...] = before
        part_ref[...] = dot_nt(before, cols_ref[:, :hidden]).astype(BF16)

    result, normal2, grad_second, grad_ffn, grad_before, partial_sum = fused(
        turn,
        [
            (full, F32), (full, F32), (full, F32), (full, BF16),
            ((count, hidden), BF16), (full, BF16),
        ],
        normed, half_sum, other_sum, biases, gains, grad_all, w_down, slope, cols,
        name="cross_turn",
    )
    half_sum = settle(partial_sum, net.hop(partial_sum, lo))
    other_sum = net.hop(half_sum, hi)

    def attend_back(
        second_ref, a_ref, b_ref, normal_ref, inverse_ref, gain_ref, out_w_ref, chance_ref,
        q_ref, have_ref, late_ref,
        normed_ref, mixed_ref, attn_ref, grad_q_ref, keep_ref, send_ref,
    ):
        grad_normed = second_ref[...] + (a_ref[...].astype(F32) + b_ref[...].astype(F32))
        normed_ref[...] = grad_normed
        grad_mixed = normalize_back(
            grad_normed * gain_ref[0:1, :], normal_ref[...], inverse_ref[...]
        )
        mixed_ref[...] = grad_mixed
        attn = grad_mixed.astype(BF16)
        attn_ref[...] = attn
        grad = dot_nt(attn, out_w_ref[...]).astype(BF16)
        grads = stack_heads(jnp.concatenate([jnp.zeros_like(grad), grad], 1), heads, part)
        q = q_ref[...]
        spread = stack_heads(jnp.concatenate([q, jnp.zeros_like(q)], 1), heads, 0)
        kv = jnp.concatenate([have_ref[...], late_ref[...]], 0)
        chance = chance_ref[...]
        slopes = dot_nt(grads, kv)
        slopes = slopes - jnp.sum(slopes * chance, axis=1, keepdims=True)
        tilt = (chance * slopes).astype(BF16)
        grad_q = merge_heads(dot(tilt, kv), heads, 0)[:, :part] * SCALE
        grad_q_ref[...] = grad_q.astype(BF16)
        grad_kv = dot_tn(tilt, spread) * SCALE + dot_tn(chance.astype(BF16), grads)
        keep_ref[...] = grad_kv[: seen // 2]
        send_ref[...] = grad_kv[seen // 2 :]

    grad_normed, grad_mixed, grad_attn, grad_q, keep, send = fused(
        attend_back,
        [
            (full, F32), (full, F32), (full, BF16), (flat, BF16),
            ((seen // 2, 2 * part), F32), ((seen // 2, 2 * part), F32),
        ],
        grad_second, half_sum, other_sum, normal1, inverse1, gains, w_out, chance,
        queries, have, late,
        name="cross_attend_back",
    )
    other = net.hop(send, 0)
    for b in up[::-1]:
        size = keep.shape[0] // 2
        total = keep + other
        keep, other = total[:size], net.hop(total[size:], b)

    def project_back(grad_q_ref, keep_ref, other_ref, cols_ref, grad_ref, back_ref):
        grad_kv = (keep_ref[...] + other_ref[...]).astype(BF16)
        grad_q = grad_q_ref[...]
        grad_ref[...] = jnp.concatenate([grad_kv, grad_q], 1)
        back = dot_nt(grad_kv, cols_ref[:, hidden : hidden + 2 * part]) + dot_nt(
            grad_q, cols_ref[:, hidden + 2 * part : hidden + 3 * part]
        )
        back_ref[...] = back.astype(BF16)

    grad_kvq, back = fused(
        project_back,
        [((count, 3 * part), BF16), (full, BF16)],
        grad_q, keep, other, cols,
        name="cross_project_back",
    )
    half_sum = settle(back, net.hop(back, lo))
    grad_in = grad_mixed + settle(half_sum, net.hop(half_sum, hi), F32)
    mine = lambda values: lax.dynamic_slice_in_dim(values, member * own, own, 0)

    def feed_grads(normed_ref, before_ref, active_ref, ffn_ref, up_ref, down_ref):
        up_ref[...] = dot_tn(normed_ref[...], before_ref[...]).astype(BF16)
        down_ref[...] = dot_tn(active_ref[...], ffn_ref[...]).astype(BF16)

    grad_up, grad_down = fused(
        feed_grads,
        [((width, hidden), BF16), (w_down.shape, BF16)],
        normed_low, grad_before, active, grad_ffn,
        name="cross_feed_grads",
    )

    def attend_grads(
        low_ref, grad_ref, context_ref, attn_ref, in_ref, onehot_ref, rest_ref, out_ref
    ):
        table = dot_tn(in_ref[...].astype(BF16), onehot_ref[...])
        rest_ref[...] = jnp.concatenate(
            [
                dot_tn(low_ref[...], grad_ref[...]),
                table,
                jnp.zeros((width, part - table.shape[1]), F32),
            ],
            1,
        ).astype(BF16)
        out_ref[...] = dot_tn(context_ref[...], attn_ref[...]).astype(BF16)

    rest, grad_wout = fused(
        attend_grads,
        [((width, width), BF16), (w_out.shape, BF16)],
        hidden_low, grad_kvq, context, grad_attn, grad_in, onehot,
        name="cross_attend_grads",
    )
    grads = grad_up, rest, grad_wout, grad_down

    def small_sums(
        member_ref, grad_ref, attn_ref, normed_ref, ffn_ref, result_grad_ref, normal1_ref,
        normal2_ref, before_ref, out_ref,
    ):
        member = member_ref[0]
        rows = lax.broadcasted_iota(jnp.int32, full, 0) // own == member
        ours = lambda values: jnp.sum(jnp.where(rows, values, 0.0), axis=0, keepdims=True)
        every = lambda values: jnp.sum(values.astype(F32), axis=0, keepdims=True)

        def spread(values):
            return jnp.concatenate([jnp.where(member == j, values, 0.0) for j in range(TP)], 1)

        sums = every(grad_ref[...])
        grad_normed, grad_result = normed_ref[...], result_grad_ref[...]
        out_ref[...] = jnp.zeros_like(out_ref)
        out_ref[0:1, :] = spread(sums[:, 2 * part :])
        out_ref[1:2, :] = spread(sums[:, part : 2 * part])
        out_ref[2:3, :] = ours(attn_ref[...].astype(F32))
        out_ref[3:4, :] = ours(grad_normed)
        out_ref[4:5, :] = ours(ffn_ref[...].astype(F32))
        out_ref[5:6, :] = ours(grad_result)
        out_ref[6:7, :] = ours(grad_normed * normal1_ref[...])
        out_ref[7:8, :] = ours(grad_result * normal2_ref[...])
        up_sums = every(before_ref[...])
        per = hidden // width
        for j in range(TP):
            for k in range(per):
                at = 8 + j * per + k
                out_ref[at : at + 1, :] = jnp.where(
                    member == j, up_sums[:, k * width : (k + 1) * width], 0.0
                )

    lines = 8 + hidden * TP // width
    small = pl.pallas_call(
        small_sums,
        out_shape=jax.ShapeDtypeStruct((lines, width), F32),
        in_specs=[pl.BlockSpec(memory_space=pltpu.SMEM)]
        + [pl.BlockSpec(memory_space=pltpu.VMEM)] * 8,
        name="cross_small_sums",
        compiler_params=pltpu.CompilerParams(vmem_limit_bytes=8 << 20),
        cost_estimate=work(2),
    )(member.reshape(1), grad_kvq, grad_attn, grad_normed, grad_ffn, grad_all, normal1, normal2,
      grad_before)
    return mine(result), mine(grad_in), grads, small


def places_of(ids, slots, seq_ids, table_rows):
    all_slots = jnp.arange(seq_ids.shape[0], dtype=jnp.int32)
    earlier = (seq_ids[None, :] == ids[:, None]) & (all_slots[None, :] < slots[:, None])
    places = jnp.sum(earlier.astype(jnp.int32), axis=1)
    rows = jnp.arange(table_rows, dtype=jnp.int32)
    return (places[:, None] == rows[None, :]).astype(BF16)


def shards(
    count, tokens, seq_ids, w_qkv, w_out, w_up, w_down, biases, up_bias, norm_gains, pos_table, cotangent
):
    net = Net(count)
    rows_here, width = tokens.shape
    segs_here = rows_here // SEG
    share, hidden = biases.shape[2], up_bias.shape[1]
    half = width // 2
    lo, hi = net.bits - 2, net.bits - 1
    planes = count // TP

    order = list(range(1, net.bits - 2)) + [0]
    masks = [0]
    for b in order:
        masks = masks + [m | 1 << b for m in masks]
    slots = jnp.arange(seq_ids.shape[0], dtype=jnp.int32).reshape(TP, planes, segs_here)
    key_slots = jnp.take(slots, (net.me & (planes - 1)) ^ jnp.array(masks, jnp.int32), axis=1)
    row_slots = key_slots[:, 0].reshape(-1)
    key_ids = seq_ids[key_slots.transpose(1, 0, 2).reshape(-1)]
    row_ids = seq_ids[row_slots]
    allowed = (row_ids[:, None] == key_ids[None, :]).astype(F32)
    onehot = places_of(row_ids, row_slots, seq_ids, pos_table.shape[0])

    grad_rows = cotangent.reshape(segs_here, SEG, width)
    table = pos_table.T
    small = jnp.concatenate(
        [v.reshape(-1, share) for v in (biases, norm_gains, up_bias)], 0
    )
    if share % 8:
        first_packed = packed = None
    else:
        first_packed = pack_first(w_qkv, table, biases, norm_gains, up_bias)
        packed = stack_columns(width, w_out[0], w_up[0])
    shares_down = w_down[0]
    cross_shares = (w_qkv[1], w_out[1], w_up[1], w_down[1])

    get_qkv = Task(gather_first(net, w_qkv[0], table, small, first_packed))
    window([], [get_qkv])
    shares_down, *cross_shares = window([shares_down, *cross_shares], [get_qkv])
    packed = tie(packed, *cross_shares)[0] if packed is not None else None
    get_middle = Task(gather_middle(net, w_out[0], w_up[0], packed))
    window([], [get_qkv])
    (shares_down,) = window([shares_down], [get_qkv, get_middle])
    tokens, *cross_shares = window([tokens, *cross_shares], [get_qkv])
    *weights_qkv, table, small = get_qkv.get()
    small = small.astype(F32)
    narrow = small[:, :16].transpose(1, 0, 2).reshape(16, width)
    long = small[:, 16:].reshape(count, 2, -1).transpose(1, 0, 2).reshape(2, 1, -1)
    biases0, gains0, up_bias0 = narrow[:6], narrow[12:14], long[0, 0]
    params1 = narrow[6:12], narrow[14:], long[1]

    allowed, onehot, biases0, gains0, up_bias0, *params1 = tie(
        allowed, onehot, biases0, gains0, up_bias0, *params1
    )

    def project(n):
        shift = jnp.concatenate(
            [
                biases0[0, n * half : (n + 1) * half],
                jnp.zeros((half,), F32),
                biases0[1, n * half : (n + 1) * half],
            ]
        )
        return (dot(tokens, weights_qkv[n]) + shift).astype(BF16)

    left = project(0)
    left, shares_down, *cross_shares = window([left, shares_down, *cross_shares], [get_middle])
    get_down = Task(gather_down(net, shares_down))
    get_cross = Task(cross_weight_steps(net, *cross_shares))
    context = segment_attend(left, 0)
    context, tokens = window([context, tokens], [get_middle, get_down, get_cross])
    right = project(1)
    (right,) = window([right], [get_down, get_cross])
    context = segment_attend(right, 1, context)
    qkv = [left, right]
    (context,) = window([context], [get_middle, get_down])
    (context,) = window([context], [get_middle])
    w_out0, w_up0 = get_middle.get()
    normed, normal1, inverse1, normed_low, active, slope = feed_up(
        tokens, context, w_out0, w_up0, biases0, gains0, up_bias0[None, :]
    )
    active, slope, normed = window([active, slope, normed], [get_down, get_cross])
    (normed,) = window([normed], [get_down])
    w_down0 = get_down.get()
    result0, firsts, normal2, inverse2 = feed_down(normed, active, w_down0, biases0, gains0)
    (firsts,) = window([firsts], [get_cross])
    weights1 = get_cross.get()
    firsts = firsts.reshape(segs_here, width)

    own_onehot = lax.dynamic_slice_in_dim(onehot, (net.me >> lo) * segs_here, segs_here, 0)
    cross_in = firsts + dot_nt(own_onehot, table)
    result1, grad_cross, grads1, small1 = cross_encoder(
        net,
        cross_in,
        grad_rows[:, 0, :].astype(F32),
        weights1,
        params1,
        allowed,
        onehot,
    )
    layer_out = put_firsts(result0, result1)

    ways, back_ways = link_orders(net)
    grad_ffn, grad_before, grad_mixed, grad_attn, grad_context, small0 = tail_backward(
        cotangent, grad_cross, (normal1, inverse1, slope, normal2, inverse2), w_out0, w_up0, w_down0,
        gains0,
    )
    grad_ffn, grad_before, grad_attn, grad_context, *grads1 = tie(
        grad_ffn, grad_before, grad_attn, grad_context, *grads1
    )
    red_cross = Task(cross_grad_steps(net, *grads1, ways))
    grad_down = dot_tn(active, grad_ffn).astype(BF16)
    grad_down, grad_before, grad_attn, grad_context = window(
        [grad_down, grad_before, grad_attn, grad_context], [red_cross]
    )
    red_down = Task(reduce_steps(net, [grad_down], back_ways + [lo, hi]))
    grad_up = dot_tn(normed_low, grad_before).astype(BF16)
    grad_out = dot_tn(context, grad_attn).astype(BF16)
    grad_up, grad_out, grad_context = window([grad_up, grad_out, grad_context], [red_down])
    red_up = Task(reduce_steps(net, [grad_up], ways + [lo, hi]))
    back_left, sums_left = segment_attend_back(qkv[0], grad_context, 0)
    back_left, grad_context = window([back_left, grad_context], [red_up])
    grad_left = dot_tn(tokens, back_left).astype(BF16)
    grad_left, grad_context = window([grad_left, grad_context], [red_cross])
    back_right, sums_right = segment_attend_back(qkv[1], grad_context, 1)
    grad_right = dot_tn(tokens, back_right).astype(BF16)
    grad_right, grad_left, grad_out, back_right, sums_left, sums_right = window(
        [grad_right, grad_left, grad_out, back_right, sums_left, sums_right], [red_down, red_up]
    )
    sums = [jnp.sum(v, axis=(0, 1)).reshape(3, half) for v in (sums_left, sums_right)]
    ends = [jnp.concatenate([v[n] for v in sums]) for n in (0, 2)]
    small0 = jnp.concatenate([jnp.stack(ends), small0[2:]])
    small = jnp.stack([small0, small1])
    narrow = small[:, :8].reshape(16, width).T
    long = small[:, 8:].reshape(2, count, -1, share).transpose(1, 3, 0, 2).reshape(width, -1)
    small = jnp.concatenate([narrow, long], 1)
    small = jnp.pad(small, ((0, 0), (0, 128 - small.shape[1]))).astype(BF16)
    red_qkv = Task(
        reduce_steps(
            net, [grad_left, grad_right, grad_out, small], list(zip(back_ways, ways)) + [lo, hi]
        )
    )
    grad_tokens = grad_mixed + dot_nt(back_left, weights_qkv[0]) + dot_nt(back_right, weights_qkv[1])
    (grad_tokens,) = window(
        [grad_tokens.astype(BF16)], [red_qkv, red_down, red_up, red_cross]
    )
    for _ in range(net.bits):
        window([], [red_qkv, red_down, red_up, red_cross])

    grad_left0, grad_right0, grad_out0, small = red_qkv.get()
    narrow = small[:, :16].T.reshape(2, 8, share)
    long = small[:, 16 : 16 + 2 * (hidden // share)]
    long = long.reshape(share, 2, -1).transpose(1, 2, 0).reshape(2, -1)
    (grad_down0,) = red_down.get()
    (grad_up0,) = red_up.get()
    halves = [r.reshape(-1, 3, half) for r in (grad_left0, grad_right0)]
    grad_qkv0 = jnp.stack(halves, 2).reshape(share, -1)
    shares1 = red_cross.get()
    return (
        layer_out,
        grad_tokens,
        jnp.stack([grad_qkv0, shares1[0]]),
        jnp.stack([grad_out0, shares1[1]]),
        jnp.stack([grad_up0, shares1[2]]),
        jnp.stack([grad_down0, shares1[3]]),
        narrow[:, :6],
        long,
        narrow[:, 6:],
        shares1[4][:, : pos_table.shape[0]].T,
    )


def solution(mesh):
    count = mesh.shape["ctx"] * mesh.shape["wa"]
    in_specs = (
        P(AXES, None),
        P(),
        P(None, AXES, None),
        P(None, AXES, None),
        P(None, AXES, None),
        P(None, AXES, None),
        P(None, None, AXES),
        P(None, AXES),
        P(None, None, AXES),
        P(None, AXES),
        P(AXES, None),
    )
    out_specs = (
        P(AXES, None),
        P(AXES, None),
        P(None, AXES, None),
        P(None, AXES, None),
        P(None, AXES, None),
        P(None, AXES, None),
        P(None, None, AXES),
        P(None, AXES),
        P(None, None, AXES),
        P(None, AXES),
    )
    return jax.shard_map(
        partial(shards, count), mesh=mesh, in_specs=in_specs, out_specs=out_specs, check_vma=False
    )
```

```python
from functools import partial

import jax
import jax.numpy as jnp
from jax import lax
from jax.experimental import pallas as pl
from jax.experimental.pallas import tpu as pltpu
from jax.sharding import PartitionSpec as P

HDIM = 64
SEG = 128
TP = 4
AXES = ("ctx", "wa")
F32 = jnp.float32
BF16 = jnp.bfloat16
SCALE = HDIM ** (-0.5)


def work(microseconds):
    return pl.CostEstimate(flops=microseconds * 10**9, transcendentals=0, bytes_accessed=0)


def dot(a, b, dims=((1,), (0,))):
    return lax.dot_general(a, b, (dims, ((), ())), preferred_element_type=F32)


def normalize(values):
    center = values - jnp.mean(values, axis=-1, keepdims=True)
    spread = jnp.mean(center * center, axis=-1, keepdims=True)
    inverse = lax.rsqrt(spread + 1e-05)
    return center * inverse, inverse


def normalize_back(grad, normal, inverse):
    return inverse * (
        grad
        - jnp.mean(grad, axis=-1, keepdims=True)
        - normal * jnp.mean(grad * normal, axis=-1, keepdims=True)
    )


def gelu_pair(values):
    phi = 0.5 * (1.0 + lax.erf(values * 0.7071067811865476))
    density = jnp.exp(-0.5 * values * values) * 0.3989422804014327
    return values * phi, phi + values * density


class Net:
    def __init__(self, count):
        self.count = count
        self.bits = count.bit_length() - 1
        self.me = lax.axis_index(AXES)

    def bit(self, b):
        return (self.me >> b) & 1

    def hop(self, value, b):
        return lax.ppermute(value, AXES, [(i, i ^ (1 << b)) for i in range(self.count)])

    def grow(self, value, b, axis):
        other = self.hop(value, b)
        return jnp.where(
            self.bit(b) == 0,
            jnp.concatenate([value, other], axis),
            jnp.concatenate([other, value], axis),
        )

    def pick(self, value, which, axis):
        return lax.dynamic_slice_in_dim(value, which, 1, axis)


def tie(*values):
    return lax.optimization_barrier(values)


def place_blocks(net, parts, blocks, shapes):
    arrays = [part[0] for part in parts]

    lists = [list(masks) for _, masks, _ in parts]
    table = net.me ^ jnp.array(lists, jnp.int32)

    def body(owner_ref, *refs):
        sources = refs[: len(parts)]
        targets = refs[len(parts) : len(parts) + len(shapes)]
        sem = refs[-1]
        for n, (source, (array, masks, half)) in enumerate(zip(sources, parts)):

            def move(j, carry, n=n, source=source, half=half):
                owner = owner_ref[n, j]
                for row, rows, lane, lanes, which, to_row, to_lane in blocks(half):
                    which, lead = which if isinstance(which, tuple) else (which, ())
                    to = lead + (owner, pl.ds(to_row, rows), pl.ds(to_lane, lanes))
                    pltpu.make_async_copy(
                        source.at[j, pl.ds(row, rows), pl.ds(lane, lanes)], targets[which].at[to], sem
                    ).start()
                return carry

            lax.fori_loop(0, len(masks), move, 0)
        for target in targets:
            pltpu.make_async_copy(target, target, sem).wait()

    return pl.pallas_call(
        body,
        out_shape=[jax.ShapeDtypeStruct(shape, BF16) for shape in shapes],
        in_specs=[pl.BlockSpec(memory_space=pltpu.SMEM)]
        + [pl.BlockSpec(memory_space=pl.ANY)] * len(parts),
        out_specs=[pl.BlockSpec(memory_space=pltpu.VMEM)] * len(shapes),
        scratch_shapes=[pltpu.SemaphoreType.DMA],
        name="place_blocks",
        cost_estimate=work(3),
        compiler_params=pltpu.CompilerParams(vmem_limit_bytes=16 << 20),
    )(table, *arrays)


def link_orders(net):
    mid = list(range(1, net.bits - 2))
    return mid, mid[::-1]


class Task:
    def __init__(self, steps):
        self.steps, self.flight, self.result = steps, None, None
        self.advance(None)

    def advance(self, arrived):
        try:
            self.flight = list(self.steps.send(arrived))
        except StopIteration as stop:
            self.flight, self.result = [], stop.value

    def get(self):
        while self.flight:
            self.advance(self.flight)
        return self.result


def window(values, tasks):
    done = tie(*values, *[f for task in tasks for f in task.flight])
    at = len(values)
    for task in tasks:
        size = len(task.flight)
        if size:
            task.advance(list(done[at : at + size]))
        at += size
    return done[: len(values)]


def gather_steps(net, have, high, early=False):
    have, masks = have[None], [0]
    for b in high:
        (other,) = yield [net.hop(have, b)]
        have = jnp.concatenate([have, other], 0)
        masks = masks + [m ^ (1 << b) for m in masks]
    cut = have.shape[2] // 2
    halves = [have[:, :, :cut], have[:, :, cut:]]
    orders = link_orders(net)
    lists = [masks, masks]
    for step in range(len(orders[0]) - 1):
        others = yield [net.hop(h, o[step]) for h, o in zip(halves, orders)]
        halves = [jnp.concatenate([h, o], 0) for h, o in zip(halves, others)]
        lists = [l + [m ^ (1 << o[step]) for m in l] for l, o in zip(lists, orders)]
    last = [o[-1] for o in orders]
    if early:
        arrived = yield [net.hop(h, b) for h, b in zip(halves, last)] + [
            net.hop(h, 0) for h in halves
        ]
        late, early_core = arrived[:2], arrived[2:]
        late_core = yield [net.hop(h, 0) for h in late]
    else:
        late = yield [net.hop(h, b) for h, b in zip(halves, last)]
        arrived = yield [net.hop(h, 0) for h in halves + late]
        early_core, late_core = arrived[:2], arrived[2:]
    core = [c for pair in zip(early_core, late_core) for c in pair]
    parts = []
    for n in (0, 1):
        late_list = [m ^ (1 << last[n]) for m in lists[n]]
        parts.append((halves[n], lists[n], n))
        parts.append((core[2 * n], [m ^ 1 for m in lists[n]], n))
        parts.append((late[n], late_list, n))
        parts.append((core[2 * n + 1], [m ^ 1 for m in late_list], n))
    return parts


def stack_columns(width, *shares):
    pieces = []
    for share in shares:
        for at in range(0, share.shape[1], width):
            pieces.append(share[:, at : at + width])
    return jnp.concatenate(pieces, 0)


def flat_rows(out):
    return out.reshape(-1, out.shape[2])


def pack_first(w_qkv, table, biases, gains, up_bias):
    rows, width = w_qkv.shape[1], w_qkv.shape[2] // 3
    share = biases.shape[2]
    groups = up_bias.shape[1] // share

    def body(qkv_ref, table_ref, bias_ref, gain_ref, up_ref, out_ref):
        for i in range(3):
            out_ref[i * rows : (i + 1) * rows, :] = qkv_ref[0, :, i * width : (i + 1) * width]
        up = up_ref[...].astype(F32)
        small = jnp.concatenate(
            [bias_ref[e].astype(F32) for e in (0, 1)]
            + [gain_ref[e].astype(F32) for e in (0, 1)]
            + [up[e : e + 1, k * share : (k + 1) * share] for e in (0, 1) for k in range(groups)],
            0,
        )
        small = jnp.concatenate([small, jnp.zeros((24, 128 - share), F32)], 1)
        table = table_ref[...].astype(F32)
        out_ref[3 * rows :, :] = jnp.concatenate(
            [v[i : i + 8] for v in (table, small) for i in (0, 8, 16)], 1
        ).astype(BF16)

    return pl.pallas_call(
        body, out_shape=jax.ShapeDtypeStruct((3 * rows + 8, width), BF16), name="pack_first",
        cost_estimate=work(2),
    )(w_qkv, table, biases, gains, up_bias)


def gather_first(net, w_qkv, table, small, packed):
    rows, width = w_qkv.shape[0], w_qkv.shape[1] // 3
    half = width // 2
    if packed is None:
        cube = lax.all_gather(w_qkv, AXES, axis=0, tiled=True).reshape(width, 3, 2, half)
        return (
            cube[:, :, 0].reshape(width, -1),
            cube[:, :, 1].reshape(width, -1),
            lax.all_gather(table, AXES, axis=0, tiled=True),
            lax.all_gather(small, AXES, axis=0),
        )
    parts = yield from gather_steps(net, packed, (net.bits - 1, net.bits - 2), True)
    left, right, table, small = place_blocks(
        net,
        parts,
        lambda h: [(i * rows, rows, 0, half, h, 0, i * half) for i in range(3)]
        + [(3 * rows, 8, i * 128, 128, 2 + h, i * 8, 0) for i in range(3)],
        [(net.count, rows, 3 * half)] * 2 + [(net.count, 24, 128)] * 2,
    )
    return flat_rows(left), flat_rows(right), flat_rows(table), small[:, :, :rows]


def gather_middle(net, w_out, w_up, packed):
    rows, width = w_out.shape
    if packed is None:
        return [lax.all_gather(w, AXES, axis=0, tiled=True) for w in (w_out, w_up)]
    parts = yield from gather_steps(net, packed, (net.bits - 1, net.bits - 2))
    columns = w_up.shape[1] // width
    half = width // 2
    out, up = place_blocks(
        net,
        parts,
        lambda h: [(0, rows, 0, half, 0, 0, h * half)]
        + [((i + 1) * rows, rows, 0, half, 1, 0, i * width + h * half) for i in range(columns)],
        [(net.count,) + w.shape for w in (w_out, w_up)],
    )
    return flat_rows(out), flat_rows(up)


def gather_down(net, w_down):
    rows, width = w_down.shape
    if rows % 32:
        return lax.all_gather(w_down, AXES, axis=0, tiled=True)
    parts = yield from gather_steps(net, w_down, (net.bits - 1, net.bits - 2))
    half = width // 2
    (down,) = place_blocks(
        net, parts, lambda h: [(0, rows, 0, half, 0, 0, h * half)], [(net.count, rows, width)]
    )
    return flat_rows(down)


def settle(keep, other, dtype=BF16):
    return (keep.astype(F32) + other.astype(F32)).astype(dtype)


def reduce_steps(net, grads, order):
    axis = lambda b: net.bits - 1 - b
    cubes = [g.reshape((2,) * net.bits + (g.shape[0] // net.count, g.shape[1])) for g in grads]
    widths = [g.shape[1] for g in grads]
    join = lambda values: jnp.concatenate(values, -1) if len(values) > 1 else values[0]
    arrived = yield [net.hop(net.pick(c, 1 - net.bit(0), axis(0)), 0) for c in cubes]
    pairs = [(net.pick(c, net.bit(0), axis(0)), f) for c, f in zip(cubes, arrived)]
    for b in order:
        if isinstance(b, tuple):
            if len(pairs) != 2:
                keep, other = join([k for k, _ in pairs]), join([f for _, f in pairs])
                cut = keep.shape[-1] // 256 * 128
                pairs = [(keep[..., :cut], other[..., :cut]), (keep[..., cut:], other[..., cut:])]
            sides = lambda turn: [
                settle(net.pick(k, t, axis(x)), net.pick(f, t, axis(x)))
                for (k, f), x in zip(pairs, b)
                for t in [net.bit(x) ^ turn]
            ]
            sent, kept = sides(1), sides(0)
            arrived = yield [net.hop(v, x) for v, x in zip(sent, b)]
            pairs = list(zip(kept, arrived))
            continue
        side = lambda which: join(
            [settle(net.pick(k, which, axis(b)), net.pick(f, which, axis(b))) for k, f in pairs]
        )
        sent, kept = side(1 - net.bit(b)), side(net.bit(b))
        (other,) = yield [net.hop(sent, b)]
        pairs = [(kept, other)]
    whole = settle(*pairs[0], F32)
    whole = whole.reshape(whole.shape[-2:])
    out, at = [], 0
    for w in widths:
        out.append(whole[:, at : at + w])
        at += w
    return out


def ordered(net, value, other, b, axis):
    return jnp.where(
        net.bit(b) == 0,
        jnp.concatenate([value, other], axis),
        jnp.concatenate([other, value], axis),
    )


def trade_pair(net, value, b, axis):
    return net.hop(net.pick(value, 1 - net.bit(b), axis), b), net.pick(value, net.bit(b), axis)


def dot_nt(a, b):
    return dot(a, b, ((1,), (1,)))


def dot_tn(a, b):
    return dot(a, b, ((0,), (0,)))


def pick_lanes(mask, values):
    return jnp.where(mask, values, jnp.zeros_like(values))


def head_masks(rows):
    lane = lax.broadcasted_iota(jnp.int32, (rows, 2 * HDIM), 1)
    return lane < HDIM, lane >= HDIM


def chance_of(keys, queries):
    scores = dot_nt(keys, queries) * SCALE
    raised = jnp.exp(scores - jnp.max(scores, axis=0, keepdims=True))
    return raised * (1.0 / jnp.sum(raised, axis=0, keepdims=True))


def attend_forward_body(heads, qkv_ref, out_ref):
    width = heads * HDIM
    for at in range(0, width, 2 * HDIM):
        queries, keys, values = [qkv_ref[:, n * width + at : n * width + at + 128] for n in range(3)]
        total = 0.0
        for mask in head_masks(SEG):
            chance = chance_of(pick_lanes(mask, keys), queries).astype(BF16)
            total = total + dot_tn(pick_lanes(mask, values), chance)
        out_ref[:, at : at + 128] = total.T.astype(BF16)


def attend_backward_body(heads, qkv_ref, grad_ref, out_ref, sums_ref):
    width = heads * HDIM
    for at in range(0, width, 2 * HDIM):
        queries, keys, values = [qkv_ref[:, n * width + at : n * width + at + 128] for n in range(3)]
        grad = grad_ref[:, at : at + 128]
        totals = [0.0, 0.0, 0.0]
        for mask in head_masks(SEG):
            own_keys = pick_lanes(mask, keys)
            chance = chance_of(own_keys, queries)
            slope = dot_nt(pick_lanes(mask, values), grad)
            slope = slope - jnp.sum(slope * chance, axis=0, keepdims=True)
            tilt = (chance * slope).astype(BF16)
            totals[0] = totals[0] + dot_tn(tilt, own_keys)
            totals[1] = totals[1] + dot(tilt, pick_lanes(mask, queries))
            totals[2] = totals[2] + dot(chance.astype(BF16), pick_lanes(mask, grad))
        for n, (total, scale) in enumerate(zip(totals, (SCALE, SCALE, 1.0))):
            low = (total * scale).astype(BF16)
            out_ref[:, n * width + at : n * width + at + 128] = low
            sums_ref[0, :, n * width + at : n * width + at + 128] = jnp.sum(
                low.astype(F32), axis=0, keepdims=True
            )


def segment_attend(qkv, half, context=None):
    rows, width = qkv.shape[0], qkv.shape[1] // 3

    def body(*refs):
        attend_forward_body(width // HDIM, refs[0], refs[-1])

    return pl.pallas_call(
        body,
        out_shape=jax.ShapeDtypeStruct((rows, 2 * width), BF16),
        grid=(rows // SEG,),
        in_specs=[pl.BlockSpec((SEG, 3 * width), lambda i: (i, 0))]
        + [pl.BlockSpec(memory_space=pl.ANY)] * half,
        out_specs=pl.BlockSpec((SEG, width), lambda i: (i, half)),
        input_output_aliases={1: 0} if half else {},
        name="segment_attend",
        compiler_params=pltpu.CompilerParams(vmem_limit_bytes=12 << 20),
        cost_estimate=work(10),
    )(*([qkv, context] if half else [qkv]))


def segment_attend_back(qkv, grad, half):
    rows, width = qkv.shape[0], qkv.shape[1] // 3
    return pl.pallas_call(
        partial(attend_backward_body, width // HDIM),
        out_shape=(
            jax.ShapeDtypeStruct((rows, 3 * width), BF16),
            jax.ShapeDtypeStruct((rows // SEG, 1, 3 * width), F32),
        ),
        grid=(rows // SEG,),
        in_specs=[
            pl.BlockSpec((SEG, 3 * width), lambda i: (i, 0)),
            pl.BlockSpec((SEG, width), lambda i: (i, half)),
        ],
        out_specs=(
            pl.BlockSpec((SEG, 3 * width), lambda i: (i, 0)),
            pl.BlockSpec((1, 1, 3 * width), lambda i: (i, 0, 0)),
        ),
        name="segment_attend_back",
        compiler_params=pltpu.CompilerParams(vmem_limit_bytes=16 << 20),
        cost_estimate=work(12),
    )(qkv, grad)


BLOCK = 256


def row_block(width):
    return pl.BlockSpec((BLOCK, width), lambda i: (i, 0))


def whole(shape):
    return pl.BlockSpec(
        shape, lambda i: (0,) * len(shape), pipeline_mode=pl.Buffered(1)
    )


def feed_up(tokens, context, w_out, w_up, biases, gains, up_bias):
    rows, width = tokens.shape
    hidden = w_up.shape[1]

    def body(
        tokens_ref, context_ref, out_ref, up_ref, bias_ref, gain_ref, up_bias_ref,
        normed_ref, normal_ref, inverse_ref, low_ref, active_ref, slope_ref,
    ):
        mixed = tokens_ref[...].astype(F32) + dot(context_ref[...], out_ref[...]) + bias_ref[2:3, :]
        normal, inverse = normalize(mixed)
        normal_ref[...] = normal.astype(BF16)
        inverse_ref[...] = inverse
        normed = normal * gain_ref[0:1, :] + bias_ref[3:4, :]
        normed_ref[...] = normed
        low = normed.astype(BF16)
        low_ref[...] = low
        for at in range(0, hidden, width):
            part = slice(at, at + width)
            active, slope = gelu_pair(dot(low, up_ref[:, part]) + up_bias_ref[:, part])
            active_ref[:, part] = active.astype(BF16)
            slope_ref[:, part] = slope.astype(BF16)

    outs = [(width, F32), (width, BF16), (1, F32), (width, BF16), (hidden, BF16), (hidden, BF16)]
    return pl.pallas_call(
        body,
        grid=(rows // BLOCK,),
        out_shape=[jax.ShapeDtypeStruct((rows, w), t) for w, t in outs],
        in_specs=[row_block(width)] * 2
        + [whole(v.shape) for v in (w_out, w_up, biases, gains, up_bias)],
        out_specs=[row_block(w) for w, _ in outs],
        name="feed_up",
        compiler_params=pltpu.CompilerParams(vmem_limit_bytes=36 << 20),
        cost_estimate=work(18),
    )(tokens, context, w_out, w_up, biases, gains, up_bias)


def feed_down(normed, active, w_down, biases, gains):
    rows, width = normed.shape
    per = BLOCK // SEG

    def body(
        normed_ref, active_ref, down_ref, bias_ref, gain_ref,
        result_ref, first_ref, normal_ref, inverse_ref,
    ):
        second = normed_ref[...] + dot(active_ref[...], down_ref[...]) + bias_ref[4:5, :]
        normal, inverse = normalize(second)
        normal_ref[...] = normal.astype(BF16)
        inverse_ref[...] = inverse
        result = normal * gain_ref[1:2, :] + bias_ref[5:6, :]
        result_ref[...] = result.astype(BF16)
        for k in range(per):
            first_ref[0, k : k + 1, :] = result[k * SEG : k * SEG + 1]

    return pl.pallas_call(
        body,
        grid=(rows // BLOCK,),
        out_shape=[
            jax.ShapeDtypeStruct((rows, width), BF16),
            jax.ShapeDtypeStruct((rows // BLOCK, per, width), F32),
            jax.ShapeDtypeStruct((rows, width), BF16),
            jax.ShapeDtypeStruct((rows, 1), F32),
        ],
        in_specs=[row_block(width), row_block(active.shape[1])]
        + [whole(v.shape) for v in (w_down, biases, gains)],
        out_specs=[
            row_block(width), pl.BlockSpec((1, per, width), lambda i: (i, 0, 0)), row_block(width),
            row_block(1),
        ],
        name="feed_down",
        compiler_params=pltpu.CompilerParams(vmem_limit_bytes=28 << 20),
        cost_estimate=work(11),
    )(normed, active, w_down, biases, gains)


def tail_backward(cotangent, firsts, kept, w_out, w_up, w_down, gains):
    normal1, inverse1, slope, normal2, inverse2 = kept
    rows, width = cotangent.shape
    hidden = w_up.shape[1]
    per = BLOCK // SEG
    lines = 8 + hidden // width

    def body(
        cotangent_ref, first_ref, normal1_ref, inverse1_ref, slope_ref, normal2_ref, inverse2_ref,
        out_ref, up_ref, down_ref, gain_ref,
        ffn_ref, before_ref, mixed_ref, attn_ref, context_ref, sums_ref,
    ):
        grad = cotangent_ref[...].astype(F32)
        row = lax.broadcasted_iota(jnp.int32, (BLOCK, 1), 0)
        for k in range(per):
            grad = jnp.where(row == k * SEG, first_ref[0, k : k + 1, :], grad)
        normal2 = normal2_ref[...].astype(F32)
        grad_second = normalize_back(grad * gain_ref[1:2, :], normal2, inverse2_ref[...])
        ffn = grad_second.astype(BF16)
        ffn_ref[...] = ffn
        grad_normed = grad_second
        up_sums = []
        for at in range(0, hidden, width):
            part = slice(at, at + width)
            before = dot_nt(ffn, down_ref[part, :]) * slope_ref[:, part].astype(F32)
            before = before.astype(BF16)
            before_ref[:, part] = before
            up_sums.append(before)
            grad_normed = grad_normed + dot_nt(before, up_ref[:, part])
        normal1 = normal1_ref[...].astype(F32)
        grad_mixed = normalize_back(grad_normed * gain_ref[0:1, :], normal1, inverse1_ref[...])
        mixed_ref[...] = grad_mixed
        attn = grad_mixed.astype(BF16)
        attn_ref[...] = attn
        context_ref[...] = dot_nt(attn, out_ref[...]).astype(BF16)

        @pl.when(pl.program_id(0) == 0)
        def _():
            sums_ref[...] = jnp.zeros_like(sums_ref)

        values = [attn, grad_normed, ffn, grad, grad_normed * normal1, grad * normal2] + up_sums
        for n, value in enumerate(values):
            sums_ref[n + 2 : n + 3, :] += jnp.sum(value.astype(F32), axis=0, keepdims=True)

    return pl.pallas_call(
        body,
        grid=(rows // BLOCK,),
        out_shape=[
            jax.ShapeDtypeStruct((rows, width), BF16),
            jax.ShapeDtypeStruct((rows, hidden), BF16),
            jax.ShapeDtypeStruct((rows, width), F32),
            jax.ShapeDtypeStruct((rows, width), BF16),
            jax.ShapeDtypeStruct((rows, width), BF16),
            jax.ShapeDtypeStruct((lines, width), F32),
        ],
        in_specs=[
            row_block(width),
            pl.BlockSpec((1, per, width), lambda i: (i, 0, 0)),
            row_block(width), row_block(1), row_block(hidden), row_block(width), row_block(1),
        ]
        + [whole(v.shape) for v in (w_out, w_up, w_down, gains)],
        out_specs=[
            row_block(width), row_block(hidden), row_block(width), row_block(width),
            row_block(width), pl.BlockSpec((lines, width), lambda i: (0, 0)),
        ],
        name="tail_backward",
        compiler_params=pltpu.CompilerParams(vmem_limit_bytes=36 << 20),
        cost_estimate=work(24),
    )(
        cotangent, firsts.reshape(-1, per, width), normal1, inverse1, slope, normal2, inverse2,
        w_out, w_up, w_down, gains,
    )


def put_firsts(values, firsts):
    rows, width = values.shape

    def body(old_ref, first_ref, out_ref):
        row = lax.broadcasted_iota(jnp.int32, (16, 1), 0)
        old = old_ref[...].astype(F32)
        out_ref[...] = jnp.where(row == 0, first_ref[0], old).astype(BF16)

    block = pl.BlockSpec((16, width), lambda i: (i * (SEG // 16), 0))
    return pl.pallas_call(
        body,
        grid=(rows // SEG,),
        out_shape=jax.ShapeDtypeStruct(values.shape, BF16),
        in_specs=[block, pl.BlockSpec((1, 1, width), lambda i: (i, 0, 0))],
        out_specs=block,
        input_output_aliases={0: 0},
        name="put_firsts",
        compiler_params=pltpu.CompilerParams(vmem_limit_bytes=4 << 20),
        cost_estimate=work(4),
    )(values, firsts[:, None, :])


def cross_weight_steps(net, w_qkv, w_out, w_up, w_down):
    rows, width = w_out.shape
    hi, lo = net.bits - 1, net.bits - 2
    part = width // TP
    planes = net.count // TP
    cube = w_qkv.reshape(rows, 3, TP, part)
    ups = w_up.reshape(rows, TP, -1)
    hidden = ups.shape[2]
    assert hidden == width
    kvq = jnp.concatenate([cube[:, 1], cube[:, 2], cube[:, 0], jnp.zeros_like(cube[:, 0])], 2)
    cols = jnp.stack([ups, kvq]).transpose(2, 0, 1, 3).reshape(2, 2, 2 * rows, width)
    for b, axis in ((hi, 0), (lo, 1)):
        flight, keep = trade_pair(net, cols, b, axis)
        (other,) = yield [flight]
        cols = ordered(net, keep, other, b, axis)
    have = jnp.concatenate([cols.reshape(-1, width), w_out, w_down], 0)
    if rows % 8:
        value = have[None]
        for b in range(net.bits - 2):
            (other,) = yield [net.hop(value, b)]
            value = ordered(net, value, other, b, 0)
        cols = value[:, : 8 * rows].reshape(planes, TP, 2, rows, width).transpose(1, 0, 3, 2, 4)
        return (
            cols.reshape(width, 2 * width),
            value[:, 8 * rows : 9 * rows].reshape(part, width),
            value[:, 9 * rows :].reshape(hidden, width),
        )
    parts = yield from gather_steps(net, have, ())
    parts = [(array, [m & (planes - 1) for m in masks], h) for array, masks, h in parts]
    half = width // 2
    plane = Net.__new__(Net)
    plane.me = net.me & (planes - 1)
    outs = place_blocks(
        plane,
        parts,
        lambda h: [
            ((2 * t + k) * rows, rows, 0, half, (0, (t,)), 0, k * width + h * half)
            for t in range(TP)
            for k in (0, 1)
        ]
        + [
            (8 * rows, rows, 0, half, 1, 0, h * half),
            (9 * rows, 4 * rows, 0, half, 2, 0, h * half),
        ],
        [(TP, planes, rows, 2 * width), (planes, rows, width), (planes, 4 * rows, width)],
    )
    return outs[0].reshape(width, 2 * width), flat_rows(outs[1]), flat_rows(outs[2])


def cross_grad_steps(net, ups, rest, grad_out, grad_down, order):
    hi, lo = net.bits - 1, net.bits - 2
    plane = net.bits - 2
    planes = net.count // TP
    width = ups.shape[0]
    rows = width // net.count
    part = width // TP
    pair = jnp.stack([ups.reshape(TP, planes, rows, width), rest.reshape(TP, planes, rows, width)])
    whole = jnp.concatenate(
        [
            pair.transpose(2, 1, 0, 3, 4).reshape(planes, 8 * rows, width),
            grad_out.reshape(planes, rows, width),
            grad_down.reshape(planes, 4 * rows, width),
        ],
        1,
    ).reshape((2,) * plane + (13 * rows, width))
    axis = lambda b: plane - 1 - b
    (other,) = yield [net.hop(net.pick(whole, 1 - net.bit(0), axis(0)), 0)]
    kept = net.pick(whole, net.bit(0), axis(0))
    for b in order:
        side = lambda which: settle(net.pick(kept, which, axis(b)), net.pick(other, which, axis(b)))
        sent, kept = side(1 - net.bit(b)), side(net.bit(b))
        (other,) = yield [net.hop(sent, b)]
    whole = settle(kept, other).reshape(13 * rows, width)
    cols = whole[: 8 * rows].reshape(2, 2, 2 * rows, width)
    for b, at in ((hi, 0), (lo, 1)):
        flight, keep = trade_pair(net, cols, b, at)
        (back,) = yield [flight]
        cols = ordered(net, keep, back, b, at)
    whole, cols = yield [whole, cols]
    cols = cols.reshape(TP, 2, rows, width).transpose(1, 2, 0, 3).astype(F32)
    deep = whole[8 * rows :].astype(F32)
    pieces = [cols[1, :, :, n * part : (n + 1) * part].reshape(rows, width) for n in (2, 0, 1)]
    return (
        jnp.concatenate(pieces, 1),
        deep[:rows],
        cols[0].reshape(rows, -1),
        deep[rows:],
        cols[1, :, 0, 3 * part :],
    )


def lanes_between(values, first, last):
    lane = lax.broadcasted_iota(jnp.int32, values.shape, values.ndim - 1)
    return jnp.where((lane >= first) & (lane < last), values, jnp.zeros_like(values))


def stack_heads(values, heads, first):
    return jnp.concatenate(
        [lanes_between(values, first + h * HDIM, first + (h + 1) * HDIM) for h in range(heads)], 0
    )


def merge_heads(values, heads, first):
    rows = values.shape[0] // heads
    return sum(
        lanes_between(values[h * rows : (h + 1) * rows], first + h * HDIM, first + (h + 1) * HDIM)
        for h in range(heads)
    )


def fused(body, outs, *args, name):
    return pl.pallas_call(
        body, out_shape=[jax.ShapeDtypeStruct(shape, dtype) for shape, dtype in outs], name=name,
        compiler_params=pltpu.CompilerParams(vmem_limit_bytes=32 << 20),
        cost_estimate=work(3),
    )(*args)


def cross_encoder(net, cross_in, grad_own, weights, params, allowed, onehot):
    cols, w_out, w_down = weights
    own, width = cross_in.shape
    part, hidden = w_out.shape[0], w_down.shape[0]
    plane = net.bits - 2
    hi, lo = net.bits - 1, net.bits - 2
    member = net.me >> lo
    up = list(range(1, plane))
    heads = part // HDIM
    biases, gains, up_bias = params
    row = lambda n: biases[n : n + 1]
    slab = lambda vector, size: lax.dynamic_slice_in_dim(vector, member * size, size, 1)
    bias_kv = jnp.concatenate([jnp.zeros((1, part), F32), slab(row(1), part)], 1)
    bias_q = slab(row(0), part)
    bias_up = slab(up_bias.reshape(1, -1), hidden)
    both = jnp.concatenate([cross_in, grad_own], 0)[None]
    both = net.grow(net.grow(both, lo, 0), hi, 0)
    count = TP * own
    full, wide, flat = (count, width), (count, 2 * part), (count, part)

    def project(x_ref, cols_ref, bias_kv_ref, bias_q_ref, hidden_ref, grad_ref, low_ref, kv_ref, q_ref):
        values = jnp.concatenate([x_ref[t, :own, :] for t in range(TP)], 0)
        hidden_ref[...] = values
        grad_ref[...] = jnp.concatenate([x_ref[t, own:, :] for t in range(TP)], 0)
        low = values.astype(BF16)
        low_ref[...] = low
        kv = dot(low, cols_ref[:, hidden : hidden + 2 * part]) + bias_kv_ref[...]
        kv_ref[...] = kv.astype(BF16)
        q_ref[...] = (dot(low, cols_ref[:, hidden + 2 * part : hidden + 3 * part]) + bias_q_ref[...]).astype(BF16)

    hidden_all, grad_all, hidden_low, kv, queries = fused(
        project,
        [(full, F32), (full, F32), (full, BF16), (wide, BF16), (flat, BF16)],
        both, cols, bias_kv, bias_q,
        name="cross_project",
    )
    have = kv
    for b in up:
        have = jnp.concatenate([have, net.hop(have, b)], 0)
    late = net.hop(have, 0)
    seen = 2 * have.shape[0]

    def attend(q_ref, have_ref, late_ref, allowed_ref, out_w_ref, chance_ref, context_ref, part_ref):
        kv = jnp.concatenate([have_ref[...], late_ref[...]], 0)
        q = q_ref[...]
        spread = stack_heads(jnp.concatenate([q, jnp.zeros_like(q)], 1), heads, 0)
        scores = dot_nt(spread, kv) * SCALE
        scores = jnp.where(jnp.concatenate([allowed_ref[...]] * heads, 0) > 0.5, scores, -1e30)
        raised = jnp.exp(scores - jnp.max(scores, axis=1, keepdims=True))
        chance = raised * (1.0 / jnp.sum(raised, axis=1, keepdims=True))
        chance_ref[...] = chance
        context = merge_heads(dot(chance.astype(BF16), kv), heads, part)[:, part:].astype(BF16)
        context_ref[...] = context
        part_ref[...] = dot(context, out_w_ref[...]).astype(BF16)

    chance, context, partial_sum = fused(
        attend,
        [((heads * count, seen), F32), (flat, BF16), (full, BF16)],
        queries, have, late, allowed, w_out,
        name="cross_attend",
    )
    half_sum = settle(partial_sum, net.hop(partial_sum, lo))
    other_sum = net.hop(half_sum, hi)

    def feed(
        x_ref, a_ref, b_ref, bias_ref, gain_ref, cols_ref, bias_up_ref, down_ref,
        normed_ref, normal_ref, inverse_ref, low_ref, active_ref, slope_ref, part_ref,
    ):
        mixed = x_ref[...] + (a_ref[...].astype(F32) + b_ref[...].astype(F32)) + bias_ref[2:3, :]
        normal, inverse = normalize(mixed)
        normed = normal * gain_ref[0:1, :] + bias_ref[3:4, :]
        low = normed.astype(BF16)
        active, slope = gelu_pair(dot(low, cols_ref[:, :hidden]) + bias_up_ref[...])
        active = active.astype(BF16)
        normed_ref[...] = normed
        normal_ref[...] = normal
        inverse_ref[...] = inverse
        low_ref[...] = low
        active_ref[...] = active
        slope_ref[...] = slope
        part_ref[...] = dot(active, down_ref[...]).astype(BF16)

    normed, normal1, inverse1, normed_low, active, slope, partial_sum = fused(
        feed,
        [
            (full, F32), (full, F32), ((count, 1), F32), (full, BF16),
            ((count, hidden), BF16), ((count, hidden), F32), (full, BF16),
        ],
        hidden_all, half_sum, other_sum, biases, gains, cols, bias_up, w_down,
        name="cross_feed",
    )
    half_sum = settle(partial_sum, net.hop(partial_sum, lo))
    other_sum = net.hop(half_sum, hi)

    def turn(
        normed_ref, a_ref, b_ref, bias_ref, gain_ref, grad_ref, down_ref, slope_ref, cols_ref,
        result_ref, normal_ref, second_ref, ffn_ref, before_ref, part_ref,
    ):
        second = normed_ref[...] + (a_ref[...].astype(F32) + b_ref[...].astype(F32)) + bias_ref[4:5, :]
        normal, inverse = normalize(second)
        gain = gain_ref[1:2, :]
        result_ref[...] = normal * gain + bias_ref[5:6, :]
        normal_ref[...] = normal
        grad_second = normalize_back(grad_ref[...] * gain, normal, inverse)
        second_ref[...] = grad_second
        ffn = grad_second.astype(BF16)
        ffn_ref[...] = ffn
        before = (dot_nt(ffn, down_ref[...]) * slope_ref[...]).astype(BF16)
        before_ref[...] = before
        part_ref[...] = dot_nt(before, cols_ref[:, :hidden]).astype(BF16)

    result, normal2, grad_second, grad_ffn, grad_before, partial_sum = fused(
        turn,
        [
            (full, F32), (full, F32), (full, F32), (full, BF16),
            ((count, hidden), BF16), (full, BF16),
        ],
        normed, half_sum, other_sum, biases, gains, grad_all, w_down, slope, cols,
        name="cross_turn",
    )
    half_sum = settle(partial_sum, net.hop(partial_sum, lo))
    other_sum = net.hop(half_sum, hi)

    def attend_back(
        second_ref, a_ref, b_ref, normal_ref, inverse_ref, gain_ref, out_w_ref, chance_ref,
        q_ref, have_ref, late_ref,
        normed_ref, mixed_ref, attn_ref, grad_q_ref, keep_ref, send_ref,
    ):
        grad_normed = second_ref[...] + (a_ref[...].astype(F32) + b_ref[...].astype(F32))
        normed_ref[...] = grad_normed
        grad_mixed = normalize_back(
            grad_normed * gain_ref[0:1, :], normal_ref[...], inverse_ref[...]
        )
        mixed_ref[...] = grad_mixed
        attn = grad_mixed.astype(BF16)
        attn_ref[...] = attn
        grad = dot_nt(attn, out_w_ref[...]).astype(BF16)
        grads = stack_heads(jnp.concatenate([jnp.zeros_like(grad), grad], 1), heads, part)
        q = q_ref[...]
        spread = stack_heads(jnp.concatenate([q, jnp.zeros_like(q)], 1), heads, 0)
        kv = jnp.concatenate([have_ref[...], late_ref[...]], 0)
        chance = chance_ref[...]
        slopes = dot_nt(grads, kv)
        slopes = slopes - jnp.sum(slopes * chance, axis=1, keepdims=True)
        tilt = (chance * slopes).astype(BF16)
        grad_q = merge_heads(dot(tilt, kv), heads, 0)[:, :part] * SCALE
        grad_q_ref[...] = grad_q.astype(BF16)
        grad_kv = dot_tn(tilt, spread) * SCALE + dot_tn(chance.astype(BF16), grads)
        keep_ref[...] = grad_kv[: seen // 2]
        send_ref[...] = grad_kv[seen // 2 :]

    grad_normed, grad_mixed, grad_attn, grad_q, keep, send = fused(
        attend_back,
        [
            (full, F32), (full, F32), (full, BF16), (flat, BF16),
            ((seen // 2, 2 * part), F32), ((seen // 2, 2 * part), F32),
        ],
        grad_second, half_sum, other_sum, normal1, inverse1, gains, w_out, chance,
        queries, have, late,
        name="cross_attend_back",
    )
    other = net.hop(send, 0)
    for b in up[::-1]:
        size = keep.shape[0] // 2
        total = keep + other
        keep, other = total[:size], net.hop(total[size:], b)

    def project_back(grad_q_ref, keep_ref, other_ref, cols_ref, grad_ref, back_ref):
        grad_kv = (keep_ref[...] + other_ref[...]).astype(BF16)
        grad_q = grad_q_ref[...]
        grad_ref[...] = jnp.concatenate([grad_kv, grad_q], 1)
        back = dot_nt(grad_kv, cols_ref[:, hidden : hidden + 2 * part]) + dot_nt(
            grad_q, cols_ref[:, hidden + 2 * part : hidden + 3 * part]
        )
        back_ref[...] = back.astype(BF16)

    grad_kvq, back = fused(
        project_back,
        [((count, 3 * part), BF16), (full, BF16)],
        grad_q, keep, other, cols,
        name="cross_project_back",
    )
    half_sum = settle(back, net.hop(back, lo))
    grad_in = grad_mixed + settle(half_sum, net.hop(half_sum, hi), F32)
    mine = lambda values: lax.dynamic_slice_in_dim(values, member * own, own, 0)

    def feed_grads(normed_ref, before_ref, active_ref, ffn_ref, up_ref, down_ref):
        up_ref[...] = dot_tn(normed_ref[...], before_ref[...]).astype(BF16)
        down_ref[...] = dot_tn(active_ref[...], ffn_ref[...]).astype(BF16)

    grad_up, grad_down = fused(
        feed_grads,
        [((width, hidden), BF16), (w_down.shape, BF16)],
        normed_low, grad_before, active, grad_ffn,
        name="cross_feed_grads",
    )

    def attend_grads(
        low_ref, grad_ref, context_ref, attn_ref, in_ref, onehot_ref, rest_ref, out_ref
    ):
        table = dot_tn(in_ref[...].astype(BF16), onehot_ref[...])
        rest_ref[...] = jnp.concatenate(
            [
                dot_tn(low_ref[...], grad_ref[...]),
                table,
                jnp.zeros((width, part - table.shape[1]), F32),
            ],
            1,
        ).astype(BF16)
        out_ref[...] = dot_tn(context_ref[...], attn_ref[...]).astype(BF16)

    rest, grad_wout = fused(
        attend_grads,
        [((width, width), BF16), (w_out.shape, BF16)],
        hidden_low, grad_kvq, context, grad_attn, grad_in, onehot,
        name="cross_attend_grads",
    )
    grads = grad_up, rest, grad_wout, grad_down

    def small_sums(
        member_ref, grad_ref, attn_ref, normed_ref, ffn_ref, result_grad_ref, normal1_ref,
        normal2_ref, before_ref, out_ref,
    ):
        member = member_ref[0]
        rows = lax.broadcasted_iota(jnp.int32, full, 0) // own == member
        ours = lambda values: jnp.sum(jnp.where(rows, values, 0.0), axis=0, keepdims=True)
        every = lambda values: jnp.sum(values.astype(F32), axis=0, keepdims=True)

        def spread(values):
            return jnp.concatenate([jnp.where(member == j, values, 0.0) for j in range(TP)], 1)

        sums = every(grad_ref[...])
        grad_normed, grad_result = normed_ref[...], result_grad_ref[...]
        out_ref[...] = jnp.zeros_like(out_ref)
        out_ref[0:1, :] = spread(sums[:, 2 * part :])
        out_ref[1:2, :] = spread(sums[:, part : 2 * part])
        out_ref[2:3, :] = ours(attn_ref[...].astype(F32))
        out_ref[3:4, :] = ours(grad_normed)
        out_ref[4:5, :] = ours(ffn_ref[...].astype(F32))
        out_ref[5:6, :] = ours(grad_result)
        out_ref[6:7, :] = ours(grad_normed * normal1_ref[...])
        out_ref[7:8, :] = ours(grad_result * normal2_ref[...])
        up_sums = every(before_ref[...])
        per = hidden // width
        for j in range(TP):
            for k in range(per):
                at = 8 + j * per + k
                out_ref[at : at + 1, :] = jnp.where(
                    member == j, up_sums[:, k * width : (k + 1) * width], 0.0
                )

    lines = 8 + hidden * TP // width
    small = pl.pallas_call(
        small_sums,
        out_shape=jax.ShapeDtypeStruct((lines, width), F32),
        in_specs=[pl.BlockSpec(memory_space=pltpu.SMEM)]
        + [pl.BlockSpec(memory_space=pltpu.VMEM)] * 8,
        name="cross_small_sums",
        compiler_params=pltpu.CompilerParams(vmem_limit_bytes=8 << 20),
        cost_estimate=work(2),
    )(member.reshape(1), grad_kvq, grad_attn, grad_normed, grad_ffn, grad_all, normal1, normal2,
      grad_before)
    return mine(result), mine(grad_in), grads, small


def places_of(ids, slots, seq_ids, table_rows):
    all_slots = jnp.arange(seq_ids.shape[0], dtype=jnp.int32)
    earlier = (seq_ids[None, :] == ids[:, None]) & (all_slots[None, :] < slots[:, None])
    places = jnp.sum(earlier.astype(jnp.int32), axis=1)
    rows = jnp.arange(table_rows, dtype=jnp.int32)
    return (places[:, None] == rows[None, :]).astype(BF16)


def shards(
    count, tokens, seq_ids, w_qkv, w_out, w_up, w_down, biases, up_bias, norm_gains, pos_table, cotangent
):
    net = Net(count)
    rows_here, width = tokens.shape
    segs_here = rows_here // SEG
    share, hidden = biases.shape[2], up_bias.shape[1]
    half = width // 2
    lo, hi = net.bits - 2, net.bits - 1
    planes = count // TP

    order = list(range(1, net.bits - 2)) + [0]
    masks = [0]
    for b in order:
        masks = masks + [m | 1 << b for m in masks]
    slots = jnp.arange(seq_ids.shape[0], dtype=jnp.int32).reshape(TP, planes, segs_here)
    key_slots = jnp.take(slots, (net.me & (planes - 1)) ^ jnp.array(masks, jnp.int32), axis=1)
    row_slots = key_slots[:, 0].reshape(-1)
    key_ids = seq_ids[key_slots.transpose(1, 0, 2).reshape(-1)]
    row_ids = seq_ids[row_slots]
    allowed = (row_ids[:, None] == key_ids[None, :]).astype(F32)
    onehot = places_of(row_ids, row_slots, seq_ids, pos_table.shape[0])

    grad_rows = cotangent.reshape(segs_here, SEG, width)
    table = pos_table.T
    small = jnp.concatenate(
        [v.reshape(-1, share) for v in (biases, norm_gains, up_bias)], 0
    )
    if share % 8:
        first_packed = packed = None
    else:
        first_packed = pack_first(w_qkv, table, biases, norm_gains, up_bias)
        packed = stack_columns(width, w_out[0], w_up[0])
    shares_down = w_down[0]
    cross_shares = (w_qkv[1], w_out[1], w_up[1], w_down[1])

    get_qkv = Task(gather_first(net, w_qkv[0], table, small, first_packed))
    window([], [get_qkv])
    shares_down, *cross_shares = window([shares_down, *cross_shares], [get_qkv])
    packed = tie(packed, *cross_shares)[0] if packed is not None else None
    get_middle = Task(gather_middle(net, w_out[0], w_up[0], packed))
    window([], [get_qkv])
    (shares_down,) = window([shares_down], [get_qkv, get_middle])
    tokens, *cross_shares = window([tokens, *cross_shares], [get_qkv])
    *weights_qkv, table, small = get_qkv.get()
    small = small.astype(F32)
    narrow = small[:, :16].transpose(1, 0, 2).reshape(16, width)
    long = small[:, 16:].reshape(count, 2, -1).transpose(1, 0, 2).reshape(2, 1, -1)
    biases0, gains0, up_bias0 = narrow[:6], narrow[12:14], long[0, 0]
    params1 = narrow[6:12], narrow[14:], long[1]

    allowed, onehot, biases0, gains0, up_bias0, *params1 = tie(
        allowed, onehot, biases0, gains0, up_bias0, *params1
    )

    def project(n):
        shift = jnp.concatenate(
            [
                biases0[0, n * half : (n + 1) * half],
                jnp.zeros((half,), F32),
                biases0[1, n * half : (n + 1) * half],
            ]
        )
        return (dot(tokens, weights_qkv[n]) + shift).astype(BF16)

    left = project(0)
    left, shares_down, *cross_shares = window([left, shares_down, *cross_shares], [get_middle])
    get_down = Task(gather_down(net, shares_down))
    get_cross = Task(cross_weight_steps(net, *cross_shares))
    context = segment_attend(left, 0)
    context, tokens = window([context, tokens], [get_middle, get_down, get_cross])
    right = project(1)
    (right,) = window([right], [get_down, get_cross])
    context = segment_attend(right, 1, context)
    qkv = [left, right]
    (context,) = window([context], [get_middle, get_down])
    (context,) = window([context], [get_middle])
    w_out0, w_up0 = get_middle.get()
    normed, normal1, inverse1, normed_low, active, slope = feed_up(
        tokens, context, w_out0, w_up0, biases0, gains0, up_bias0[None, :]
    )
    active, slope, normed = window([active, slope, normed], [get_down, get_cross])
    (normed,) = window([normed], [get_down])
    w_down0 = get_down.get()
    result0, firsts, normal2, inverse2 = feed_down(normed, active, w_down0, biases0, gains0)
    (firsts,) = window([firsts], [get_cross])
    weights1 = get_cross.get()
    firsts = firsts.reshape(segs_here, width)

    own_onehot = lax.dynamic_slice_in_dim(onehot, (net.me >> lo) * segs_here, segs_here, 0)
    cross_in = firsts + dot_nt(own_onehot, table)
    result1, grad_cross, grads1, small1 = cross_encoder(
        net,
        cross_in,
        grad_rows[:, 0, :].astype(F32),
        weights1,
        params1,
        allowed,
        onehot,
    )
    layer_out = put_firsts(result0, result1)

    ways, back_ways = link_orders(net)
    grad_ffn, grad_before, grad_mixed, grad_attn, grad_context, small0 = tail_backward(
        cotangent, grad_cross, (normal1, inverse1, slope, normal2, inverse2), w_out0, w_up0, w_down0,
        gains0,
    )
    grad_ffn, grad_before, grad_attn, grad_context, *grads1 = tie(
        grad_ffn, grad_before, grad_attn, grad_context, *grads1
    )
    red_cross = Task(cross_grad_steps(net, *grads1, ways))
    grad_down = dot_tn(active, grad_ffn).astype(BF16)
    grad_down, grad_before, grad_attn, grad_context = window(
        [grad_down, grad_before, grad_attn, grad_context], [red_cross]
    )
    red_down = Task(reduce_steps(net, [grad_down], back_ways + [lo, hi]))
    grad_up = dot_tn(normed_low, grad_before).astype(BF16)
    grad_out = dot_tn(context, grad_attn).astype(BF16)
    grad_up, grad_out, grad_context = window([grad_up, grad_out, grad_context], [red_down])
    red_up = Task(reduce_steps(net, [grad_up], ways + [lo, hi]))
    back_left, sums_left = segment_attend_back(qkv[0], grad_context, 0)
    back_left, grad_context = window([back_left, grad_context], [red_up])
    grad_left = dot_tn(tokens, back_left).astype(BF16)
    grad_left, grad_context = window([grad_left, grad_context], [red_cross])
    back_right, sums_right = segment_attend_back(qkv[1], grad_context, 1)
    (back_right,) = window([back_right], [red_down])
    grad_right = dot_tn(tokens, back_right).astype(BF16)
    grad_right, grad_left, grad_out, back_right, sums_left, sums_right = window(
        [grad_right, grad_left, grad_out, back_right, sums_left, sums_right], [red_up]
    )
    sums = [jnp.sum(v, axis=(0, 1)).reshape(3, half) for v in (sums_left, sums_right)]
    ends = [jnp.concatenate([v[n] for v in sums]) for n in (0, 2)]
    small0 = jnp.concatenate([jnp.stack(ends), small0[2:]])
    small = jnp.stack([small0, small1])
    narrow = small[:, :8].reshape(16, width).T
    long = small[:, 8:].reshape(2, count, -1, share).transpose(1, 3, 0, 2).reshape(width, -1)
    small = jnp.concatenate([narrow, long], 1)
    small = jnp.pad(small, ((0, 0), (0, 128 - small.shape[1]))).astype(BF16)
    red_qkv = Task(
        reduce_steps(
            net, [grad_left, grad_right, grad_out, small], list(zip(back_ways, ways)) + [lo, hi]
        )
    )
    grad_tokens = grad_mixed + dot_nt(back_left, weights_qkv[0]) + dot_nt(back_right, weights_qkv[1])
    (grad_tokens,) = window(
        [grad_tokens.astype(BF16)], [red_qkv, red_down, red_up, red_cross]
    )
    for _ in range(net.bits):
        window([], [red_qkv, red_down, red_up, red_cross])

    grad_left0, grad_right0, grad_out0, small = red_qkv.get()
    narrow = small[:, :16].T.reshape(2, 8, share)
    long = small[:, 16 : 16 + 2 * (hidden // share)]
    long = long.reshape(share, 2, -1).transpose(1, 2, 0).reshape(2, -1)
    (grad_down0,) = red_down.get()
    (grad_up0,) = red_up.get()
    halves = [r.reshape(-1, 3, half) for r in (grad_left0, grad_right0)]
    grad_qkv0 = jnp.stack(halves, 2).reshape(share, -1)
    shares1 = red_cross.get()
    return (
        layer_out,
        grad_tokens,
        jnp.stack([grad_qkv0, shares1[0]]),
        jnp.stack([grad_out0, shares1[1]]),
        jnp.stack([grad_up0, shares1[2]]),
        jnp.stack([grad_down0, shares1[3]]),
        narrow[:, :6],
        long,
        narrow[:, 6:],
        shares1[4][:, : pos_table.shape[0]].T,
    )


def solution(mesh):
    count = mesh.shape["ctx"] * mesh.shape["wa"]
    in_specs = (
        P(AXES, None),
        P(),
        P(None, AXES, None),
        P(None, AXES, None),
        P(None, AXES, None),
        P(None, AXES, None),
        P(None, None, AXES),
        P(None, AXES),
        P(None, None, AXES),
        P(None, AXES),
        P(AXES, None),
    )
    out_specs = (
        P(AXES, None),
        P(AXES, None),
        P(None, AXES, None),
        P(None, AXES, None),
        P(None, AXES, None),
        P(None, AXES, None),
        P(None, None, AXES),
        P(None, AXES),
        P(None, None, AXES),
        P(None, AXES),
    )
    return jax.shard_map(
        partial(shards, count), mesh=mesh, in_specs=in_specs, out_specs=out_specs, check_vma=False
    )
```
